128 devices in a mesh: req: 16 (over y, x), mlp: 8 (over z, core).
Axes of the slice: x: 4, y: 4, z: 4, core: 2. Of those that a mesh axis runs over, the one named last changes fastest.
Arguments:
- tokens: bfloat16 [16384, 1024], P(('req', 'mlp')), may hold values from -6 to 6
- token_owner: int32 [16384, 1], replicated, may hold values from 0 to 127; in each aligned block of 128 rows (0 to 127, 128 to 255, ...) at most 2 rows name the same one
- token_request: int32 [16384], replicated, may hold values from 0 to 3
- cache_len: int32 [512], P(('req', 'mlp')), may hold values from 1 to 512, 131072 in all
- cache_k: bfloat16 [512, 512, 1024], P(('req', 'mlp')), may hold values from -6 to 6
- cache_v: bfloat16 [512, 512, 1024], P(('req', 'mlp')), may hold values from -12 to 12
- w_qkv: bfloat16 [1024, 3072], replicated, may hold values from -0.1875 to 0.1875
- w_out: bfloat16 [1024, 1024], replicated, may hold values from -0.375 to 0.375
- w_fc1: bfloat16 [1024, 4096], P(None, 'mlp'), may hold values from -0.1875 to 0.1875
- w_fc2: bfloat16 [4096, 1024], P('mlp'), may hold values from -0.09375 to 0.09375
- ln1_gain: float32 [1024], replicated, may hold values from 0.1 to 1.9
- ln1_bias: float32 [1024], replicated, may hold values from -3 to 3
- ln2_gain: float32 [1024], replicated, may hold values from 0.1 to 1.9
- ln2_bias: float32 [1024], replicated, may hold values from -3 to 3
Outputs:
- layer_out: bfloat16 [16384, 1024], P(('req', 'mlp'))
The draws below stay inside these ranges and needn't reach their ends.
Inputs may be any that keep to these rules, and one draw needn't show every extreme that they name: `token_owner`: in each aligned block of 128 rows (the rows of one device) no owner is named more than 2 times, a bound that some block reaches; every owner is named somewhere. `cache_len`: some request has exactly 512 cached positions.
All inputs are finite; a program needn't handle non-finite values. No bound on the sum of `cache_len` on one device may be relied on, other than what follows from the above.
Results may differ from the reference program's by a relative error of at most 0.01.
Values may be sent and summed in bfloat16 or wider, within the bound.
A program may use at most 128 MiB of HBM per device.

```python
import math
import jax
import jax.numpy as jnp
import numpy as np
from jax import lax

D = 1024
HEADS = 16
FF = 4096
TOK_DEV = 128
REQS = 4
CTX = 512
CAP = 2
TOKENS = 16384
OWNED = 512
N_REQ = 16
N_MLP = 8
DEVICES = 128


def set_ends(drawn, stream_key, least, largest):
    place = [jax.random.randint(jax.random.fold_in(stream_key, axis), (), 0, length) for axis, length in enumerate(drawn.shape)]
    longest = drawn.shape.index(max(drawn.shape))
    neighbour = place[:longest] + [(place[longest] + 1) % drawn.shape[longest]] + place[longest + 1:]
    return drawn.at[tuple(place)].set(least).at[tuple(neighbour)].set(largest)


def shard_levels(own_key, extent, split, least, top_value):
    factor_of = 1.0
    for position, blocks in split:
        steps = jax.random.uniform(jax.random.fold_in(jax.random.fold_in(own_key, 6), position), (blocks,), jnp.float32, least / len(split), top_value / len(split))
        factor_of = factor_of * jnp.repeat(jnp.exp(steps), extent[position] // blocks).reshape((-1,) + (1,) * (len(extent) - 1 - position))
    return factor_of


def profile(number_of, total, limit, lean):
    loads = [(1 << 20) // math.isqrt(grade ** lean) + 1 for grade in range(2, number_of + 1)]
    surplus, counts = total - limit - (number_of - 1), [1] * (number_of - 1)
    while surplus > 0:
        free = [i for i in range(number_of - 1) if counts[i] < limit]
        pool, budget = sum([loads[i] for i in free]), surplus
        for i in free:
            addition = min(limit - counts[i], max(1, budget * loads[i] // pool), surplus)
            counts[i] = counts[i] + addition
            surplus = surplus - addition
    return np.array([limit] + counts)


def ragged(rng, number_of, total, reach, lean):
    if number_of == 2:
        one = jax.random.randint(rng, (), max(1, total - reach), min(reach, total - 1) + 1)
        return jnp.stack([one, total - one])
    sizes = jnp.asarray(profile(number_of, total, reach, lean), jnp.int32)
    pairs = (number_of - 1) // 2
    donor, taker = sizes[1:1 + 2 * pairs:2], sizes[2:2 + 2 * pairs:2]
    room = jnp.minimum(donor - 1, reach - taker)
    moved = jax.random.randint(jax.random.fold_in(rng, 1), (pairs,), 0, 1 << 20) % (room + 1)
    sizes = sizes.at[1:1 + 2 * pairs:2].set(donor - moved).at[2:2 + 2 * pairs:2].set(taker + moved)
    return sizes[jax.random.permutation(jax.random.fold_in(rng, 2), number_of)]


def shared_out(own_key, own, number, rows, count, top, bound, slope):
    order = jax.random.permutation(own_key, count)
    crowded, ordinary = load_shares(count, rows * top, bound, slope, True), load_shares(count, rows * top, bound, slope, False)
    places = jnp.arange(count)

    def named(sizes, turn):
        used = int((sizes > 0).sum())
        fixed = max(1, used // 4)
        passed = fixed + (places - fixed + turn * (used - fixed)) % max(1, count - fixed)
        return jnp.zeros((count,), jnp.int32).at[order[jnp.where(places < fixed, places, passed)]].set(jnp.asarray(sizes, jnp.int32))

    sizes = jnp.where(number % 4 == 0, named(crowded, number // 4), named(ordinary, number - number // 4 - 1))
    mixed = jax.random.permutation(jax.random.fold_in(own, 3), count)
    source_of, taker = mixed[0:count // 2 * 2:2], mixed[1:count // 2 * 2:2]
    margin = jnp.minimum(sizes[source_of] - 1, bound - sizes[taker]) // 2
    margin = jnp.where((source_of == order[0]) | (taker == order[0]) | (sizes[taker] == 0), 0, jnp.maximum(margin, 0))
    passed = jax.random.randint(jax.random.fold_in(own, 4), (count // 2,), 0, 1 << 20) % (margin + 1)
    sizes = sizes.at[source_of].add(-passed).at[taker].add(passed)
    labels = jnp.searchsorted(jnp.cumsum(sizes), jnp.arange(rows * top), side="right").astype(jnp.int32)
    table = labels.reshape(top, rows).T
    table = table[jax.random.permutation(jax.random.fold_in(own, 1), rows)]
    turn = jax.random.randint(jax.random.fold_in(own, 2), (rows, 1), 0, top)
    return jnp.take_along_axis(table, (jnp.arange(top)[None, :] + turn) % top, axis=1)


def load_shares(amount, total, limit, slope, full):
    weights = [(1 << 20) // math.isqrt(grade ** slope) + 1 for grade in range(1, amount + 1)]
    largest = limit if full else min(limit, max(-(-total // amount), total * weights[0] // sum(weights)))
    least = 1 if total - largest >= amount - 1 else 0
    given, surplus = [largest] + [least] * (amount - 1), total - largest - least * (amount - 1)
    while surplus > 0:
        free = [i for i in range(1, amount) if given[i] < largest] or [i for i in range(1, amount) if given[i] < limit]
        pool, budget = sum([weights[i] for i in free]), surplus
        for i in free:
            extra = min(limit - given[i], max(1, budget * weights[i] // pool), surplus)
            given[i] = given[i] + extra
            surplus = surplus - extra
    return np.array(given)


def normal_values(key, shape, scale, reach, cuts=(), held_as=jnp.bfloat16):
    entries = scale * jax.random.normal(key, shape, jnp.float32)
    if cuts:
        entries = entries * shard_levels(key, shape, cuts, -0.22, 0.18)
    return jnp.clip(entries, -reach, reach).astype(held_as)


def setup_inputs(seed: int = 0) -> dict:
    key_of = jax.random.split(jax.random.key(seed), 15)
    tokens = normal_values(key_of[0], (TOKENS, D), 1.0, 6.0, ((0, 128),))
    token_owner_keys = jax.random.split(jax.random.fold_in(key_of[1], 1), TOKENS // TOK_DEV)
    token_owner_turns = jax.random.permutation(jax.random.fold_in(key_of[1], 3), TOKENS // TOK_DEV)
    token_owner = jax.vmap(lambda own, number: shared_out(jax.random.fold_in(key_of[1], 2), own, number, TOK_DEV, DEVICES, 1, CAP, 1))(token_owner_keys, token_owner_turns).reshape((TOKENS, 1))
    token_request = set_ends(jax.random.randint(key_of[2], (TOKENS,), 0, REQS), jax.random.fold_in(key_of[2], 1), 0, REQS - 1).astype(jnp.int32)
    cache_len = ragged(key_of[3], OWNED, OWNED * CTX // 2, CTX, 1).astype(jnp.int32)
    cache_k = normal_values(key_of[4], (OWNED, CTX, D), 1.0, 6.0, ((0, 128),))
    cache_v = normal_values(key_of[5], (OWNED, CTX, D), 2.0, 12.0, ((0, 128),))
    w_qkv = normal_values(key_of[6], (D, 3 * D), D ** -0.5, 0.1875)
    w_out = normal_values(key_of[7], (D, D), (D // 4) ** -0.5, 0.375)
    w_fc1 = normal_values(key_of[8], (D, FF), D ** -0.5, 0.1875, ((1, 8),))
    w_fc2 = normal_values(key_of[9], (FF, D), FF ** -0.5, 0.09375, ((0, 8),))
    ln1_gain = jnp.clip(1.0 + 0.18 * jax.random.normal(key_of[10], (D,), jnp.float32), 0.1, 1.9)
    ln1_bias = normal_values(key_of[11], (D,), 0.5, 3.0, (), jnp.float32)
    ln2_gain = jnp.clip(1.0 + 0.18 * jax.random.normal(key_of[12], (D,), jnp.float32), 0.1, 1.9)
    ln2_bias = normal_values(key_of[13], (D,), 0.5, 3.0, (), jnp.float32)
    return dict(tokens=tokens, token_owner=token_owner, token_request=token_request, cache_len=cache_len, cache_k=cache_k, cache_v=cache_v, w_qkv=w_qkv, w_out=w_out, w_fc1=w_fc1, w_fc2=w_fc2, ln1_gain=ln1_gain, ln1_bias=ln1_bias, ln2_gain=ln2_gain, ln2_bias=ln2_bias)


epsilon = 1e-05

def layer_norm(values, gain, shift):
    center = values - lax.optimization_barrier(jnp.mean(values, axis=-1, keepdims=True))
    spread = lax.optimization_barrier(jnp.mean(center * center, axis=-1, keepdims=True))
    return center * lax.rsqrt(spread + epsilon) * gain + shift

def slot_table(owners_flat, requests_flat, owner_index, devices, tok_dev, capacity):
    owners = owners_flat.reshape(devices, tok_dev)
    requests = requests_flat.reshape(devices, tok_dev)
    mine_mask = (owners == owner_index).astype(jnp.int32)
    ranking = (jnp.cumsum(mine_mask, axis=1) - 1).astype(jnp.int32)
    places = jnp.arange(capacity, dtype=jnp.int32)
    hit_table = mine_mask[:, :, None] * (ranking[:, :, None] == places[None, None, :]).astype(jnp.int32)
    filled = lax.optimization_barrier(jnp.sum(hit_table, axis=1)).astype(jnp.int32)
    positions = jnp.arange(tok_dev, dtype=jnp.int32)
    local_row = lax.optimization_barrier(jnp.sum(hit_table * positions[None, :, None], axis=1)).astype(jnp.int32)
    sources = jnp.arange(devices, dtype=jnp.int32)[:, None]
    global_row = jnp.where(filled > 0, sources * tok_dev + local_row, -1).astype(jnp.int32).reshape(-1)
    slot_request = lax.optimization_barrier(jnp.sum(hit_table * requests[:, :, None], axis=1)).astype(jnp.int32).reshape(-1)
    return (global_row, slot_request, filled.reshape(-1))

def attend(projections, cache_keys, cache_values, lengths, global_row, slot_request, filled):
    slot_count = projections.shape[0]
    width = projections.shape[1] // 3
    head_dim = width // HEADS
    score_scale = head_dim ** (-0.5)
    queries = projections[:, :width].reshape(slot_count, HEADS, head_dim).astype(jnp.float32)
    key_new = projections[:, width:2 * width].reshape(slot_count, HEADS, head_dim).astype(jnp.float32)
    value_new = projections[:, 2 * width:].reshape(slot_count, HEADS, head_dim).astype(jnp.float32)
    key_old = cache_keys.reshape(REQS * CTX, HEADS, head_dim).astype(jnp.float32)
    value_old = cache_values.reshape(REQS * CTX, HEADS, head_dim).astype(jnp.float32)
    key_owner = jnp.arange(REQS * CTX, dtype=jnp.int32) // CTX
    key_place = jnp.arange(REQS * CTX, dtype=jnp.int32) % CTX
    key_limit = jnp.repeat(lengths, CTX)
    old_mask = (key_owner[None, :] == slot_request[:, None]) & (key_place[None, :] < key_limit[None, :])
    new_mask = (filled[None, :] > 0) & (slot_request[None, :] == slot_request[:, None]) & (global_row[None, :] <= global_row[:, None])
    old_score = jnp.einsum('rhd,khd->hrk', queries, key_old) * score_scale
    new_score = jnp.einsum('rhd,shd->hrs', queries, key_new) * score_scale
    old_exp = jnp.where(old_mask[None], jnp.exp(old_score), jnp.float32(0.0))
    new_exp = jnp.where(new_mask[None], jnp.exp(new_score), jnp.float32(0.0))
    denominator = lax.optimization_barrier(jnp.sum(old_exp, axis=-1)) + lax.optimization_barrier(jnp.sum(new_exp, axis=-1))
    old_weight = (old_exp / denominator[:, :, None]).astype(jnp.bfloat16)
    new_weight = (new_exp / denominator[:, :, None]).astype(jnp.bfloat16)
    result = jnp.einsum('hrk,khd->rhd', old_weight.astype(jnp.float32), value_old)
    result = result + jnp.einsum('hrs,shd->rhd', new_weight.astype(jnp.float32), value_new)
    return result.reshape(slot_count, width).astype(jnp.bfloat16)

def reference(tokens, token_owner, token_request, cache_len, cache_k, cache_v, w_qkv, w_out, w_fc1, w_fc2, ln1_gain, ln1_bias, ln2_gain, ln2_bias):
    devices = N_REQ * N_MLP
    projections = jnp.dot(tokens, w_qkv, preferred_element_type=jnp.float32).astype(jnp.bfloat16)
    owners_flat = token_owner.reshape(-1)

    def one_owner(owner_index):
        global_row, slot_request, filled = slot_table(owners_flat, token_request, owner_index, devices, TOK_DEV, CAP)
        picked = projections[jnp.maximum(global_row, 0)]
        lengths = lax.dynamic_slice_in_dim(cache_len, owner_index * REQS, REQS)
        keys_here = lax.dynamic_slice_in_dim(cache_k, owner_index * REQS, REQS)
        values_here = lax.dynamic_slice_in_dim(cache_v, owner_index * REQS, REQS)
        return (attend(picked, keys_here, values_here, lengths, global_row, slot_request, filled), global_row)
    attended, row_index = lax.map(one_owner, jnp.arange(devices, dtype=jnp.int32))
    target = jnp.where(row_index >= 0, row_index, TOKENS).astype(jnp.int32).reshape(-1)
    attn_rows = jnp.zeros((TOKENS, D), jnp.bfloat16).at[target].set(attended.reshape(-1, D), mode='drop')
    normed = layer_norm(jnp.dot(attn_rows, w_out, preferred_element_type=jnp.float32) + tokens.astype(jnp.float32), ln1_gain, ln1_bias).astype(jnp.bfloat16)
    hidden = jax.nn.gelu(jnp.dot(normed, w_fc1, preferred_element_type=jnp.float32), approximate=False).astype(jnp.bfloat16)
    summed = jnp.dot(hidden, w_fc2, preferred_element_type=jnp.float32)
    return layer_norm(normed.astype(jnp.float32) + summed, ln2_gain, ln2_bias).astype(jnp.bfloat16)
```

```python
import jax
import jax.numpy as jnp
from jax import lax
from jax.sharding import PartitionSpec as P
from jax.experimental import pallas as pl
from jax.experimental.pallas import tpu as pltpu

HEADS = 16


epsilon = 1e-05


def layer_norm(values, gain, shift):
    center = values - jnp.mean(values, axis=-1, keepdims=True)
    spread = jnp.mean(center * center, axis=-1, keepdims=True)
    return center * lax.rsqrt(spread + epsilon) * gain + shift


def slot_table(owners_flat, requests_flat, owner_index, devices, tok_dev, capacity):
    owners = owners_flat.reshape(devices, tok_dev)
    requests = requests_flat.reshape(devices, tok_dev)
    mine_mask = (owners == owner_index).astype(jnp.int32)
    ranking = jnp.cumsum(mine_mask, axis=1) - 1
    places = jnp.arange(capacity, dtype=jnp.int32)
    hit_table = mine_mask[:, :, None] * (ranking[:, :, None] == places[None, None, :]).astype(
        jnp.int32
    )
    filled = jnp.sum(hit_table, axis=1)
    positions = jnp.arange(tok_dev, dtype=jnp.int32)
    local_row = jnp.sum(hit_table * positions[None, :, None], axis=1)
    sources = jnp.arange(devices, dtype=jnp.int32)[:, None]
    global_row = jnp.where(filled > 0, sources * tok_dev + local_row, -1).reshape(-1)
    slot_request = jnp.sum(hit_table * requests[:, :, None], axis=1).reshape(-1)
    return (global_row, slot_request, filled.reshape(-1))


def attention_kernel(
    q_ref, kn_ref, vn_ref, k_ref, v_ref, rreq_ref, rrow_ref, rfill_ref, ctag_ref, ntag_ref, nrow_ref, o_ref
):
    head_dim = q_ref.shape[1] // 2
    score_scale = head_dim ** (-0.5)
    q = q_ref[...]
    keys = k_ref[...]
    values = v_ref[...]
    key_new = kn_ref[...]
    value_new = vn_ref[...]
    row_request = rreq_ref[...]
    old_mask = ctag_ref[...] == row_request
    new_mask = (ntag_ref[...] == row_request) & (nrow_ref[...] <= rrow_ref[...])
    lane = lax.broadcasted_iota(jnp.int32, (1, q.shape[1]), 1)
    contract = (((1,), (1,)), ((), ()))
    result = None
    for half in range(2):
        in_head = (lane // head_dim) == half
        q_head = jnp.where(in_head, q, jnp.zeros_like(q))
        old_score = (
            lax.dot_general(q_head, keys, contract, preferred_element_type=jnp.float32) * score_scale
        )
        new_score = (
            lax.dot_general(q_head, key_new, contract, preferred_element_type=jnp.float32)
            * score_scale
        )
        old_exp = jnp.where(old_mask, jnp.exp(old_score), jnp.float32(0.0))
        new_exp = jnp.where(new_mask, jnp.exp(new_score), jnp.float32(0.0))
        total = jnp.sum(old_exp, axis=1, keepdims=True) + jnp.sum(new_exp, axis=1, keepdims=True)
        total = jnp.where(total > 0, total, jnp.float32(1.0))
        inverse = 1.0 / total
        old_weight = (old_exp * inverse).astype(jnp.bfloat16)
        new_weight = (new_exp * inverse).astype(jnp.bfloat16)
        part = jnp.dot(old_weight, values, preferred_element_type=jnp.float32) + jnp.dot(
            new_weight, value_new, preferred_element_type=jnp.float32
        )
        result = part if result is None else jnp.where(in_head, part, result)
    result = jnp.where(rfill_ref[...] > 0, result, jnp.float32(0.0))
    o_ref[...] = result.astype(o_ref.dtype)


def attend(projections, cache_keys, cache_values, lengths, global_row, slot_request, filled):
    slot_count = projections.shape[0]
    width = projections.shape[1] // 3
    requests, context = cache_keys.shape[0], cache_keys.shape[1]
    pair = 128
    pairs = width // pair
    keys = cache_keys.reshape(requests * context, width)
    values = cache_values.reshape(requests * context, width)
    key_owner = jnp.arange(requests * context, dtype=jnp.int32) // context
    key_place = jnp.arange(requests * context, dtype=jnp.int32) % context
    key_limit = jnp.repeat(lengths, context)
    column_tag = jnp.where(key_place < key_limit, key_owner, -1).reshape(1, -1)
    new_tag = jnp.where(filled > 0, slot_request, -1).reshape(1, -1)
    new_row = global_row.reshape(1, -1)
    row_request = slot_request.reshape(-1, 1)
    row_index = global_row.reshape(-1, 1)
    row_filled = filled.reshape(-1, 1)
    keyed = requests * context
    whole = lambda shape: pl.BlockSpec(shape, lambda p: (0, 0))
    return pl.pallas_call(
        attention_kernel,
        grid=(pairs,),
        in_specs=[
            pl.BlockSpec((slot_count, pair), lambda p: (0, p)),
            pl.BlockSpec((slot_count, pair), lambda p: (0, pairs + p)),
            pl.BlockSpec((slot_count, pair), lambda p: (0, 2 * pairs + p)),
            pl.BlockSpec((keyed, pair), lambda p: (0, p)),
            pl.BlockSpec((keyed, pair), lambda p: (0, p)),
            whole((slot_count, 1)),
            whole((slot_count, 1)),
            whole((slot_count, 1)),
            whole((1, keyed)),
            whole((1, slot_count)),
            whole((1, slot_count)),
        ],
        out_specs=pl.BlockSpec((slot_count, pair), lambda p: (0, p)),
        out_shape=jax.ShapeDtypeStruct((slot_count, width), jnp.bfloat16),
        compiler_params=pltpu.CompilerParams(vmem_limit_bytes=48 * 1024 * 1024),
    )(
        projections,
        projections,
        projections,
        keys,
        values,
        row_request,
        row_index,
        row_filled,
        column_tag,
        new_tag,
        new_row,
    )


def per_device(
    tokens,
    token_owner,
    token_request,
    cache_len,
    cache_k,
    cache_v,
    w_qkv,
    w_out,
    w_fc1,
    w_fc2,
    ln1_gain,
    ln1_bias,
    ln2_gain,
    ln2_bias,
):
    n_req = lax.axis_size("req")
    n_mlp = lax.axis_size("mlp")
    devices = n_req * n_mlp
    owner_index = lax.axis_index("req") * n_mlp + lax.axis_index("mlp")
    tok_dev, width = tokens.shape
    capacity = max(2, 2 * tok_dev // devices)
    slot_count = devices * capacity
    owners_flat = token_owner.reshape(-1)
    my_owners = lax.dynamic_slice_in_dim(owners_flat, owner_index * tok_dev, tok_dev)
    owner_onehot = (my_owners[:, None] == jnp.arange(devices, dtype=jnp.int32)[None, :]).astype(
        jnp.int32
    )
    ranking = jnp.cumsum(owner_onehot, axis=0) - 1
    my_rank = jnp.sum(owner_onehot * ranking, axis=1)
    column = my_owners * capacity + my_rank
    dispatch = (column[:, None] == jnp.arange(slot_count, dtype=jnp.int32)[None, :]).astype(
        jnp.bfloat16
    )
    outgoing = jnp.einsum("tr,td->rd", dispatch, tokens, preferred_element_type=jnp.float32).astype(
        jnp.bfloat16
    )
    arrived = lax.all_to_all(
        outgoing.reshape(devices, capacity, width),
        ("req", "mlp"),
        split_axis=0,
        concat_axis=0,
        tiled=True,
    )
    projections = jnp.dot(
        arrived.reshape(slot_count, width), w_qkv, preferred_element_type=jnp.float32
    ).astype(jnp.bfloat16)
    global_row, slot_request, filled = slot_table(
        owners_flat, token_request, owner_index, devices, tok_dev, capacity
    )
    attended = attend(projections, cache_k, cache_v, cache_len, global_row, slot_request, filled)
    returned = lax.all_to_all(
        attended.reshape(devices, capacity, width),
        ("req", "mlp"),
        split_axis=0,
        concat_axis=0,
        tiled=True,
    )
    attn_rows = jnp.dot(
        dispatch, returned.reshape(slot_count, width), preferred_element_type=jnp.float32
    ).astype(jnp.bfloat16)
    projected_out = jnp.dot(attn_rows, w_out, preferred_element_type=jnp.float32)
    normed = layer_norm(projected_out + tokens.astype(jnp.float32), ln1_gain, ln1_bias).astype(
        jnp.bfloat16
    )
    gathered = lax.all_gather(normed, "mlp", axis=0, tiled=True)
    hidden = jax.nn.gelu(
        jnp.dot(gathered, w_fc1, preferred_element_type=jnp.float32), approximate=False
    ).astype(jnp.bfloat16)
    summed = lax.psum_scatter(
        jnp.dot(hidden, w_fc2, preferred_element_type=jnp.float32).astype(jnp.bfloat16),
        "mlp",
        scatter_dimension=0,
        tiled=True,
    ).astype(jnp.float32)
    return layer_norm(normed.astype(jnp.float32) + summed, ln2_gain, ln2_bias).astype(jnp.bfloat16)


def solution(mesh):
    placed = (
        P(("req", "mlp"), None),
        P(),
        P(),
        P(("req", "mlp")),
        P(("req", "mlp"), None, None),
        P(("req", "mlp"), None, None),
        P(),
        P(),
        P(None, "mlp"),
        P("mlp", None),
        P(),
        P(),
        P(),
        P(),
    )
    return jax.shard_map(
        per_device, mesh=mesh, in_specs=placed, out_specs=P(("req", "mlp"), None), check_vma=False
    )
```

```python
import functools

import jax
import jax.numpy as jnp
from jax import lax
from jax.sharding import PartitionSpec as P
from jax.experimental import pallas as pl
from jax.experimental.pallas import tpu as pltpu

HEADS = 16


epsilon = 1e-05


def layer_norm(values, gain, shift):
    center = values - jnp.mean(values, axis=-1, keepdims=True)
    spread = jnp.mean(center * center, axis=-1, keepdims=True)
    return center * lax.rsqrt(spread + epsilon) * gain + shift


def slot_table(owners_flat, requests_flat, owner_index, devices, tok_dev, capacity):
    owners = owners_flat.reshape(devices, tok_dev)
    requests = requests_flat.reshape(devices, tok_dev)
    mine_mask = (owners == owner_index).astype(jnp.int32)
    ranking = jnp.cumsum(mine_mask, axis=1) - 1
    places = jnp.arange(capacity, dtype=jnp.int32)
    hit_table = mine_mask[:, :, None] * (ranking[:, :, None] == places[None, None, :]).astype(
        jnp.int32
    )
    filled = jnp.sum(hit_table, axis=1)
    positions = jnp.arange(tok_dev, dtype=jnp.int32)
    local_row = jnp.sum(hit_table * positions[None, :, None], axis=1)
    sources = jnp.arange(devices, dtype=jnp.int32)[:, None]
    global_row = jnp.where(filled > 0, sources * tok_dev + local_row, -1).reshape(-1)
    slot_request = jnp.sum(hit_table * requests[:, :, None], axis=1).reshape(-1)
    return (global_row, slot_request, filled.reshape(-1))


def attention_kernel(
    q_ref, kn_ref, vn_ref, k_ref, v_ref, rreq_ref, rrow_ref, rfill_ref, ctag_ref, ntag_ref, nrow_ref, o_ref
):
    head_dim = q_ref.shape[1] // 2
    score_scale = head_dim ** (-0.5)
    q = q_ref[...]
    keys = k_ref[...]
    values = v_ref[...]
    key_new = kn_ref[...]
    value_new = vn_ref[...]
    row_request = rreq_ref[...]
    old_mask = ctag_ref[...] == row_request
    new_mask = (ntag_ref[...] == row_request) & (nrow_ref[...] <= rrow_ref[...])
    lane = lax.broadcasted_iota(jnp.int32, (1, q.shape[1]), 1)
    contract = (((1,), (1,)), ((), ()))
    result = None
    for half in range(2):
        in_head = (lane // head_dim) == half
        q_head = jnp.where(in_head, q, jnp.zeros_like(q))
        old_score = (
            lax.dot_general(q_head, keys, contract, preferred_element_type=jnp.float32) * score_scale
        )
        new_score = (
            lax.dot_general(q_head, key_new, contract, preferred_element_type=jnp.float32)
            * score_scale
        )
        old_exp = jnp.where(old_mask, jnp.exp(old_score), jnp.float32(0.0))
        new_exp = jnp.where(new_mask, jnp.exp(new_score), jnp.float32(0.0))
        total = jnp.sum(old_exp, axis=1, keepdims=True) + jnp.sum(new_exp, axis=1, keepdims=True)
        total = jnp.where(total > 0, total, jnp.float32(1.0))
        inverse = 1.0 / total
        old_weight = (old_exp * inverse).astype(jnp.bfloat16)
        new_weight = (new_exp * inverse).astype(jnp.bfloat16)
        part = jnp.dot(old_weight, values, preferred_element_type=jnp.float32) + jnp.dot(
            new_weight, value_new, preferred_element_type=jnp.float32
        )
        result = part if result is None else jnp.where(in_head, part, result)
    result = jnp.where(rfill_ref[...] > 0, result, jnp.float32(0.0))
    o_ref[...] = result.astype(o_ref.dtype)


def attend(projections, cache_keys, cache_values, lengths, global_row, slot_request, filled):
    slot_count = projections.shape[0]
    width = projections.shape[1] // 3
    requests, context = cache_keys.shape[0], cache_keys.shape[1]
    pair = 128
    pairs = width // pair
    keys = cache_keys.reshape(requests * context, width)
    values = cache_values.reshape(requests * context, width)
    key_owner = jnp.arange(requests * context, dtype=jnp.int32) // context
    key_place = jnp.arange(requests * context, dtype=jnp.int32) % context
    key_limit = jnp.repeat(lengths, context)
    column_tag = jnp.where(key_place < key_limit, key_owner, -1).reshape(1, -1)
    new_tag = jnp.where(filled > 0, slot_request, -1).reshape(1, -1)
    new_row = global_row.reshape(1, -1)
    row_request = slot_request.reshape(-1, 1)
    row_index = global_row.reshape(-1, 1)
    row_filled = filled.reshape(-1, 1)
    keyed = requests * context
    whole = lambda shape: pl.BlockSpec(shape, lambda p: (0, 0))
    return pl.pallas_call(
        attention_kernel,
        grid=(pairs,),
        in_specs=[
            pl.BlockSpec((slot_count, pair), lambda p: (0, p)),
            pl.BlockSpec((slot_count, pair), lambda p: (0, pairs + p)),
            pl.BlockSpec((slot_count, pair), lambda p: (0, 2 * pairs + p)),
            pl.BlockSpec((keyed, pair), lambda p: (0, p)),
            pl.BlockSpec((keyed, pair), lambda p: (0, p)),
            whole((slot_count, 1)),
            whole((slot_count, 1)),
            whole((slot_count, 1)),
            whole((1, keyed)),
            whole((1, slot_count)),
            whole((1, slot_count)),
        ],
        out_specs=pl.BlockSpec((slot_count, pair), lambda p: (0, p)),
        out_shape=jax.ShapeDtypeStruct((slot_count, width), jnp.bfloat16),
        compiler_params=pltpu.CompilerParams(vmem_limit_bytes=48 * 1024 * 1024),
    )(
        projections,
        projections,
        projections,
        keys,
        values,
        row_request,
        row_index,
        row_filled,
        column_tag,
        new_tag,
        new_row,
    )


def exchange_kernel(groups, x_ref, o_ref, send_sem, recv_sem, local_sem):
    n = x_ref.shape[0]
    me = lax.axis_index("req") * groups + lax.axis_index("mlp")

    def remote(k):
        peer = lax.rem(me + k, n)
        return pltpu.make_async_remote_copy(
            src_ref=x_ref.at[peer],
            dst_ref=o_ref.at[me],
            send_sem=send_sem.at[k],
            recv_sem=recv_sem.at[k],
            device_id=(peer // groups, lax.rem(peer, groups)),
            device_id_type=pl.DeviceIdType.MESH,
        )

    own = pltpu.make_async_copy(x_ref.at[me], o_ref.at[me], local_sem)
    own.start()

    def start(k, carry):
        remote(k).start()
        return carry

    def finish(k, carry):
        copy = remote(k)
        copy.wait_send()
        copy.wait_recv()
        return carry

    lax.fori_loop(1, n, start, 0)
    own.wait()
    lax.fori_loop(1, n, finish, 0)


def exchange(blocks):
    n = blocks.shape[0]
    groups = lax.axis_size("mlp")
    return pl.pallas_call(
        functools.partial(exchange_kernel, groups),
        in_specs=[pl.BlockSpec(memory_space=pl.ANY)],
        out_specs=pl.BlockSpec(memory_space=pl.ANY),
        out_shape=jax.ShapeDtypeStruct(blocks.shape, blocks.dtype),
        scratch_shapes=[
            pltpu.SemaphoreType.DMA((n,)),
            pltpu.SemaphoreType.DMA((n,)),
            pltpu.SemaphoreType.DMA(()),
        ],
        compiler_params=pltpu.CompilerParams(has_side_effects=True),
    )(blocks)


def per_device(
    tokens,
    token_owner,
    token_request,
    cache_len,
    cache_k,
    cache_v,
    w_qkv,
    w_out,
    w_fc1,
    w_fc2,
    ln1_gain,
    ln1_bias,
    ln2_gain,
    ln2_bias,
):
    n_req = lax.axis_size("req")
    n_mlp = lax.axis_size("mlp")
    devices = n_req * n_mlp
    owner_index = lax.axis_index("req") * n_mlp + lax.axis_index("mlp")
    tok_dev, width = tokens.shape
    capacity = max(2, 2 * tok_dev // devices)
    slot_count = devices * capacity
    owners_flat = token_owner.reshape(-1)
    my_owners = lax.dynamic_slice_in_dim(owners_flat, owner_index * tok_dev, tok_dev)
    owner_onehot = (my_owners[:, None] == jnp.arange(devices, dtype=jnp.int32)[None, :]).astype(
        jnp.int32
    )
    ranking = jnp.cumsum(owner_onehot, axis=0) - 1
    my_rank = jnp.sum(owner_onehot * ranking, axis=1)
    column = my_owners * capacity + my_rank
    dispatch = (column[:, None] == jnp.arange(slot_count, dtype=jnp.int32)[None, :]).astype(
        jnp.bfloat16
    )
    outgoing = jnp.einsum("tr,td->rd", dispatch, tokens, preferred_element_type=jnp.float32).astype(
        jnp.bfloat16
    )
    arrived = exchange(outgoing.reshape(devices, capacity, width))
    projections = jnp.dot(
        arrived.reshape(slot_count, width), w_qkv, preferred_element_type=jnp.float32
    ).astype(jnp.bfloat16)
    global_row, slot_request, filled = slot_table(
        owners_flat, token_request, owner_index, devices, tok_dev, capacity
    )
    attended = attend(projections, cache_k, cache_v, cache_len, global_row, slot_request, filled)
    returned = exchange(attended.reshape(devices, capacity, width))
    attn_rows = jnp.dot(
        dispatch, returned.reshape(slot_count, width), preferred_element_type=jnp.float32
    ).astype(jnp.bfloat16)
    projected_out = jnp.dot(attn_rows, w_out, preferred_element_type=jnp.float32)
    normed = layer_norm(projected_out + tokens.astype(jnp.float32), ln1_gain, ln1_bias).astype(
        jnp.bfloat16
    )
    gathered = lax.all_gather(normed, "mlp", axis=0, tiled=True)
    hidden = jax.nn.gelu(
        jnp.dot(gathered, w_fc1, preferred_element_type=jnp.float32), approximate=False
    ).astype(jnp.bfloat16)
    summed = lax.psum_scatter(
        jnp.dot(hidden, w_fc2, preferred_element_type=jnp.float32).astype(jnp.bfloat16),
        "mlp",
        scatter_dimension=0,
        tiled=True,
    ).astype(jnp.float32)
    return layer_norm(normed.astype(jnp.float32) + summed, ln2_gain, ln2_bias).astype(jnp.bfloat16)


def solution(mesh):
    placed = (
        P(("req", "mlp"), None),
        P(),
        P(),
        P(("req", "mlp")),
        P(("req", "mlp"), None, None),
        P(("req", "mlp"), None, None),
        P(),
        P(),
        P(None, "mlp"),
        P("mlp", None),
        P(),
        P(),
        P(),
        P(),
    )
    return jax.shard_map(
        per_device, mesh=mesh, in_specs=placed, out_specs=P(("req", "mlp"), None), check_vma=False
    )
```

```python
import jax
import jax.numpy as jnp
from jax import lax
from jax.sharding import PartitionSpec as P
from jax.experimental import pallas as pl
from jax.experimental.pallas import tpu as pltpu

HEADS = 16


epsilon = 1e-05


def layer_norm(values, gain, shift):
    center = values - jnp.mean(values, axis=-1, keepdims=True)
    spread = jnp.mean(center * center, axis=-1, keepdims=True)
    return center * lax.rsqrt(spread + epsilon) * gain + shift


def slot_table(owners_flat, requests_flat, owner_index, devices, tok_dev, capacity):
    owners = owners_flat.reshape(devices, tok_dev)
    requests = requests_flat.reshape(devices, tok_dev)
    mine_mask = (owners == owner_index).astype(jnp.int32)
    ranking = jnp.cumsum(mine_mask, axis=1) - 1
    places = jnp.arange(capacity, dtype=jnp.int32)
    hit_table = mine_mask[:, :, None] * (ranking[:, :, None] == places[None, None, :]).astype(
        jnp.int32
    )
    filled = jnp.sum(hit_table, axis=1)
    positions = jnp.arange(tok_dev, dtype=jnp.int32)
    local_row = jnp.sum(hit_table * positions[None, :, None], axis=1)
    sources = jnp.arange(devices, dtype=jnp.int32)[:, None]
    global_row = jnp.where(filled > 0, sources * tok_dev + local_row, -1).reshape(-1)
    slot_request = jnp.sum(hit_table * requests[:, :, None], axis=1).reshape(-1)
    return (global_row, slot_request, filled.reshape(-1))


def attention_kernel(
    q_ref, kn_ref, vn_ref, k_ref, v_ref, rreq_ref, rrow_ref, rfill_ref, ctag_ref, ntag_ref, nrow_ref, o_ref
):
    head_dim = q_ref.shape[1] // 2
    score_scale = head_dim ** (-0.5)
    q = q_ref[...]
    keys = k_ref[...]
    values = v_ref[...]
    key_new = kn_ref[...]
    value_new = vn_ref[...]
    row_request = rreq_ref[...]
    old_mask = ctag_ref[...] == row_request
    new_mask = (ntag_ref[...] == row_request) & (nrow_ref[...] <= rrow_ref[...])
    lane = lax.broadcasted_iota(jnp.int32, (1, q.shape[1]), 1)
    contract = (((1,), (1,)), ((), ()))
    result = None
    for half in range(2):
        in_head = (lane // head_dim) == half
        q_head = jnp.where(in_head, q, jnp.zeros_like(q))
        old_score = (
            lax.dot_general(q_head, keys, contract, preferred_element_type=jnp.float32) * score_scale
        )
        new_score = (
            lax.dot_general(q_head, key_new, contract, preferred_element_type=jnp.float32)
            * score_scale
        )
        old_exp = jnp.where(old_mask, jnp.exp(old_score), jnp.float32(0.0))
        new_exp = jnp.where(new_mask, jnp.exp(new_score), jnp.float32(0.0))
        total = jnp.sum(old_exp, axis=1, keepdims=True) + jnp.sum(new_exp, axis=1, keepdims=True)
        total = jnp.where(total > 0, total, jnp.float32(1.0))
        inverse = 1.0 / total
        old_weight = (old_exp * inverse).astype(jnp.bfloat16)
        new_weight = (new_exp * inverse).astype(jnp.bfloat16)
        part = jnp.dot(old_weight, values, preferred_element_type=jnp.float32) + jnp.dot(
            new_weight, value_new, preferred_element_type=jnp.float32
        )
        result = part if result is None else jnp.where(in_head, part, result)
    result = jnp.where(rfill_ref[...] > 0, result, jnp.float32(0.0))
    o_ref[...] = result.astype(o_ref.dtype)


def attend(projections, cache_keys, cache_values, lengths, global_row, slot_request, filled):
    slot_count = projections.shape[0]
    width = projections.shape[1] // 3
    requests, context = cache_keys.shape[0], cache_keys.shape[1]
    pair = 128
    pairs = width // pair
    keys = cache_keys.reshape(requests * context, width)
    values = cache_values.reshape(requests * context, width)
    key_owner = jnp.arange(requests * context, dtype=jnp.int32) // context
    key_place = jnp.arange(requests * context, dtype=jnp.int32) % context
    key_limit = jnp.repeat(lengths, context)
    column_tag = jnp.where(key_place < key_limit, key_owner, -1).reshape(1, -1)
    new_tag = jnp.where(filled > 0, slot_request, -1).reshape(1, -1)
    new_row = global_row.reshape(1, -1)
    row_request = slot_request.reshape(-1, 1)
    row_index = global_row.reshape(-1, 1)
    row_filled = filled.reshape(-1, 1)
    keyed = requests * context
    whole = lambda shape: pl.BlockSpec(shape, lambda p: (0, 0))
    return pl.pallas_call(
        attention_kernel,
        grid=(pairs,),
        in_specs=[
            pl.BlockSpec((slot_count, pair), lambda p: (0, p)),
            pl.BlockSpec((slot_count, pair), lambda p: (0, pairs + p)),
            pl.BlockSpec((slot_count, pair), lambda p: (0, 2 * pairs + p)),
            pl.BlockSpec((keyed, pair), lambda p: (0, p)),
            pl.BlockSpec((keyed, pair), lambda p: (0, p)),
            whole((slot_count, 1)),
            whole((slot_count, 1)),
            whole((slot_count, 1)),
            whole((1, keyed)),
            whole((1, slot_count)),
            whole((1, slot_count)),
        ],
        out_specs=pl.BlockSpec((slot_count, pair), lambda p: (0, p)),
        out_shape=jax.ShapeDtypeStruct((slot_count, width), jnp.bfloat16),
        compiler_params=pltpu.CompilerParams(vmem_limit_bytes=48 * 1024 * 1024),
    )(
        projections,
        projections,
        projections,
        keys,
        values,
        row_request,
        row_index,
        row_filled,
        column_tag,
        new_tag,
        new_row,
    )


def exchange(blocks):
    n_req = lax.axis_size("req")
    n_mlp = lax.axis_size("mlp")
    rest = blocks.shape[1:]
    staged = blocks.reshape((n_req, n_mlp) + rest).swapaxes(0, 1)
    staged = lax.all_to_all(staged, "mlp", split_axis=0, concat_axis=0, tiled=True)
    staged = staged.swapaxes(0, 1)
    staged = lax.all_to_all(staged, "req", split_axis=0, concat_axis=0, tiled=True)
    return staged.reshape(blocks.shape)


def per_device(
    tokens,
    token_owner,
    token_request,
    cache_len,
    cache_k,
    cache_v,
    w_qkv,
    w_out,
    w_fc1,
    w_fc2,
    ln1_gain,
    ln1_bias,
    ln2_gain,
    ln2_bias,
):
    n_req = lax.axis_size("req")
    n_mlp = lax.axis_size("mlp")
    devices = n_req * n_mlp
    owner_index = lax.axis_index("req") * n_mlp + lax.axis_index("mlp")
    tok_dev, width = tokens.shape
    capacity = max(2, 2 * tok_dev // devices)
    slot_count = devices * capacity
    owners_flat = token_owner.reshape(-1)
    my_owners = lax.dynamic_slice_in_dim(owners_flat, owner_index * tok_dev, tok_dev)
    owner_onehot = (my_owners[:, None] == jnp.arange(devices, dtype=jnp.int32)[None, :]).astype(
        jnp.int32
    )
    ranking = jnp.cumsum(owner_onehot, axis=0) - 1
    my_rank = jnp.sum(owner_onehot * ranking, axis=1)
    column = my_owners * capacity + my_rank
    dispatch = (column[:, None] == jnp.arange(slot_count, dtype=jnp.int32)[None, :]).astype(
        jnp.bfloat16
    )
    outgoing = jnp.einsum("tr,td->rd", dispatch, tokens, preferred_element_type=jnp.float32).astype(
        jnp.bfloat16
    )
    arrived = exchange(outgoing.reshape(devices, capacity, width))
    projections = jnp.dot(
        arrived.reshape(slot_count, width), w_qkv, preferred_element_type=jnp.float32
    ).astype(jnp.bfloat16)
    global_row, slot_request, filled = slot_table(
        owners_flat, token_request, owner_index, devices, tok_dev, capacity
    )
    attended = attend(projections, cache_k, cache_v, cache_len, global_row, slot_request, filled)
    returned = exchange(attended.reshape(devices, capacity, width))
    attn_rows = jnp.dot(
        dispatch, returned.reshape(slot_count, width), preferred_element_type=jnp.float32
    ).astype(jnp.bfloat16)
    projected_out = jnp.dot(attn_rows, w_out, preferred_element_type=jnp.float32)
    normed = layer_norm(projected_out + tokens.astype(jnp.float32), ln1_gain, ln1_bias).astype(
        jnp.bfloat16
    )
    gathered = lax.all_gather(normed, "mlp", axis=0, tiled=True)
    hidden = jax.nn.gelu(
        jnp.dot(gathered, w_fc1, preferred_element_type=jnp.float32), approximate=False
    ).astype(jnp.bfloat16)
    summed = lax.psum_scatter(
        jnp.dot(hidden, w_fc2, preferred_element_type=jnp.float32).astype(jnp.bfloat16),
        "mlp",
        scatter_dimension=0,
        tiled=True,
    ).astype(jnp.float32)
    return layer_norm(normed.astype(jnp.float32) + summed, ln2_gain, ln2_bias).astype(jnp.bfloat16)


def solution(mesh):
    placed = (
        P(("req", "mlp"), None),
        P(),
        P(),
        P(("req", "mlp")),
        P(("req", "mlp"), None, None),
        P(("req", "mlp"), None, None),
        P(),
        P(),
        P(None, "mlp"),
        P("mlp", None),
        P(),
        P(),
        P(),
        P(),
    )
    return jax.shard_map(
        per_device, mesh=mesh, in_specs=placed, out_specs=P(("req", "mlp"), None), check_vma=False
    )
```

```python
import jax
import jax.numpy as jnp
from jax import lax
from jax.sharding import PartitionSpec as P
from jax.experimental import pallas as pl
from jax.experimental.pallas import tpu as pltpu

HEADS = 16


epsilon = 1e-05


def layer_norm(values, gain, shift):
    center = values - jnp.mean(values, axis=-1, keepdims=True)
    spread = jnp.mean(center * center, axis=-1, keepdims=True)
    return center * lax.rsqrt(spread + epsilon) * gain + shift


def slot_table(owners_flat, requests_flat, owner_index, devices, tok_dev, capacity):
    owners = owners_flat.reshape(devices, tok_dev)
    requests = requests_flat.reshape(devices, tok_dev)
    mine_mask = (owners == owner_index).astype(jnp.int32)
    ranking = jnp.cumsum(mine_mask, axis=1) - 1
    places = jnp.arange(capacity, dtype=jnp.int32)
    hit_table = mine_mask[:, :, None] * (ranking[:, :, None] == places[None, None, :]).astype(
        jnp.int32
    )
    filled = jnp.sum(hit_table, axis=1)
    positions = jnp.arange(tok_dev, dtype=jnp.int32)
    local_row = jnp.sum(hit_table * positions[None, :, None], axis=1)
    sources = jnp.arange(devices, dtype=jnp.int32)[:, None]
    global_row = jnp.where(filled > 0, sources * tok_dev + local_row, -1).reshape(-1)
    slot_request = jnp.sum(hit_table * requests[:, :, None], axis=1).reshape(-1)
    return (global_row, slot_request, filled.reshape(-1))


def attention_kernel(
    q_ref, kn_ref, vn_ref, k_ref, v_ref, rreq_ref, rrow_ref, rfill_ref, ctag_ref, ntag_ref, nrow_ref, o_ref
):
    head_dim = q_ref.shape[1] // 2
    score_scale = head_dim ** (-0.5)
    q = q_ref[...]
    keys = k_ref[...]
    values = v_ref[...]
    key_new = kn_ref[...]
    value_new = vn_ref[...]
    row_request = rreq_ref[...]
    old_mask = ctag_ref[...] == row_request
    new_mask = (ntag_ref[...] == row_request) & (nrow_ref[...] <= rrow_ref[...])
    lane = lax.broadcasted_iota(jnp.int32, (1, q.shape[1]), 1)
    contract = (((1,), (1,)), ((), ()))
    result = None
    for half in range(2):
        in_head = (lane // head_dim) == half
        q_head = jnp.where(in_head, q, jnp.zeros_like(q))
        old_score = (
            lax.dot_general(q_head, keys, contract, preferred_element_type=jnp.float32) * score_scale
        )
        new_score = (
            lax.dot_general(q_head, key_new, contract, preferred_element_type=jnp.float32)
            * score_scale
        )
        old_exp = jnp.where(old_mask, jnp.exp(old_score), jnp.float32(0.0))
        new_exp = jnp.where(new_mask, jnp.exp(new_score), jnp.float32(0.0))
        total = jnp.sum(old_exp, axis=1, keepdims=True) + jnp.sum(new_exp, axis=1, keepdims=True)
        total = jnp.where(total > 0, total, jnp.float32(1.0))
        inverse = 1.0 / total
        old_weight = (old_exp * inverse).astype(jnp.bfloat16)
        new_weight = (new_exp * inverse).astype(jnp.bfloat16)
        part = jnp.dot(old_weight, values, preferred_element_type=jnp.float32) + jnp.dot(
            new_weight, value_new, preferred_element_type=jnp.float32
        )
        result = part if result is None else jnp.where(in_head, part, result)
    result = jnp.where(rfill_ref[...] > 0, result, jnp.float32(0.0))
    o_ref[...] = result.astype(o_ref.dtype)


def attend(projections, cache_keys, cache_values, lengths, global_row, slot_request, filled):
    slot_count = projections.shape[0]
    width = projections.shape[1] // 3
    requests, context = cache_keys.shape[0], cache_keys.shape[1]
    pair = 128
    pairs = width // pair
    keys = cache_keys.reshape(requests * context, width)
    values = cache_values.reshape(requests * context, width)
    key_owner = jnp.arange(requests * context, dtype=jnp.int32) // context
    key_place = jnp.arange(requests * context, dtype=jnp.int32) % context
    key_limit = jnp.repeat(lengths, context)
    column_tag = jnp.where(key_place < key_limit, key_owner, -1).reshape(1, -1)
    new_tag = jnp.where(filled > 0, slot_request, -1).reshape(1, -1)
    new_row = global_row.reshape(1, -1)
    row_request = slot_request.reshape(-1, 1)
    row_index = global_row.reshape(-1, 1)
    row_filled = filled.reshape(-1, 1)
    keyed = requests * context
    whole = lambda shape: pl.BlockSpec(shape, lambda p: (0, 0))
    return pl.pallas_call(
        attention_kernel,
        grid=(pairs,),
        in_specs=[
            pl.BlockSpec((slot_count, pair), lambda p: (0, p)),
            pl.BlockSpec((slot_count, pair), lambda p: (0, pairs + p)),
            pl.BlockSpec((slot_count, pair), lambda p: (0, 2 * pairs + p)),
            pl.BlockSpec((keyed, pair), lambda p: (0, p)),
            pl.BlockSpec((keyed, pair), lambda p: (0, p)),
            whole((slot_count, 1)),
            whole((slot_count, 1)),
            whole((slot_count, 1)),
            whole((1, keyed)),
            whole((1, slot_count)),
            whole((1, slot_count)),
        ],
        out_specs=pl.BlockSpec((slot_count, pair), lambda p: (0, p)),
        out_shape=jax.ShapeDtypeStruct((slot_count, width), jnp.bfloat16),
        compiler_params=pltpu.CompilerParams(vmem_limit_bytes=48 * 1024 * 1024),
    )(
        projections,
        projections,
        projections,
        keys,
        values,
        row_request,
        row_index,
        row_filled,
        column_tag,
        new_tag,
        new_row,
    )


def scatter_kernel(part_ref, o_ref, pair_buf, send_buf, ring_buf, pair_send, pair_recv, ring_send, ring_recv):
    req = lax.axis_index("req")
    me = lax.axis_index("mlp")
    chips = lax.axis_size("mlp") // 2
    chip, core = me // 2, lax.rem(me, 2)
    partner = chip * 2 + 1 - core
    rows = o_ref.shape[0]
    barrier = pltpu.get_barrier_semaphore()
    pl.semaphore_signal(barrier, 1, device_id=(req, partner), device_id_type=pl.DeviceIdType.MESH)
    for k in range(1, chips):
        other = lax.rem(chip + k, chips) * 2 + core
        pl.semaphore_signal(barrier, 1, device_id=(req, other), device_id_type=pl.DeviceIdType.MESH)
    pl.semaphore_wait(barrier, chips)

    def pair_copy(z):
        block = z * 2 + 1 - core
        return pltpu.make_async_remote_copy(
            src_ref=part_ref.at[pl.ds(pl.multiple_of(block * rows, rows), rows)],
            dst_ref=pair_buf.at[z],
            send_sem=pair_send.at[z],
            recv_sem=pair_recv.at[z],
            device_id=(req, partner),
            device_id_type=pl.DeviceIdType.MESH,
        )

    for z in range(chips):
        pair_copy(z).start()
    for z in range(chips):
        pair_copy(z).wait()

    def ring_copy(k):
        target = lax.rem(chip + k, chips)
        return pltpu.make_async_remote_copy(
            src_ref=send_buf.at[k],
            dst_ref=ring_buf.at[k],
            send_sem=ring_send.at[k],
            recv_sem=ring_recv.at[k],
            device_id=(req, target * 2 + core),
            device_id_type=pl.DeviceIdType.MESH,
        )

    for k in range(1, chips):
        target = lax.rem(chip + k, chips)
        mine = part_ref[pl.ds(pl.multiple_of((target * 2 + core) * rows, rows), rows), :]
        send_buf[k] = (mine.astype(jnp.float32) + pair_buf[target].astype(jnp.float32)).astype(
            send_buf.dtype
        )
        ring_copy(k).start()
    own = part_ref[pl.ds(pl.multiple_of(me * rows, rows), rows), :]
    total = own.astype(jnp.float32) + pair_buf[chip].astype(jnp.float32)
    for k in range(1, chips):
        ring_copy(k).wait()
        total = total + ring_buf[k].astype(jnp.float32)
    o_ref[...] = total


def scatter_sum(partial):
    groups = lax.axis_size("mlp")
    chips = groups // 2
    rows = partial.shape[0] // groups
    width = partial.shape[1]
    return pl.pallas_call(
        scatter_kernel,
        in_specs=[pl.BlockSpec(memory_space=pltpu.VMEM)],
        out_specs=pl.BlockSpec(memory_space=pltpu.VMEM),
        out_shape=jax.ShapeDtypeStruct((rows, width), jnp.float32),
        scratch_shapes=[
            pltpu.VMEM((chips, rows, width), partial.dtype),
            pltpu.VMEM((chips, rows, width), partial.dtype),
            pltpu.VMEM((chips, rows, width), partial.dtype),
            pltpu.SemaphoreType.DMA((chips,)),
            pltpu.SemaphoreType.DMA((chips,)),
            pltpu.SemaphoreType.DMA((chips,)),
            pltpu.SemaphoreType.DMA((chips,)),
        ],
        compiler_params=pltpu.CompilerParams(
            collective_id=1, has_side_effects=True, vmem_limit_bytes=48 * 1024 * 1024
        ),
    )(partial)


def per_device(
    tokens,
    token_owner,
    token_request,
    cache_len,
    cache_k,
    cache_v,
    w_qkv,
    w_out,
    w_fc1,
    w_fc2,
    ln1_gain,
    ln1_bias,
    ln2_gain,
    ln2_bias,
):
    n_req = lax.axis_size("req")
    n_mlp = lax.axis_size("mlp")
    devices = n_req * n_mlp
    owner_index = lax.axis_index("req") * n_mlp + lax.axis_index("mlp")
    tok_dev, width = tokens.shape
    capacity = max(2, 2 * tok_dev // devices)
    slot_count = devices * capacity
    owners_flat = token_owner.reshape(-1)
    my_owners = lax.dynamic_slice_in_dim(owners_flat, owner_index * tok_dev, tok_dev)
    owner_onehot = (my_owners[:, None] == jnp.arange(devices, dtype=jnp.int32)[None, :]).astype(
        jnp.int32
    )
    ranking = jnp.cumsum(owner_onehot, axis=0) - 1
    my_rank = jnp.sum(owner_onehot * ranking, axis=1)
    column = my_owners * capacity + my_rank
    dispatch = (column[:, None] == jnp.arange(slot_count, dtype=jnp.int32)[None, :]).astype(
        jnp.bfloat16
    )
    outgoing = jnp.einsum("tr,td->rd", dispatch, tokens, preferred_element_type=jnp.float32).astype(
        jnp.bfloat16
    )
    arrived = lax.all_to_all(
        outgoing.reshape(devices, capacity, width),
        ("req", "mlp"),
        split_axis=0,
        concat_axis=0,
        tiled=True,
    )
    projections = jnp.dot(
        arrived.reshape(slot_count, width), w_qkv, preferred_element_type=jnp.float32
    ).astype(jnp.bfloat16)
    global_row, slot_request, filled = slot_table(
        owners_flat, token_request, owner_index, devices, tok_dev, capacity
    )
    attended = attend(projections, cache_k, cache_v, cache_len, global_row, slot_request, filled)
    returned = lax.all_to_all(
        attended.reshape(devices, capacity, width),
        ("req", "mlp"),
        split_axis=0,
        concat_axis=0,
        tiled=True,
    )
    attn_rows = jnp.dot(
        dispatch, returned.reshape(slot_count, width), preferred_element_type=jnp.float32
    ).astype(jnp.bfloat16)
    projected_out = jnp.dot(attn_rows, w_out, preferred_element_type=jnp.float32)
    normed = layer_norm(projected_out + tokens.astype(jnp.float32), ln1_gain, ln1_bias).astype(
        jnp.bfloat16
    )
    gathered = lax.all_gather(normed, "mlp", axis=0, tiled=True)
    hidden = jax.nn.gelu(
        jnp.dot(gathered, w_fc1, preferred_element_type=jnp.float32), approximate=False
    ).astype(jnp.bfloat16)
    summed = scatter_sum(
        jnp.dot(hidden, w_fc2, preferred_element_type=jnp.float32).astype(jnp.bfloat16)
    )
    return layer_norm(normed.astype(jnp.float32) + summed, ln2_gain, ln2_bias).astype(jnp.bfloat16)


def solution(mesh):
    placed = (
        P(("req", "mlp"), None),
        P(),
        P(),
        P(("req", "mlp")),
        P(("req", "mlp"), None, None),
        P(("req", "mlp"), None, None),
        P(),
        P(),
        P(None, "mlp"),
        P("mlp", None),
        P(),
        P(),
        P(),
        P(),
    )
    return jax.shard_map(
        per_device, mesh=mesh, in_specs=placed, out_specs=P(("req", "mlp"), None), check_vma=False
    )
```

```python
import jax
import jax.numpy as jnp
from jax import lax
from jax.sharding import PartitionSpec as P
from jax.experimental import pallas as pl
from jax.experimental.pallas import tpu as pltpu

HEADS = 16


epsilon = 1e-05


def layer_norm(values, gain, shift):
    center = values - jnp.mean(values, axis=-1, keepdims=True)
    spread = jnp.mean(center * center, axis=-1, keepdims=True)
    return center * lax.rsqrt(spread + epsilon) * gain + shift


def slot_table(owners_flat, requests_flat, owner_index, devices, tok_dev, capacity):
    owners = owners_flat.reshape(devices, tok_dev)
    requests = requests_flat.reshape(devices, tok_dev)
    mine_mask = (owners == owner_index).astype(jnp.int32)
    ranking = jnp.cumsum(mine_mask, axis=1) - 1
    places = jnp.arange(capacity, dtype=jnp.int32)
    hit_table = mine_mask[:, :, None] * (ranking[:, :, None] == places[None, None, :]).astype(
        jnp.int32
    )
    filled = jnp.sum(hit_table, axis=1)
    positions = jnp.arange(tok_dev, dtype=jnp.int32)
    local_row = jnp.sum(hit_table * positions[None, :, None], axis=1)
    sources = jnp.arange(devices, dtype=jnp.int32)[:, None]
    global_row = jnp.where(filled > 0, sources * tok_dev + local_row, -1).reshape(-1)
    slot_request = jnp.sum(hit_table * requests[:, :, None], axis=1).reshape(-1)
    return (global_row, slot_request, filled.reshape(-1))


def attention_kernel(
    q_ref, kn_ref, vn_ref, k_ref, v_ref, rreq_ref, rrow_ref, rfill_ref, ctag_ref, ntag_ref, nrow_ref, o_ref
):
    head_dim = q_ref.shape[1] // 2
    score_scale = head_dim ** (-0.5)
    q = q_ref[...]
    keys = k_ref[...]
    values = v_ref[...]
    key_new = kn_ref[...]
    value_new = vn_ref[...]
    row_request = rreq_ref[...]
    old_mask = ctag_ref[...] == row_request
    new_mask = (ntag_ref[...] == row_request) & (nrow_ref[...] <= rrow_ref[...])
    lane = lax.broadcasted_iota(jnp.int32, (1, q.shape[1]), 1)
    contract = (((1,), (1,)), ((), ()))
    result = None
    for half in range(2):
        in_head = (lane // head_dim) == half
        q_head = jnp.where(in_head, q, jnp.zeros_like(q))
        old_score = (
            lax.dot_general(q_head, keys, contract, preferred_element_type=jnp.float32) * score_scale
        )
        new_score = (
            lax.dot_general(q_head, key_new, contract, preferred_element_type=jnp.float32)
            * score_scale
        )
        old_exp = jnp.where(old_mask, jnp.exp(old_score), jnp.float32(0.0))
        new_exp = jnp.where(new_mask, jnp.exp(new_score), jnp.float32(0.0))
        total = jnp.sum(old_exp, axis=1, keepdims=True) + jnp.sum(new_exp, axis=1, keepdims=True)
        total = jnp.where(total > 0, total, jnp.float32(1.0))
        inverse = 1.0 / total
        old_weight = (old_exp * inverse).astype(jnp.bfloat16)
        new_weight = (new_exp * inverse).astype(jnp.bfloat16)
        part = jnp.dot(old_weight, values, preferred_element_type=jnp.float32) + jnp.dot(
            new_weight, value_new, preferred_element_type=jnp.float32
        )
        result = part if result is None else jnp.where(in_head, part, result)
    result = jnp.where(rfill_ref[...] > 0, result, jnp.float32(0.0))
    o_ref[...] = result.astype(o_ref.dtype)


def attend(projections, cache_keys, cache_values, lengths, global_row, slot_request, filled):
    slot_count = projections.shape[0]
    width = projections.shape[1] // 3
    requests, context = cache_keys.shape[0], cache_keys.shape[1]
    pair = 128
    pairs = width // pair
    keys = cache_keys.reshape(requests * context, width)
    values = cache_values.reshape(requests * context, width)
    key_owner = jnp.arange(requests * context, dtype=jnp.int32) // context
    key_place = jnp.arange(requests * context, dtype=jnp.int32) % context
    key_limit = jnp.repeat(lengths, context)
    column_tag = jnp.where(key_place < key_limit, key_owner, -1).reshape(1, -1)
    new_tag = jnp.where(filled > 0, slot_request, -1).reshape(1, -1)
    new_row = global_row.reshape(1, -1)
    row_request = slot_request.reshape(-1, 1)
    row_index = global_row.reshape(-1, 1)
    row_filled = filled.reshape(-1, 1)
    keyed = requests * context
    whole = lambda shape: pl.BlockSpec(shape, lambda p: (0, 0))
    return pl.pallas_call(
        attention_kernel,
        grid=(pairs,),
        in_specs=[
            pl.BlockSpec((slot_count, pair), lambda p: (0, p)),
            pl.BlockSpec((slot_count, pair), lambda p: (0, pairs + p)),
            pl.BlockSpec((slot_count, pair), lambda p: (0, 2 * pairs + p)),
            pl.BlockSpec((keyed, pair), lambda p: (0, p)),
            pl.BlockSpec((keyed, pair), lambda p: (0, p)),
            whole((slot_count, 1)),
            whole((slot_count, 1)),
            whole((slot_count, 1)),
            whole((1, keyed)),
            whole((1, slot_count)),
            whole((1, slot_count)),
        ],
        out_specs=pl.BlockSpec((slot_count, pair), lambda p: (0, p)),
        out_shape=jax.ShapeDtypeStruct((slot_count, width), jnp.bfloat16),
        compiler_params=pltpu.CompilerParams(vmem_limit_bytes=48 * 1024 * 1024),
    )(
        projections,
        projections,
        projections,
        keys,
        values,
        row_request,
        row_index,
        row_filled,
        column_tag,
        new_tag,
        new_row,
    )


def scatter_kernel(part_ref, o_ref, pair_buf, send_buf, ring_buf, pair_send, pair_recv, ring_send, ring_recv):
    req = lax.axis_index("req")
    me = lax.axis_index("mlp")
    chips = lax.axis_size("mlp") // 2
    chip, core = me // 2, lax.rem(me, 2)
    partner = chip * 2 + 1 - core
    rows = o_ref.shape[0]
    barrier = pltpu.get_barrier_semaphore()
    pl.semaphore_signal(barrier, 1, device_id=(req, partner), device_id_type=pl.DeviceIdType.MESH)
    for k in range(1, chips):
        other = lax.rem(chip + k, chips) * 2 + core
        pl.semaphore_signal(barrier, 1, device_id=(req, other), device_id_type=pl.DeviceIdType.MESH)
    pl.semaphore_wait(barrier, chips)

    def pair_copy(z):
        block = z * 2 + 1 - core
        return pltpu.make_async_remote_copy(
            src_ref=part_ref.at[pl.ds(pl.multiple_of(block * rows, rows), rows)],
            dst_ref=pair_buf.at[z],
            send_sem=pair_send.at[z],
            recv_sem=pair_recv.at[z],
            device_id=(req, partner),
            device_id_type=pl.DeviceIdType.MESH,
        )

    for z in range(chips):
        pair_copy(z).start()
    for z in range(chips):
        pair_copy(z).wait()

    def ring_copy(k):
        target = lax.rem(chip + k, chips)
        return pltpu.make_async_remote_copy(
            src_ref=send_buf.at[k],
            dst_ref=ring_buf.at[k],
            send_sem=ring_send.at[k],
            recv_sem=ring_recv.at[k],
            device_id=(req, target * 2 + core),
            device_id_type=pl.DeviceIdType.MESH,
        )

    for k in range(1, chips):
        target = lax.rem(chip + k, chips)
        mine = part_ref[pl.ds(pl.multiple_of((target * 2 + core) * rows, rows), rows), :]
        send_buf[k] = (mine.astype(jnp.float32) + pair_buf[target].astype(jnp.float32)).astype(
            send_buf.dtype
        )
        ring_copy(k).start()
    own = part_ref[pl.ds(pl.multiple_of(me * rows, rows), rows), :]
    total = own.astype(jnp.float32) + pair_buf[chip].astype(jnp.float32)
    for k in range(1, chips):
        ring_copy(k).wait()
        total = total + ring_buf[k].astype(jnp.float32)
    o_ref[...] = total


def scatter_sum(partial):
    groups = lax.axis_size("mlp")
    chips = groups // 2
    rows = partial.shape[0] // groups
    width = partial.shape[1]
    return pl.pallas_call(
        scatter_kernel,
        in_specs=[pl.BlockSpec(memory_space=pltpu.VMEM)],
        out_specs=pl.BlockSpec(memory_space=pltpu.VMEM),
        out_shape=jax.ShapeDtypeStruct((rows, width), jnp.float32),
        scratch_shapes=[
            pltpu.VMEM((chips, rows, width), partial.dtype),
            pltpu.VMEM((chips, rows, width), partial.dtype),
            pltpu.VMEM((chips, rows, width), partial.dtype),
            pltpu.SemaphoreType.DMA((chips,)),
            pltpu.SemaphoreType.DMA((chips,)),
            pltpu.SemaphoreType.DMA((chips,)),
            pltpu.SemaphoreType.DMA((chips,)),
        ],
        compiler_params=pltpu.CompilerParams(
            collective_id=1, has_side_effects=True, vmem_limit_bytes=48 * 1024 * 1024
        ),
    )(partial)


def gather_kernel(x_ref, o_ref, ring_send, ring_recv, pair_send, pair_recv):
    req = lax.axis_index("req")
    me = lax.axis_index("mlp")
    chips = lax.axis_size("mlp") // 2
    chip, core = me // 2, lax.rem(me, 2)
    partner = chip * 2 + 1 - core
    rows = x_ref.shape[0]
    barrier = pltpu.get_barrier_semaphore()
    pl.semaphore_signal(barrier, 1, device_id=(req, partner), device_id_type=pl.DeviceIdType.MESH)
    for k in range(1, chips):
        other = lax.rem(chip + k, chips) * 2 + core
        pl.semaphore_signal(barrier, 1, device_id=(req, other), device_id_type=pl.DeviceIdType.MESH)
    pl.semaphore_wait(barrier, chips)

    def block_rows(block):
        return pl.ds(pl.multiple_of(block * rows, rows), rows)

    def ring_copy(k):
        target = lax.rem(chip + k, chips)
        return pltpu.make_async_remote_copy(
            src_ref=x_ref,
            dst_ref=o_ref.at[block_rows(me)],
            send_sem=ring_send.at[k],
            recv_sem=ring_recv.at[k],
            device_id=(req, target * 2 + core),
            device_id_type=pl.DeviceIdType.MESH,
        )

    def pair_copy(k):
        source = lax.rem(chip + chips - k, chips) * 2 + core
        return pltpu.make_async_remote_copy(
            src_ref=x_ref if k == 0 else o_ref.at[block_rows(source)],
            dst_ref=o_ref.at[block_rows(source)],
            send_sem=pair_send.at[k],
            recv_sem=pair_recv.at[k],
            device_id=(req, partner),
            device_id_type=pl.DeviceIdType.MESH,
        )

    for k in range(1, chips):
        ring_copy(k).start()
    pair_copy(0).start()
    o_ref[block_rows(me), :] = x_ref[...]
    for k in range(1, chips):
        ring_copy(k).wait_recv()
        pair_copy(k).start()
    for k in range(1, chips):
        ring_copy(k).wait_send()
    for k in range(chips):
        pair_copy(k).wait()


def gather_rows(block):
    groups = lax.axis_size("mlp")
    chips = groups // 2
    return pl.pallas_call(
        gather_kernel,
        in_specs=[pl.BlockSpec(memory_space=pltpu.VMEM)],
        out_specs=pl.BlockSpec(memory_space=pltpu.VMEM),
        out_shape=jax.ShapeDtypeStruct((groups * block.shape[0], block.shape[1]), block.dtype),
        scratch_shapes=[
            pltpu.SemaphoreType.DMA((chips,)),
            pltpu.SemaphoreType.DMA((chips,)),
            pltpu.SemaphoreType.DMA((chips,)),
            pltpu.SemaphoreType.DMA((chips,)),
        ],
        compiler_params=pltpu.CompilerParams(
            collective_id=2, has_side_effects=True, vmem_limit_bytes=48 * 1024 * 1024
        ),
    )(block)


def per_device(
    tokens,
    token_owner,
    token_request,
    cache_len,
    cache_k,
    cache_v,
    w_qkv,
    w_out,
    w_fc1,
    w_fc2,
    ln1_gain,
    ln1_bias,
    ln2_gain,
    ln2_bias,
):
    n_req = lax.axis_size("req")
    n_mlp = lax.axis_size("mlp")
    devices = n_req * n_mlp
    owner_index = lax.axis_index("req") * n_mlp + lax.axis_index("mlp")
    tok_dev, width = tokens.shape
    capacity = max(2, 2 * tok_dev // devices)
    slot_count = devices * capacity
    owners_flat = token_owner.reshape(-1)
    my_owners = lax.dynamic_slice_in_dim(owners_flat, owner_index * tok_dev, tok_dev)
    owner_onehot = (my_owners[:, None] == jnp.arange(devices, dtype=jnp.int32)[None, :]).astype(
        jnp.int32
    )
    ranking = jnp.cumsum(owner_onehot, axis=0) - 1
    my_rank = jnp.sum(owner_onehot * ranking, axis=1)
    column = my_owners * capacity + my_rank
    dispatch = (column[:, None] == jnp.arange(slot_count, dtype=jnp.int32)[None, :]).astype(
        jnp.bfloat16
    )
    outgoing = jnp.einsum("tr,td->rd", dispatch, tokens, preferred_element_type=jnp.float32).astype(
        jnp.bfloat16
    )
    arrived = lax.all_to_all(
        outgoing.reshape(devices, capacity, width),
        ("req", "mlp"),
        split_axis=0,
        concat_axis=0,
        tiled=True,
    )
    projections = jnp.dot(
        arrived.reshape(slot_count, width), w_qkv, preferred_element_type=jnp.float32
    ).astype(jnp.bfloat16)
    global_row, slot_request, filled = slot_table(
        owners_flat, token_request, owner_index, devices, tok_dev, capacity
    )
    attended = attend(projections, cache_k, cache_v, cache_len, global_row, slot_request, filled)
    returned = lax.all_to_all(
        attended.reshape(devices, capacity, width),
        ("req", "mlp"),
        split_axis=0,
        concat_axis=0,
        tiled=True,
    )
    attn_rows = jnp.dot(
        dispatch, returned.reshape(slot_count, width), preferred_element_type=jnp.float32
    ).astype(jnp.bfloat16)
    projected_out = jnp.dot(attn_rows, w_out, preferred_element_type=jnp.float32)
    normed = layer_norm(projected_out + tokens.astype(jnp.float32), ln1_gain, ln1_bias).astype(
        jnp.bfloat16
    )
    gathered = gather_rows(normed)
    hidden = jax.nn.gelu(
        jnp.dot(gathered, w_fc1, preferred_element_type=jnp.float32), approximate=False
    ).astype(jnp.bfloat16)
    summed = scatter_sum(
        jnp.dot(hidden, w_fc2, preferred_element_type=jnp.float32).astype(jnp.bfloat16)
    )
    return layer_norm(normed.astype(jnp.float32) + summed, ln2_gain, ln2_bias).astype(jnp.bfloat16)


def solution(mesh):
    placed = (
        P(("req", "mlp"), None),
        P(),
        P(),
        P(("req", "mlp")),
        P(("req", "mlp"), None, None),
        P(("req", "mlp"), None, None),
        P(),
        P(),
        P(None, "mlp"),
        P("mlp", None),
        P(),
        P(),
        P(),
        P(),
    )
    return jax.shard_map(
        per_device, mesh=mesh, in_specs=placed, out_specs=P(("req", "mlp"), None), check_vma=False
    )
```

```python
import functools

import jax
import jax.numpy as jnp
from jax import lax
from jax.sharding import PartitionSpec as P
from jax.experimental import pallas as pl
from jax.experimental.pallas import tpu as pltpu

HEADS = 16


epsilon = 1e-05


def layer_norm(values, gain, shift):
    center = values - jnp.mean(values, axis=-1, keepdims=True)
    spread = jnp.mean(center * center, axis=-1, keepdims=True)
    return center * lax.rsqrt(spread + epsilon) * gain + shift


def slot_table(owners_flat, requests_flat, owner_index, devices, tok_dev, capacity):
    owners = owners_flat.reshape(devices, tok_dev)
    requests = requests_flat.reshape(devices, tok_dev)
    mine_mask = (owners == owner_index).astype(jnp.int32)
    ranking = jnp.cumsum(mine_mask, axis=1) - 1
    places = jnp.arange(capacity, dtype=jnp.int32)
    hit_table = mine_mask[:, :, None] * (ranking[:, :, None] == places[None, None, :]).astype(
        jnp.int32
    )
    filled = jnp.sum(hit_table, axis=1)
    positions = jnp.arange(tok_dev, dtype=jnp.int32)
    local_row = jnp.sum(hit_table * positions[None, :, None], axis=1)
    sources = jnp.arange(devices, dtype=jnp.int32)[:, None]
    global_row = jnp.where(filled > 0, sources * tok_dev + local_row, -1).reshape(-1)
    slot_request = jnp.sum(hit_table * requests[:, :, None], axis=1).reshape(-1)
    return (global_row, slot_request, filled.reshape(-1))


def attention_kernel(
    q_ref, kn_ref, vn_ref, k_ref, v_ref, rreq_ref, rrow_ref, rfill_ref, ctag_ref, ntag_ref, nrow_ref, o_ref
):
    head_dim = q_ref.shape[1] // 2
    score_scale = head_dim ** (-0.5)
    q = q_ref[...]
    keys = k_ref[...]
    values = v_ref[...]
    key_new = kn_ref[...]
    value_new = vn_ref[...]
    row_request = rreq_ref[...]
    old_mask = ctag_ref[...] == row_request
    new_mask = (ntag_ref[...] == row_request) & (nrow_ref[...] <= rrow_ref[...])
    lane = lax.broadcasted_iota(jnp.int32, (1, q.shape[1]), 1)
    contract = (((1,), (1,)), ((), ()))
    result = None
    for half in range(2):
        in_head = (lane // head_dim) == half
        q_head = jnp.where(in_head, q, jnp.zeros_like(q))
        old_score = (
            lax.dot_general(q_head, keys, contract, preferred_element_type=jnp.float32) * score_scale
        )
        new_score = (
            lax.dot_general(q_head, key_new, contract, preferred_element_type=jnp.float32)
            * score_scale
        )
        old_exp = jnp.where(old_mask, jnp.exp(old_score), jnp.float32(0.0))
        new_exp = jnp.where(new_mask, jnp.exp(new_score), jnp.float32(0.0))
        total = jnp.sum(old_exp, axis=1, keepdims=True) + jnp.sum(new_exp, axis=1, keepdims=True)
        total = jnp.where(total > 0, total, jnp.float32(1.0))
        inverse = 1.0 / total
        old_weight = (old_exp * inverse).astype(jnp.bfloat16)
        new_weight = (new_exp * inverse).astype(jnp.bfloat16)
        part = jnp.dot(old_weight, values, preferred_element_type=jnp.float32) + jnp.dot(
            new_weight, value_new, preferred_element_type=jnp.float32
        )
        result = part if result is None else jnp.where(in_head, part, result)
    result = jnp.where(rfill_ref[...] > 0, result, jnp.float32(0.0))
    o_ref[...] = result.astype(o_ref.dtype)


def attend(projections, cache_keys, cache_values, lengths, global_row, slot_request, filled):
    slot_count = projections.shape[0]
    width = projections.shape[1] // 3
    requests, context = cache_keys.shape[0], cache_keys.shape[1]
    pair = 128
    pairs = width // pair
    keys = cache_keys.reshape(requests * context, width)
    values = cache_values.reshape(requests * context, width)
    key_owner = jnp.arange(requests * context, dtype=jnp.int32) // context
    key_place = jnp.arange(requests * context, dtype=jnp.int32) % context
    key_limit = jnp.repeat(lengths, context)
    column_tag = jnp.where(key_place < key_limit, key_owner, -1).reshape(1, -1)
    new_tag = jnp.where(filled > 0, slot_request, -1).reshape(1, -1)
    new_row = global_row.reshape(1, -1)
    row_request = slot_request.reshape(-1, 1)
    row_index = global_row.reshape(-1, 1)
    row_filled = filled.reshape(-1, 1)
    keyed = requests * context
    whole = lambda shape: pl.BlockSpec(shape, lambda p: (0, 0))
    return pl.pallas_call(
        attention_kernel,
        grid=(pairs,),
        in_specs=[
            pl.BlockSpec((slot_count, pair), lambda p: (0, p)),
            pl.BlockSpec((slot_count, pair), lambda p: (0, pairs + p)),
            pl.BlockSpec((slot_count, pair), lambda p: (0, 2 * pairs + p)),
            pl.BlockSpec((keyed, pair), lambda p: (0, p)),
            pl.BlockSpec((keyed, pair), lambda p: (0, p)),
            whole((slot_count, 1)),
            whole((slot_count, 1)),
            whole((slot_count, 1)),
            whole((1, keyed)),
            whole((1, slot_count)),
            whole((1, slot_count)),
        ],
        out_specs=pl.BlockSpec((slot_count, pair), lambda p: (0, p)),
        out_shape=jax.ShapeDtypeStruct((slot_count, width), jnp.bfloat16),
        compiler_params=pltpu.CompilerParams(vmem_limit_bytes=48 * 1024 * 1024),
    )(
        projections,
        projections,
        projections,
        keys,
        values,
        row_request,
        row_index,
        row_filled,
        column_tag,
        new_tag,
        new_row,
    )


def scatter_kernel(part_ref, o_ref, pair_buf, send_buf, ring_buf, pair_send, pair_recv, ring_send, ring_recv):
    req = lax.axis_index("req")
    me = lax.axis_index("mlp")
    chips = lax.axis_size("mlp") // 2
    chip, core = me // 2, lax.rem(me, 2)
    partner = chip * 2 + 1 - core
    rows = o_ref.shape[0]
    barrier = pltpu.get_barrier_semaphore()
    pl.semaphore_signal(barrier, 1, device_id=(req, partner), device_id_type=pl.DeviceIdType.MESH)
    for k in range(1, chips):
        other = lax.rem(chip + k, chips) * 2 + core
        pl.semaphore_signal(barrier, 1, device_id=(req, other), device_id_type=pl.DeviceIdType.MESH)
    pl.semaphore_wait(barrier, chips)

    def pair_copy(z):
        block = z * 2 + 1 - core
        return pltpu.make_async_remote_copy(
            src_ref=part_ref.at[pl.ds(pl.multiple_of(block * rows, rows), rows)],
            dst_ref=pair_buf.at[z],
            send_sem=pair_send.at[z],
            recv_sem=pair_recv.at[z],
            device_id=(req, partner),
            device_id_type=pl.DeviceIdType.MESH,
        )

    for z in range(chips):
        pair_copy(z).start()
    for z in range(chips):
        pair_copy(z).wait()

    def ring_copy(k):
        target = lax.rem(chip + k, chips)
        return pltpu.make_async_remote_copy(
            src_ref=send_buf.at[k],
            dst_ref=ring_buf.at[k],
            send_sem=ring_send.at[k],
            recv_sem=ring_recv.at[k],
            device_id=(req, target * 2 + core),
            device_id_type=pl.DeviceIdType.MESH,
        )

    for k in range(1, chips):
        target = lax.rem(chip + k, chips)
        mine = part_ref[pl.ds(pl.multiple_of((target * 2 + core) * rows, rows), rows), :]
        send_buf[k] = (mine.astype(jnp.float32) + pair_buf[target].astype(jnp.float32)).astype(
            send_buf.dtype
        )
        ring_copy(k).start()
    own = part_ref[pl.ds(pl.multiple_of(me * rows, rows), rows), :]
    total = own.astype(jnp.float32) + pair_buf[chip].astype(jnp.float32)
    for k in range(1, chips):
        ring_copy(k).wait()
        total = total + ring_buf[k].astype(jnp.float32)
    o_ref[...] = total


def scatter_sum(partial):
    groups = lax.axis_size("mlp")
    chips = groups // 2
    rows = partial.shape[0] // groups
    width = partial.shape[1]
    return pl.pallas_call(
        scatter_kernel,
        in_specs=[pl.BlockSpec(memory_space=pltpu.VMEM)],
        out_specs=pl.BlockSpec(memory_space=pltpu.VMEM),
        out_shape=jax.ShapeDtypeStruct((rows, width), jnp.float32),
        scratch_shapes=[
            pltpu.VMEM((chips, rows, width), partial.dtype),
            pltpu.VMEM((chips, rows, width), partial.dtype),
            pltpu.VMEM((chips, rows, width), partial.dtype),
            pltpu.SemaphoreType.DMA((chips,)),
            pltpu.SemaphoreType.DMA((chips,)),
            pltpu.SemaphoreType.DMA((chips,)),
            pltpu.SemaphoreType.DMA((chips,)),
        ],
        compiler_params=pltpu.CompilerParams(
            collective_id=1, has_side_effects=True, vmem_limit_bytes=48 * 1024 * 1024
        ),
    )(partial)


def gather_kernel(x_ref, o_ref, ring_send, ring_recv, pair_send, pair_recv):
    req = lax.axis_index("req")
    me = lax.axis_index("mlp")
    chips = lax.axis_size("mlp") // 2
    chip, core = me // 2, lax.rem(me, 2)
    partner = chip * 2 + 1 - core
    rows = x_ref.shape[0]
    barrier = pltpu.get_barrier_semaphore()
    pl.semaphore_signal(barrier, 1, device_id=(req, partner), device_id_type=pl.DeviceIdType.MESH)
    for k in range(1, chips):
        other = lax.rem(chip + k, chips) * 2 + core
        pl.semaphore_signal(barrier, 1, device_id=(req, other), device_id_type=pl.DeviceIdType.MESH)
    pl.semaphore_wait(barrier, chips)

    def block_rows(block):
        return pl.ds(pl.multiple_of(block * rows, rows), rows)

    def ring_copy(k):
        target = lax.rem(chip + k, chips)
        return pltpu.make_async_remote_copy(
            src_ref=x_ref,
            dst_ref=o_ref.at[block_rows(me)],
            send_sem=ring_send.at[k],
            recv_sem=ring_recv.at[k],
            device_id=(req, target * 2 + core),
            device_id_type=pl.DeviceIdType.MESH,
        )

    def pair_copy(k):
        source = lax.rem(chip + chips - k, chips) * 2 + core
        return pltpu.make_async_remote_copy(
            src_ref=x_ref if k == 0 else o_ref.at[block_rows(source)],
            dst_ref=o_ref.at[block_rows(source)],
            send_sem=pair_send.at[k],
            recv_sem=pair_recv.at[k],
            device_id=(req, partner),
            device_id_type=pl.DeviceIdType.MESH,
        )

    for k in range(1, chips):
        ring_copy(k).start()
    pair_copy(0).start()
    o_ref[block_rows(me), :] = x_ref[...]
    for k in range(1, chips):
        ring_copy(k).wait_recv()
        pair_copy(k).start()
    for k in range(1, chips):
        ring_copy(k).wait_send()
    for k in range(chips):
        pair_copy(k).wait()


def gather_rows(block):
    groups = lax.axis_size("mlp")
    chips = groups // 2
    return pl.pallas_call(
        gather_kernel,
        in_specs=[pl.BlockSpec(memory_space=pltpu.VMEM)],
        out_specs=pl.BlockSpec(memory_space=pltpu.VMEM),
        out_shape=jax.ShapeDtypeStruct((groups * block.shape[0], block.shape[1]), block.dtype),
        scratch_shapes=[
            pltpu.SemaphoreType.DMA((chips,)),
            pltpu.SemaphoreType.DMA((chips,)),
            pltpu.SemaphoreType.DMA((chips,)),
            pltpu.SemaphoreType.DMA((chips,)),
        ],
        compiler_params=pltpu.CompilerParams(
            collective_id=2, has_side_effects=True, vmem_limit_bytes=48 * 1024 * 1024
        ),
    )(block)


def staged_kernel(first, second, strided_out, x_ref, o_ref, mid, sends, recvs, locals_):
    axes = {"req": lax.axis_index("req"), "mlp": lax.axis_index("mlp")}
    n1, n2 = x_ref.shape[0], x_ref.shape[1]
    me1, me2 = axes[first], axes[second]

    def device(one, two):
        coords = {first: one, second: two}
        return (coords["req"], coords["mlp"])

    barrier = pltpu.get_barrier_semaphore()
    for k in range(1, n1):
        pl.semaphore_signal(
            barrier, 1, device_id=device(lax.rem(me1 + k, n1), me2), device_id_type=pl.DeviceIdType.MESH
        )
    for k in range(1, n2):
        pl.semaphore_signal(
            barrier, 1, device_id=device(me1, lax.rem(me2 + k, n2)), device_id_type=pl.DeviceIdType.MESH
        )
    pl.semaphore_wait(barrier, n1 + n2 - 2)

    def out_view(index):
        return o_ref.at[:, index] if strided_out else o_ref.at[index]

    def stage_one(k):
        target = lax.rem(me1 + k, n1)
        return pltpu.make_async_remote_copy(
            src_ref=x_ref.at[target],
            dst_ref=mid.at[:, me1],
            send_sem=sends.at[0, k],
            recv_sem=recvs.at[0, k],
            device_id=device(target, me2),
            device_id_type=pl.DeviceIdType.MESH,
        )

    def stage_two(k):
        target = lax.rem(me2 + k, n2)
        return pltpu.make_async_remote_copy(
            src_ref=mid.at[target],
            dst_ref=out_view(me2),
            send_sem=sends.at[1, k],
            recv_sem=recvs.at[1, k],
            device_id=device(me1, target),
            device_id_type=pl.DeviceIdType.MESH,
        )

    own_one = pltpu.make_async_copy(x_ref.at[me1], mid.at[:, me1], locals_.at[0])
    own_one.start()
    for k in range(1, n1):
        stage_one(k).start()
    own_one.wait()
    for k in range(1, n1):
        stage_one(k).wait()
    own_two = pltpu.make_async_copy(mid.at[me2], out_view(me2), locals_.at[1])
    own_two.start()
    for k in range(1, n2):
        stage_two(k).start()
    own_two.wait()
    for k in range(1, n2):
        stage_two(k).wait()


def staged_exchange(blocks, first, second, strided_out, ident):
    n1, n2 = blocks.shape[0], blocks.shape[1]
    rest = blocks.shape[2:]
    out_shape = (n2, n1) + rest if not strided_out else (n1, n2) + rest
    most = max(n1, n2)
    return pl.pallas_call(
        functools.partial(staged_kernel, first, second, strided_out),
        in_specs=[pl.BlockSpec(memory_space=pl.ANY)],
        out_specs=pl.BlockSpec(memory_space=pl.ANY),
        out_shape=jax.ShapeDtypeStruct(out_shape, blocks.dtype),
        scratch_shapes=[
            pltpu.VMEM((n2, n1) + rest, blocks.dtype),
            pltpu.SemaphoreType.DMA((2, most)),
            pltpu.SemaphoreType.DMA((2, most)),
            pltpu.SemaphoreType.DMA((2,)),
        ],
        compiler_params=pltpu.CompilerParams(collective_id=ident, has_side_effects=True),
    )(blocks)


def per_device(
    tokens,
    token_owner,
    token_request,
    cache_len,
    cache_k,
    cache_v,
    w_qkv,
    w_out,
    w_fc1,
    w_fc2,
    ln1_gain,
    ln1_bias,
    ln2_gain,
    ln2_bias,
):
    n_req = lax.axis_size("req")
    n_mlp = lax.axis_size("mlp")
    devices = n_req * n_mlp
    owner_index = lax.axis_index("req") * n_mlp + lax.axis_index("mlp")
    tok_dev, width = tokens.shape
    capacity = max(2, 2 * tok_dev // devices)
    slot_count = devices * capacity
    owners_flat = token_owner.reshape(-1)
    my_owners = lax.dynamic_slice_in_dim(owners_flat, owner_index * tok_dev, tok_dev)
    owner_onehot = (my_owners[:, None] == jnp.arange(devices, dtype=jnp.int32)[None, :]).astype(
        jnp.int32
    )
    ranking = jnp.cumsum(owner_onehot, axis=0) - 1
    my_rank = jnp.sum(owner_onehot * ranking, axis=1)
    column = my_owners * capacity + my_rank
    dispatch = (column[:, None] == jnp.arange(slot_count, dtype=jnp.int32)[None, :]).astype(
        jnp.bfloat16
    )
    send_column = ((my_owners % n_mlp) * n_req + my_owners // n_mlp) * capacity + my_rank
    send_dispatch = (
        send_column[:, None] == jnp.arange(slot_count, dtype=jnp.int32)[None, :]
    ).astype(jnp.bfloat16)
    outgoing = jnp.einsum(
        "tr,td->rd", send_dispatch, tokens, preferred_element_type=jnp.float32
    ).astype(jnp.bfloat16)
    arrived = staged_exchange(
        outgoing.reshape(n_mlp, n_req, capacity, width), "mlp", "req", False, 3
    )
    projections = jnp.dot(
        arrived.reshape(slot_count, width), w_qkv, preferred_element_type=jnp.float32
    ).astype(jnp.bfloat16)
    global_row, slot_request, filled = slot_table(
        owners_flat, token_request, owner_index, devices, tok_dev, capacity
    )
    attended = attend(projections, cache_k, cache_v, cache_len, global_row, slot_request, filled)
    returned = staged_exchange(
        attended.reshape(n_req, n_mlp, capacity, width), "req", "mlp", True, 4
    )
    attn_rows = jnp.dot(
        dispatch, returned.reshape(slot_count, width), preferred_element_type=jnp.float32
    ).astype(jnp.bfloat16)
    projected_out = jnp.dot(attn_rows, w_out, preferred_element_type=jnp.float32)
    normed = layer_norm(projected_out + tokens.astype(jnp.float32), ln1_gain, ln1_bias).astype(
        jnp.bfloat16
    )
    gathered = gather_rows(normed)
    hidden = jax.nn.gelu(
        jnp.dot(gathered, w_fc1, preferred_element_type=jnp.float32), approximate=False
    ).astype(jnp.bfloat16)
    summed = scatter_sum(
        jnp.dot(hidden, w_fc2, preferred_element_type=jnp.float32).astype(jnp.bfloat16)
    )
    return layer_norm(normed.astype(jnp.float32) + summed, ln2_gain, ln2_bias).astype(jnp.bfloat16)


def solution(mesh):
    placed = (
        P(("req", "mlp"), None),
        P(),
        P(),
        P(("req", "mlp")),
        P(("req", "mlp"), None, None),
        P(("req", "mlp"), None, None),
        P(),
        P(),
        P(None, "mlp"),
        P("mlp", None),
        P(),
        P(),
        P(),
        P(),
    )
    return jax.shard_map(
        per_device, mesh=mesh, in_specs=placed, out_specs=P(("req", "mlp"), None), check_vma=False
    )
```

```python
import jax
import jax.numpy as jnp
from jax import lax
from jax.sharding import PartitionSpec as P
from jax.experimental import pallas as pl
from jax.experimental.pallas import tpu as pltpu

HEADS = 16


epsilon = 1e-05


def layer_norm(values, gain, shift):
    center = values - jnp.mean(values, axis=-1, keepdims=True)
    spread = jnp.mean(center * center, axis=-1, keepdims=True)
    return center * lax.rsqrt(spread + epsilon) * gain + shift


def slot_table(owners_flat, requests_flat, owner_index, devices, tok_dev, capacity):
    owners = owners_flat.reshape(devices, tok_dev)
    requests = requests_flat.reshape(devices, tok_dev)
    mine_mask = (owners == owner_index).astype(jnp.int32)
    ranking = jnp.cumsum(mine_mask, axis=1) - 1
    places = jnp.arange(capacity, dtype=jnp.int32)
    hit_table = mine_mask[:, :, None] * (ranking[:, :, None] == places[None, None, :]).astype(
        jnp.int32
    )
    filled = jnp.sum(hit_table, axis=1)
    positions = jnp.arange(tok_dev, dtype=jnp.int32)
    local_row = jnp.sum(hit_table * positions[None, :, None], axis=1)
    sources = jnp.arange(devices, dtype=jnp.int32)[:, None]
    global_row = jnp.where(filled > 0, sources * tok_dev + local_row, -1).reshape(-1)
    slot_request = jnp.sum(hit_table * requests[:, :, None], axis=1).reshape(-1)
    return (global_row, slot_request, filled.reshape(-1))


def attention_kernel(
    tiles_ref, q_ref, kn_ref, vn_ref, k_ref, v_ref, rreq_ref, rrow_ref, ctag_ref, ntag_ref, nrow_ref, o_ref
):
    head_dim = q_ref.shape[1] // 2
    score_scale = head_dim ** (-0.5)
    requests = tiles_ref.shape[0] // 2
    context = k_ref.shape[0] // requests
    tile = 64
    lane = lax.broadcasted_iota(jnp.int32, (1, q_ref.shape[1]), 1)
    contract = (((1,), (1,)), ((), ()))
    key_new = kn_ref[...]
    value_new = vn_ref[...]
    new_tag = ntag_ref[...]
    new_row = nrow_ref[...]
    o_ref[...] = jnp.zeros(o_ref.shape, o_ref.dtype)
    for request in range(requests):
        keys = k_ref[request * context : (request + 1) * context, :]
        values = v_ref[request * context : (request + 1) * context, :]
        column_tag = ctag_ref[:, request * context : (request + 1) * context]

        def body(t, carry):
            rows = pl.ds(pl.multiple_of(t * tile, tile), tile)
            q = q_ref[rows, :] * jnp.asarray(score_scale, q_ref.dtype)
            row_request = rreq_ref[rows, :]
            old_mask = column_tag == row_request
            new_mask = (new_tag == row_request) & (new_row <= rrow_ref[rows, :])
            result = None
            for half in range(2):
                in_head = (lane // head_dim) == half
                q_head = jnp.where(in_head, q, jnp.zeros_like(q))
                old_score = lax.dot_general(q_head, keys, contract, preferred_element_type=jnp.float32)
                new_score = lax.dot_general(q_head, key_new, contract, preferred_element_type=jnp.float32)
                old_exp = jnp.where(old_mask, jnp.exp(old_score), jnp.float32(0.0))
                new_exp = jnp.where(new_mask, jnp.exp(new_score), jnp.float32(0.0))
                total = jnp.sum(old_exp, axis=1, keepdims=True) + jnp.sum(new_exp, axis=1, keepdims=True)
                total = jnp.where(total > 0, total, jnp.float32(1.0))
                inverse = 1.0 / total
                old_weight = (old_exp * inverse).astype(jnp.bfloat16)
                new_weight = (new_exp * inverse).astype(jnp.bfloat16)
                part = jnp.dot(old_weight, values, preferred_element_type=jnp.float32) + jnp.dot(
                    new_weight, value_new, preferred_element_type=jnp.float32
                )
                result = part if result is None else jnp.where(in_head, part, result)
            previous = o_ref[rows, :]
            o_ref[rows, :] = jnp.where(row_request == request, result.astype(o_ref.dtype), previous)
            return carry

        lax.fori_loop(tiles_ref[request], tiles_ref[requests + request], body, 0)


def attend(projections, cache_keys, cache_values, lengths, global_row, slot_request, filled):
    slot_count = projections.shape[0]
    width = projections.shape[1] // 3
    requests, context = cache_keys.shape[0], cache_keys.shape[1]
    pair = 128
    pairs = width // pair
    tile = 64
    keys = cache_keys.reshape(requests * context, width)
    values = cache_values.reshape(requests * context, width)
    key_owner = jnp.arange(requests * context, dtype=jnp.int32) // context
    key_place = jnp.arange(requests * context, dtype=jnp.int32) % context
    key_limit = jnp.repeat(lengths, context)
    column_tag = jnp.where(key_place < key_limit, key_owner, -1).reshape(1, -1)
    sort_key = jnp.where(filled > 0, slot_request, requests)
    key_hot = (sort_key[:, None] == jnp.arange(requests + 1, dtype=jnp.int32)[None, :]).astype(jnp.int32)
    counts = jnp.sum(key_hot, axis=0)
    starts = jnp.cumsum(counts) - counts
    before = jnp.cumsum(key_hot, axis=0) - key_hot
    position = jnp.sum(key_hot * (starts[None, :] + before), axis=1)
    order = position[None, :] == jnp.arange(slot_count, dtype=jnp.int32)[:, None]
    order_int = order.astype(jnp.int32)
    sorted_projections = jnp.dot(
        order.astype(projections.dtype), projections, preferred_element_type=jnp.float32
    ).astype(projections.dtype)
    sorted_key = jnp.sum(order_int * sort_key[None, :], axis=1)
    sorted_row = jnp.sum(order_int * global_row[None, :], axis=1)
    first = starts[:requests] // tile
    last = jnp.where(
        counts[:requests] > 0, (starts[:requests] + counts[:requests] + tile - 1) // tile, first
    )
    tiles = jnp.concatenate([first, last]).astype(jnp.int32)
    whole = lambda shape: pl.BlockSpec(shape, lambda p, t: (0, 0))
    keyed = requests * context
    sorted_out = pl.pallas_call(
        attention_kernel,
        grid_spec=pltpu.PrefetchScalarGridSpec(
            num_scalar_prefetch=1,
            grid=(pairs,),
            in_specs=[
                pl.BlockSpec((slot_count, pair), lambda p, t: (0, p)),
                pl.BlockSpec((slot_count, pair), lambda p, t: (0, pairs + p)),
                pl.BlockSpec((slot_count, pair), lambda p, t: (0, 2 * pairs + p)),
                pl.BlockSpec((keyed, pair), lambda p, t: (0, p)),
                pl.BlockSpec((keyed, pair), lambda p, t: (0, p)),
                whole((slot_count, 1)),
                whole((slot_count, 1)),
                whole((1, keyed)),
                whole((1, slot_count)),
                whole((1, slot_count)),
            ],
            out_specs=pl.BlockSpec((slot_count, pair), lambda p, t: (0, p)),
        ),
        out_shape=jax.ShapeDtypeStruct((slot_count, width), jnp.bfloat16),
        compiler_params=pltpu.CompilerParams(vmem_limit_bytes=48 * 1024 * 1024),
    )(
        tiles,
        sorted_projections,
        sorted_projections,
        sorted_projections,
        keys,
        values,
        sorted_key.reshape(-1, 1),
        sorted_row.reshape(-1, 1),
        column_tag,
        sorted_key.reshape(1, -1),
        sorted_row.reshape(1, -1),
    )
    return jnp.dot(
        order.T.astype(sorted_out.dtype), sorted_out, preferred_element_type=jnp.float32
    ).astype(sorted_out.dtype)


def scatter_kernel(part_ref, o_ref, pair_buf, send_buf, ring_buf, pair_send, pair_recv, ring_send, ring_recv):
    req = lax.axis_index("req")
    me = lax.axis_index("mlp")
    chips = lax.axis_size("mlp") // 2
    chip, core = me // 2, lax.rem(me, 2)
    partner = chip * 2 + 1 - core
    rows = o_ref.shape[0]
    barrier = pltpu.get_barrier_semaphore()
    pl.semaphore_signal(barrier, 1, device_id=(req, partner), device_id_type=pl.DeviceIdType.MESH)
    for k in range(1, chips):
        other = lax.rem(chip + k, chips) * 2 + core
        pl.semaphore_signal(barrier, 1, device_id=(req, other), device_id_type=pl.DeviceIdType.MESH)
    pl.semaphore_wait(barrier, chips)

    def pair_copy(z):
        block = z * 2 + 1 - core
        return pltpu.make_async_remote_copy(
            src_ref=part_ref.at[pl.ds(pl.multiple_of(block * rows, rows), rows)],
            dst_ref=pair_buf.at[z],
            send_sem=pair_send.at[z],
            recv_sem=pair_recv.at[z],
            device_id=(req, partner),
            device_id_type=pl.DeviceIdType.MESH,
        )

    for z in range(chips):
        pair_copy(z).start()
    for z in range(chips):
        pair_copy(z).wait()

    def ring_copy(k):
        target = lax.rem(chip + k, chips)
        return pltpu.make_async_remote_copy(
            src_ref=send_buf.at[k],
            dst_ref=ring_buf.at[k],
            send_sem=ring_send.at[k],
            recv_sem=ring_recv.at[k],
            device_id=(req, target * 2 + core),
            device_id_type=pl.DeviceIdType.MESH,
        )

    for k in range(1, chips):
        target = lax.rem(chip + k, chips)
        mine = part_ref[pl.ds(pl.multiple_of((target * 2 + core) * rows, rows), rows), :]
        send_buf[k] = (mine.astype(jnp.float32) + pair_buf[target].astype(jnp.float32)).astype(
            send_buf.dtype
        )
        ring_copy(k).start()
    own = part_ref[pl.ds(pl.multiple_of(me * rows, rows), rows), :]
    total = own.astype(jnp.float32) + pair_buf[chip].astype(jnp.float32)
    for k in range(1, chips):
        ring_copy(k).wait()
        total = total + ring_buf[k].astype(jnp.float32)
    o_ref[...] = total


def scatter_sum(partial):
    groups = lax.axis_size("mlp")
    chips = groups // 2
    rows = partial.shape[0] // groups
    width = partial.shape[1]
    return pl.pallas_call(
        scatter_kernel,
        in_specs=[pl.BlockSpec(memory_space=pltpu.VMEM)],
        out_specs=pl.BlockSpec(memory_space=pltpu.VMEM),
        out_shape=jax.ShapeDtypeStruct((rows, width), jnp.float32),
        scratch_shapes=[
            pltpu.VMEM((chips, rows, width), partial.dtype),
            pltpu.VMEM((chips, rows, width), partial.dtype),
            pltpu.VMEM((chips, rows, width), partial.dtype),
            pltpu.SemaphoreType.DMA((chips,)),
            pltpu.SemaphoreType.DMA((chips,)),
            pltpu.SemaphoreType.DMA((chips,)),
            pltpu.SemaphoreType.DMA((chips,)),
        ],
        compiler_params=pltpu.CompilerParams(
            collective_id=1, has_side_effects=True, vmem_limit_bytes=48 * 1024 * 1024
        ),
    )(partial)


def gather_kernel(x_ref, o_ref, ring_send, ring_recv, pair_send, pair_recv):
    req = lax.axis_index("req")
    me = lax.axis_index("mlp")
    chips = lax.axis_size("mlp") // 2
    chip, core = me // 2, lax.rem(me, 2)
    partner = chip * 2 + 1 - core
    rows = x_ref.shape[0]
    barrier = pltpu.get_barrier_semaphore()
    pl.semaphore_signal(barrier, 1, device_id=(req, partner), device_id_type=pl.DeviceIdType.MESH)
    for k in range(1, chips):
        other = lax.rem(chip + k, chips) * 2 + core
        pl.semaphore_signal(barrier, 1, device_id=(req, other), device_id_type=pl.DeviceIdType.MESH)
    pl.semaphore_wait(barrier, chips)

    def block_rows(block):
        return pl.ds(pl.multiple_of(block * rows, rows), rows)

    def ring_copy(k):
        target = lax.rem(chip + k, chips)
        return pltpu.make_async_remote_copy(
            src_ref=x_ref,
            dst_ref=o_ref.at[block_rows(me)],
            send_sem=ring_send.at[k],
            recv_sem=ring_recv.at[k],
            device_id=(req, target * 2 + core),
            device_id_type=pl.DeviceIdType.MESH,
        )

    def pair_copy(k):
        source = lax.rem(chip + chips - k, chips) * 2 + core
        return pltpu.make_async_remote_copy(
            src_ref=x_ref if k == 0 else o_ref.at[block_rows(source)],
            dst_ref=o_ref.at[block_rows(source)],
            send_sem=pair_send.at[k],
            recv_sem=pair_recv.at[k],
            device_id=(req, partner),
            device_id_type=pl.DeviceIdType.MESH,
        )

    for k in range(1, chips):
        ring_copy(k).start()
    pair_copy(0).start()
    o_ref[block_rows(me), :] = x_ref[...]
    for k in range(1, chips):
        ring_copy(k).wait_recv()
        pair_copy(k).start()
    for k in range(1, chips):
        ring_copy(k).wait_send()
    for k in range(chips):
        pair_copy(k).wait()


def gather_rows(block):
    groups = lax.axis_size("mlp")
    chips = groups // 2
    return pl.pallas_call(
        gather_kernel,
        in_specs=[pl.BlockSpec(memory_space=pltpu.VMEM)],
        out_specs=pl.BlockSpec(memory_space=pltpu.VMEM),
        out_shape=jax.ShapeDtypeStruct((groups * block.shape[0], block.shape[1]), block.dtype),
        scratch_shapes=[
            pltpu.SemaphoreType.DMA((chips,)),
            pltpu.SemaphoreType.DMA((chips,)),
            pltpu.SemaphoreType.DMA((chips,)),
            pltpu.SemaphoreType.DMA((chips,)),
        ],
        compiler_params=pltpu.CompilerParams(
            collective_id=2, has_side_effects=True, vmem_limit_bytes=48 * 1024 * 1024
        ),
    )(block)


def per_device(
    tokens,
    token_owner,
    token_request,
    cache_len,
    cache_k,
    cache_v,
    w_qkv,
    w_out,
    w_fc1,
    w_fc2,
    ln1_gain,
    ln1_bias,
    ln2_gain,
    ln2_bias,
):
    n_req = lax.axis_size("req")
    n_mlp = lax.axis_size("mlp")
    devices = n_req * n_mlp
    owner_index = lax.axis_index("req") * n_mlp + lax.axis_index("mlp")
    tok_dev, width = tokens.shape
    capacity = max(2, 2 * tok_dev // devices)
    slot_count = devices * capacity
    owners_flat = token_owner.reshape(-1)
    my_owners = lax.dynamic_slice_in_dim(owners_flat, owner_index * tok_dev, tok_dev)
    owner_onehot = (my_owners[:, None] == jnp.arange(devices, dtype=jnp.int32)[None, :]).astype(
        jnp.int32
    )
    ranking = jnp.cumsum(owner_onehot, axis=0) - 1
    my_rank = jnp.sum(owner_onehot * ranking, axis=1)
    column = my_owners * capacity + my_rank
    dispatch = (column[:, None] == jnp.arange(slot_count, dtype=jnp.int32)[None, :]).astype(
        jnp.bfloat16
    )
    outgoing = jnp.einsum("tr,td->rd", dispatch, tokens, preferred_element_type=jnp.float32).astype(
        jnp.bfloat16
    )
    arrived = lax.all_to_all(
        outgoing.reshape(devices, capacity, width),
        ("req", "mlp"),
        split_axis=0,
        concat_axis=0,
        tiled=True,
    )
    projections = jnp.dot(
        arrived.reshape(slot_count, width), w_qkv, preferred_element_type=jnp.float32
    ).astype(jnp.bfloat16)
    global_row, slot_request, filled = slot_table(
        owners_flat, token_request, owner_index, devices, tok_dev, capacity
    )
    attended = attend(projections, cache_k, cache_v, cache_len, global_row, slot_request, filled)
    returned = lax.all_to_all(
        attended.reshape(devices, capacity, width),
        ("req", "mlp"),
        split_axis=0,
        concat_axis=0,
        tiled=True,
    )
    attn_rows = jnp.dot(
        dispatch, returned.reshape(slot_count, width), preferred_element_type=jnp.float32
    ).astype(jnp.bfloat16)
    projected_out = jnp.dot(attn_rows, w_out, preferred_element_type=jnp.float32)
    normed = layer_norm(projected_out + tokens.astype(jnp.float32), ln1_gain, ln1_bias).astype(
        jnp.bfloat16
    )
    gathered = gather_rows(normed)
    hidden = jax.nn.gelu(
        jnp.dot(gathered, w_fc1, preferred_element_type=jnp.float32), approximate=False
    ).astype(jnp.bfloat16)
    summed = scatter_sum(
        jnp.dot(hidden, w_fc2, preferred_element_type=jnp.float32).astype(jnp.bfloat16)
    )
    return layer_norm(normed.astype(jnp.float32) + summed, ln2_gain, ln2_bias).astype(jnp.bfloat16)


def solution(mesh):
    placed = (
        P(("req", "mlp"), None),
        P(),
        P(),
        P(("req", "mlp")),
        P(("req", "mlp"), None, None),
        P(("req", "mlp"), None, None),
        P(),
        P(),
        P(None, "mlp"),
        P("mlp", None),
        P(),
        P(),
        P(),
        P(),
    )
    return jax.shard_map(
        per_device, mesh=mesh, in_specs=placed, out_specs=P(("req", "mlp"), None), check_vma=False
    )
```

```python
import jax
import jax.numpy as jnp
from jax import lax
from jax.sharding import PartitionSpec as P
from jax.experimental import pallas as pl
from jax.experimental.pallas import tpu as pltpu

HEADS = 16


epsilon = 1e-05


def layer_norm(values, gain, shift):
    center = values - jnp.mean(values, axis=-1, keepdims=True)
    spread = jnp.mean(center * center, axis=-1, keepdims=True)
    return center * lax.rsqrt(spread + epsilon) * gain + shift


def slot_table(owners_flat, requests_flat, owner_index, devices, tok_dev, capacity):
    owners = owners_flat.reshape(devices, tok_dev)
    requests = requests_flat.reshape(devices, tok_dev)
    mine_mask = (owners == owner_index).astype(jnp.int32)
    ranking = jnp.cumsum(mine_mask, axis=1) - 1
    places = jnp.arange(capacity, dtype=jnp.int32)
    hit_table = mine_mask[:, :, None] * (ranking[:, :, None] == places[None, None, :]).astype(
        jnp.int32
    )
    filled = jnp.sum(hit_table, axis=1)
    positions = jnp.arange(tok_dev, dtype=jnp.int32)
    local_row = jnp.sum(hit_table * positions[None, :, None], axis=1)
    sources = jnp.arange(devices, dtype=jnp.int32)[:, None]
    global_row = jnp.where(filled > 0, sources * tok_dev + local_row, -1).reshape(-1)
    slot_request = jnp.sum(hit_table * requests[:, :, None], axis=1).reshape(-1)
    return (global_row, slot_request, filled.reshape(-1))


def attention_kernel(
    q_ref, kn_ref, vn_ref, k_ref, v_ref, rreq_ref, rrow_ref, rfill_ref, ctag_ref, ntag_ref, nrow_ref, o_ref
):
    head_dim = q_ref.shape[1] // 2
    score_scale = head_dim ** (-0.5)
    q = q_ref[...]
    keys = k_ref[...]
    values = v_ref[...]
    key_new = kn_ref[...]
    value_new = vn_ref[...]
    row_request = rreq_ref[...]
    old_mask = ctag_ref[...] == row_request
    new_mask = (ntag_ref[...] == row_request) & (nrow_ref[...] <= rrow_ref[...])
    lane = lax.broadcasted_iota(jnp.int32, (1, q.shape[1]), 1)
    contract = (((1,), (1,)), ((), ()))
    result = None
    for half in range(2):
        in_head = (lane // head_dim) == half
        q_head = jnp.where(in_head, q, jnp.zeros_like(q))
        old_score = (
            lax.dot_general(q_head, keys, contract, preferred_element_type=jnp.float32) * score_scale
        )
        new_score = (
            lax.dot_general(q_head, key_new, contract, preferred_element_type=jnp.float32)
            * score_scale
        )
        old_exp = jnp.where(old_mask, jnp.exp(old_score), jnp.float32(0.0))
        new_exp = jnp.where(new_mask, jnp.exp(new_score), jnp.float32(0.0))
        total = jnp.sum(old_exp, axis=1, keepdims=True) + jnp.sum(new_exp, axis=1, keepdims=True)
        total = jnp.where(total > 0, total, jnp.float32(1.0))
        inverse = 1.0 / total
        old_weight = (old_exp * inverse).astype(jnp.bfloat16)
        new_weight = (new_exp * inverse).astype(jnp.bfloat16)
        part = jnp.dot(old_weight, values, preferred_element_type=jnp.float32) + jnp.dot(
            new_weight, value_new, preferred_element_type=jnp.float32
        )
        result = part if result is None else jnp.where(in_head, part, result)
    result = jnp.where(rfill_ref[...] > 0, result, jnp.float32(0.0))
    o_ref[...] = result.astype(o_ref.dtype)


def attend(projections, cache_keys, cache_values, lengths, global_row, slot_request, filled):
    slot_count = projections.shape[0]
    width = projections.shape[1] // 3
    requests, context = cache_keys.shape[0], cache_keys.shape[1]
    pair = 128
    pairs = width // pair
    keys = cache_keys.reshape(requests * context, width)
    values = cache_values.reshape(requests * context, width)
    key_owner = jnp.arange(requests * context, dtype=jnp.int32) // context
    key_place = jnp.arange(requests * context, dtype=jnp.int32) % context
    key_limit = jnp.repeat(lengths, context)
    column_tag = jnp.where(key_place < key_limit, key_owner, -1).reshape(1, -1)
    new_tag = jnp.where(filled > 0, slot_request, -1).reshape(1, -1)
    new_row = global_row.reshape(1, -1)
    row_request = slot_request.reshape(-1, 1)
    row_index = global_row.reshape(-1, 1)
    row_filled = filled.reshape(-1, 1)
    keyed = requests * context
    whole = lambda shape: pl.BlockSpec(shape, lambda p: (0, 0))
    return pl.pallas_call(
        attention_kernel,
        grid=(pairs,),
        in_specs=[
            pl.BlockSpec((slot_count, pair), lambda p: (0, p)),
            pl.BlockSpec((slot_count, pair), lambda p: (0, pairs + p)),
            pl.BlockSpec((slot_count, pair), lambda p: (0, 2 * pairs + p)),
            pl.BlockSpec((keyed, pair), lambda p: (0, p)),
            pl.BlockSpec((keyed, pair), lambda p: (0, p)),
            whole((slot_count, 1)),
            whole((slot_count, 1)),
            whole((slot_count, 1)),
            whole((1, keyed)),
            whole((1, slot_count)),
            whole((1, slot_count)),
        ],
        out_specs=pl.BlockSpec((slot_count, pair), lambda p: (0, p)),
        out_shape=jax.ShapeDtypeStruct((slot_count, width), jnp.bfloat16),
        compiler_params=pltpu.CompilerParams(vmem_limit_bytes=48 * 1024 * 1024),
    )(
        projections,
        projections,
        projections,
        keys,
        values,
        row_request,
        row_index,
        row_filled,
        column_tag,
        new_tag,
        new_row,
    )


def scatter_kernel(part_ref, o_ref, pair_buf, send_buf, ring_buf, pair_send, pair_recv, ring_send, ring_recv):
    req = lax.axis_index("req")
    me = lax.axis_index("mlp")
    chips = lax.axis_size("mlp") // 2
    chip, core = me // 2, lax.rem(me, 2)
    partner = chip * 2 + 1 - core
    step = 1 - 2 * core
    ahead = lax.rem(chip + step + chips, chips)
    behind = lax.rem(chip - step + chips, chips)
    across = lax.rem(chip + 2, chips)
    rows = o_ref.shape[0]
    barrier = pltpu.get_barrier_semaphore()
    pl.semaphore_signal(barrier, 1, device_id=(req, partner), device_id_type=pl.DeviceIdType.MESH)
    pl.semaphore_signal(barrier, 1, device_id=(req, ahead * 2 + core), device_id_type=pl.DeviceIdType.MESH)
    pl.semaphore_signal(barrier, 1, device_id=(req, behind * 2 + core), device_id_type=pl.DeviceIdType.MESH)
    pl.semaphore_wait(barrier, 3)

    def pair_copy(z):
        block = z * 2 + 1 - core
        return pltpu.make_async_remote_copy(
            src_ref=part_ref.at[pl.ds(pl.multiple_of(block * rows, rows), rows)],
            dst_ref=pair_buf.at[z],
            send_sem=pair_send.at[z],
            recv_sem=pair_recv.at[z],
            device_id=(req, partner),
            device_id_type=pl.DeviceIdType.MESH,
        )

    for z in range(chips):
        pair_copy(z).start()
    for z in range(chips):
        pair_copy(z).wait()

    def summed(z):
        mine = part_ref[pl.ds(pl.multiple_of((z * 2 + core) * rows, rows), rows), :]
        return mine.astype(jnp.float32) + pair_buf[z].astype(jnp.float32)

    def ring_copy(kind, target):
        return pltpu.make_async_remote_copy(
            src_ref=send_buf.at[kind],
            dst_ref=ring_buf.at[kind],
            send_sem=ring_send.at[kind],
            recv_sem=ring_recv.at[kind],
            device_id=(req, target * 2 + core),
            device_id_type=pl.DeviceIdType.MESH,
        )

    send_buf[1] = summed(across).astype(send_buf.dtype)
    ring_copy(1, ahead).start()
    send_buf[0] = summed(behind).astype(send_buf.dtype)
    ring_copy(0, behind).start()
    ring_copy(1, ahead).wait_recv()
    send_buf[2] = (summed(ahead) + ring_buf[1].astype(jnp.float32)).astype(send_buf.dtype)
    ring_copy(2, ahead).start()
    total = summed(chip)
    ring_copy(0, behind).wait()
    total = total + ring_buf[0].astype(jnp.float32)
    ring_copy(1, ahead).wait_send()
    ring_copy(2, ahead).wait()
    o_ref[...] = total + ring_buf[2].astype(jnp.float32)


def scatter_sum(partial):
    groups = lax.axis_size("mlp")
    chips = groups // 2
    rows = partial.shape[0] // groups
    width = partial.shape[1]
    return pl.pallas_call(
        scatter_kernel,
        in_specs=[pl.BlockSpec(memory_space=pltpu.VMEM)],
        out_specs=pl.BlockSpec(memory_space=pltpu.VMEM),
        out_shape=jax.ShapeDtypeStruct((rows, width), jnp.float32),
        scratch_shapes=[
            pltpu.VMEM((chips, rows, width), partial.dtype),
            pltpu.VMEM((3, rows, width), partial.dtype),
            pltpu.VMEM((3, rows, width), partial.dtype),
            pltpu.SemaphoreType.DMA((chips,)),
            pltpu.SemaphoreType.DMA((chips,)),
            pltpu.SemaphoreType.DMA((3,)),
            pltpu.SemaphoreType.DMA((3,)),
        ],
        compiler_params=pltpu.CompilerParams(
            collective_id=1, has_side_effects=True, vmem_limit_bytes=48 * 1024 * 1024
        ),
    )(partial)


def gather_kernel(x_ref, o_ref, ring_send, ring_recv, pair_send, pair_recv):
    req = lax.axis_index("req")
    me = lax.axis_index("mlp")
    chips = lax.axis_size("mlp") // 2
    chip, core = me // 2, lax.rem(me, 2)
    partner = chip * 2 + 1 - core
    step = 1 - 2 * core
    ahead = lax.rem(chip + step + chips, chips)
    behind = lax.rem(chip - step + chips, chips)
    across = lax.rem(chip + 2, chips)
    rows = x_ref.shape[0]
    barrier = pltpu.get_barrier_semaphore()
    pl.semaphore_signal(barrier, 1, device_id=(req, partner), device_id_type=pl.DeviceIdType.MESH)
    pl.semaphore_signal(barrier, 1, device_id=(req, ahead * 2 + core), device_id_type=pl.DeviceIdType.MESH)
    pl.semaphore_signal(barrier, 1, device_id=(req, behind * 2 + core), device_id_type=pl.DeviceIdType.MESH)
    pl.semaphore_wait(barrier, 3)

    def block_rows(z):
        return pl.ds(pl.multiple_of((z * 2 + core) * rows, rows), rows)

    origins = (me // 2, behind, ahead, across)

    def ring_copy(kind):
        source = x_ref if kind < 2 else o_ref.at[block_rows(behind)]
        origin = chip if kind < 2 else behind
        target = ahead if kind != 1 else behind
        return pltpu.make_async_remote_copy(
            src_ref=source,
            dst_ref=o_ref.at[block_rows(origin)],
            send_sem=ring_send.at[kind],
            recv_sem=ring_recv.at[kind],
            device_id=(req, target * 2 + core),
            device_id_type=pl.DeviceIdType.MESH,
        )

    def pair_copy(kind):
        source = x_ref if kind == 0 else o_ref.at[block_rows(origins[kind])]
        return pltpu.make_async_remote_copy(
            src_ref=source,
            dst_ref=o_ref.at[block_rows(origins[kind])],
            send_sem=pair_send.at[kind],
            recv_sem=pair_recv.at[kind],
            device_id=(req, partner),
            device_id_type=pl.DeviceIdType.MESH,
        )

    ring_copy(0).start()
    ring_copy(1).start()
    pair_copy(0).start()
    o_ref[block_rows(chip), :] = x_ref[...]
    ring_copy(0).wait_recv()
    ring_copy(2).start()
    pair_copy(1).start()
    ring_copy(1).wait_recv()
    pair_copy(2).start()
    ring_copy(2).wait_recv()
    pair_copy(3).start()
    for kind in range(3):
        ring_copy(kind).wait_send()
    for kind in range(4):
        pair_copy(kind).wait()


def gather_rows(block):
    groups = lax.axis_size("mlp")
    chips = groups // 2
    return pl.pallas_call(
        gather_kernel,
        in_specs=[pl.BlockSpec(memory_space=pltpu.VMEM)],
        out_specs=pl.BlockSpec(memory_space=pltpu.VMEM),
        out_shape=jax.ShapeDtypeStruct((groups * block.shape[0], block.shape[1]), block.dtype),
        scratch_shapes=[
            pltpu.SemaphoreType.DMA((chips,)),
            pltpu.SemaphoreType.DMA((chips,)),
            pltpu.SemaphoreType.DMA((chips,)),
            pltpu.SemaphoreType.DMA((chips,)),
        ],
        compiler_params=pltpu.CompilerParams(
            collective_id=2, has_side_effects=True, vmem_limit_bytes=48 * 1024 * 1024
        ),
    )(block)


def per_device(
    tokens,
    token_owner,
    token_request,
    cache_len,
    cache_k,
    cache_v,
    w_qkv,
    w_out,
    w_fc1,
    w_fc2,
    ln1_gain,
    ln1_bias,
    ln2_gain,
    ln2_bias,
):
    n_req = lax.axis_size("req")
    n_mlp = lax.axis_size("mlp")
    devices = n_req * n_mlp
    owner_index = lax.axis_index("req") * n_mlp + lax.axis_index("mlp")
    tok_dev, width = tokens.shape
    capacity = max(2, 2 * tok_dev // devices)
    slot_count = devices * capacity
    owners_flat = token_owner.reshape(-1)
    my_owners = lax.dynamic_slice_in_dim(owners_flat, owner_index * tok_dev, tok_dev)
    owner_onehot = (my_owners[:, None] == jnp.arange(devices, dtype=jnp.int32)[None, :]).astype(
        jnp.int32
    )
    ranking = jnp.cumsum(owner_onehot, axis=0) - 1
    my_rank = jnp.sum(owner_onehot * ranking, axis=1)
    column = my_owners * capacity + my_rank
    dispatch = (column[:, None] == jnp.arange(slot_count, dtype=jnp.int32)[None, :]).astype(
        jnp.bfloat16
    )
    outgoing = jnp.einsum("tr,td->rd", dispatch, tokens, preferred_element_type=jnp.float32).astype(
        jnp.bfloat16
    )
    arrived = lax.all_to_all(
        outgoing.reshape(devices, capacity, width),
        ("req", "mlp"),
        split_axis=0,
        concat_axis=0,
        tiled=True,
    )
    projections = jnp.dot(
        arrived.reshape(slot_count, width), w_qkv, preferred_element_type=jnp.float32
    ).astype(jnp.bfloat16)
    global_row, slot_request, filled = slot_table(
        owners_flat, token_request, owner_index, devices, tok_dev, capacity
    )
    attended = attend(projections, cache_k, cache_v, cache_len, global_row, slot_request, filled)
    returned = lax.all_to_all(
        attended.reshape(devices, capacity, width),
        ("req", "mlp"),
        split_axis=0,
        concat_axis=0,
        tiled=True,
    )
    attn_rows = jnp.dot(
        dispatch, returned.reshape(slot_count, width), preferred_element_type=jnp.float32
    ).astype(jnp.bfloat16)
    projected_out = jnp.dot(attn_rows, w_out, preferred_element_type=jnp.float32)
    normed = layer_norm(projected_out + tokens.astype(jnp.float32), ln1_gain, ln1_bias).astype(
        jnp.bfloat16
    )
    gathered = gather_rows(normed)
    hidden = jax.nn.gelu(
        jnp.dot(gathered, w_fc1, preferred_element_type=jnp.float32), approximate=False
    ).astype(jnp.bfloat16)
    summed = scatter_sum(
        jnp.dot(hidden, w_fc2, preferred_element_type=jnp.float32).astype(jnp.bfloat16)
    )
    return layer_norm(normed.astype(jnp.float32) + summed, ln2_gain, ln2_bias).astype(jnp.bfloat16)


def solution(mesh):
    placed = (
        P(("req", "mlp"), None),
        P(),
        P(),
        P(("req", "mlp")),
        P(("req", "mlp"), None, None),
        P(("req", "mlp"), None, None),
        P(),
        P(),
        P(None, "mlp"),
        P("mlp", None),
        P(),
        P(),
        P(),
        P(),
    )
    return jax.shard_map(
        per_device, mesh=mesh, in_specs=placed, out_specs=P(("req", "mlp"), None), check_vma=False
    )
```

```python
import jax
import jax.numpy as jnp
from jax import lax
from jax.sharding import PartitionSpec as P
from jax.experimental import pallas as pl
from jax.experimental.pallas import tpu as pltpu

HEADS = 16


epsilon = 1e-05


def layer_norm(values, gain, shift):
    center = values - jnp.mean(values, axis=-1, keepdims=True)
    spread = jnp.mean(center * center, axis=-1, keepdims=True)
    return center * lax.rsqrt(spread + epsilon) * gain + shift


def slot_table(owners_flat, requests_flat, owner_index, devices, tok_dev, capacity):
    owners = owners_flat.reshape(devices, tok_dev)
    requests = requests_flat.reshape(devices, tok_dev)
    mine_mask = (owners == owner_index).astype(jnp.int32)
    ranking = jnp.cumsum(mine_mask, axis=1) - 1
    places = jnp.arange(capacity, dtype=jnp.int32)
    hit_table = mine_mask[:, :, None] * (ranking[:, :, None] == places[None, None, :]).astype(
        jnp.int32
    )
    filled = jnp.sum(hit_table, axis=1)
    positions = jnp.arange(tok_dev, dtype=jnp.int32)
    local_row = jnp.sum(hit_table * positions[None, :, None], axis=1)
    sources = jnp.arange(devices, dtype=jnp.int32)[:, None]
    global_row = jnp.where(filled > 0, sources * tok_dev + local_row, -1).reshape(-1)
    slot_request = jnp.sum(hit_table * requests[:, :, None], axis=1).reshape(-1)
    return (global_row, slot_request, filled.reshape(-1))


def attention_kernel(
    q_ref, kn_ref, vn_ref, k_ref, v_ref, rreq_ref, rrow_ref, rfill_ref, ctag_ref, ntag_ref, nrow_ref, o_ref
):
    head_dim = q_ref.shape[1] // 2
    score_scale = head_dim ** (-0.5)
    q = q_ref[...]
    keys = k_ref[...]
    values = v_ref[...]
    key_new = kn_ref[...]
    value_new = vn_ref[...]
    row_request = rreq_ref[...]
    old_mask = ctag_ref[...] == row_request
    new_mask = (ntag_ref[...] == row_request) & (nrow_ref[...] <= rrow_ref[...])
    lane = lax.broadcasted_iota(jnp.int32, (1, q.shape[1]), 1)
    contract = (((1,), (1,)), ((), ()))
    result = None
    for half in range(2):
        in_head = (lane // head_dim) == half
        q_head = jnp.where(in_head, q, jnp.zeros_like(q))
        old_score = (
            lax.dot_general(q_head, keys, contract, preferred_element_type=jnp.float32) * score_scale
        )
        new_score = (
            lax.dot_general(q_head, key_new, contract, preferred_element_type=jnp.float32)
            * score_scale
        )
        old_exp = jnp.where(old_mask, jnp.exp(old_score), jnp.float32(0.0))
        new_exp = jnp.where(new_mask, jnp.exp(new_score), jnp.float32(0.0))
        total = jnp.sum(old_exp, axis=1, keepdims=True) + jnp.sum(new_exp, axis=1, keepdims=True)
        total = jnp.where(total > 0, total, jnp.float32(1.0))
        inverse = 1.0 / total
        old_weight = (old_exp * inverse).astype(jnp.bfloat16)
        new_weight = (new_exp * inverse).astype(jnp.bfloat16)
        part = jnp.dot(old_weight, values, preferred_element_type=jnp.float32) + jnp.dot(
            new_weight, value_new, preferred_element_type=jnp.float32
        )
        result = part if result is None else jnp.where(in_head, part, result)
    result = jnp.where(rfill_ref[...] > 0, result, jnp.float32(0.0))
    o_ref[...] = result.astype(o_ref.dtype)


def attend(projections, cache_keys, cache_values, lengths, global_row, slot_request, filled, first, count):
    slot_count = projections.shape[0]
    width = projections.shape[1] // 3
    requests, context = cache_keys.shape[0], cache_keys.shape[1]
    pair = 128
    pairs = width // pair
    keys = cache_keys.reshape(requests * context, width)
    values = cache_values.reshape(requests * context, width)
    key_owner = jnp.arange(requests * context, dtype=jnp.int32) // context
    key_place = jnp.arange(requests * context, dtype=jnp.int32) % context
    key_limit = jnp.repeat(lengths, context)
    column_tag = jnp.where(key_place < key_limit, key_owner, -1).reshape(1, -1)
    new_tag = jnp.where(filled > 0, slot_request, -1).reshape(1, -1)
    new_row = global_row.reshape(1, -1)
    row_request = slot_request.reshape(-1, 1)
    row_index = global_row.reshape(-1, 1)
    row_filled = filled.reshape(-1, 1)
    keyed = requests * context
    whole = lambda shape: pl.BlockSpec(shape, lambda p: (0, 0))
    return pl.pallas_call(
        attention_kernel,
        grid=(count,),
        in_specs=[
            pl.BlockSpec((slot_count, pair), lambda p: (0, first + p)),
            pl.BlockSpec((slot_count, pair), lambda p: (0, pairs + first + p)),
            pl.BlockSpec((slot_count, pair), lambda p: (0, 2 * pairs + first + p)),
            pl.BlockSpec((keyed, pair), lambda p: (0, first + p)),
            pl.BlockSpec((keyed, pair), lambda p: (0, first + p)),
            whole((slot_count, 1)),
            whole((slot_count, 1)),
            whole((slot_count, 1)),
            whole((1, keyed)),
            whole((1, slot_count)),
            whole((1, slot_count)),
        ],
        out_specs=pl.BlockSpec((slot_count, pair), lambda p: (0, p)),
        out_shape=jax.ShapeDtypeStruct((slot_count, count * pair), jnp.bfloat16),
        compiler_params=pltpu.CompilerParams(vmem_limit_bytes=48 * 1024 * 1024),
    )(
        projections,
        projections,
        projections,
        keys,
        values,
        row_request,
        row_index,
        row_filled,
        column_tag,
        new_tag,
        new_row,
    )


def scatter_kernel(part_ref, o_ref, pair_buf, send_buf, ring_buf, pair_send, pair_recv, ring_send, ring_recv):
    req = lax.axis_index("req")
    me = lax.axis_index("mlp")
    chips = lax.axis_size("mlp") // 2
    chip, core = me // 2, lax.rem(me, 2)
    partner = chip * 2 + 1 - core
    step = 1 - 2 * core
    ahead = lax.rem(chip + step + chips, chips)
    behind = lax.rem(chip - step + chips, chips)
    across = lax.rem(chip + 2, chips)
    rows = o_ref.shape[0]
    barrier = pltpu.get_barrier_semaphore()
    pl.semaphore_signal(barrier, 1, device_id=(req, partner), device_id_type=pl.DeviceIdType.MESH)
    pl.semaphore_signal(barrier, 1, device_id=(req, ahead * 2 + core), device_id_type=pl.DeviceIdType.MESH)
    pl.semaphore_signal(barrier, 1, device_id=(req, behind * 2 + core), device_id_type=pl.DeviceIdType.MESH)
    pl.semaphore_wait(barrier, 3)

    def pair_copy(z):
        block = z * 2 + 1 - core
        return pltpu.make_async_remote_copy(
            src_ref=part_ref.at[pl.ds(pl.multiple_of(block * rows, rows), rows)],
            dst_ref=pair_buf.at[z],
            send_sem=pair_send.at[z],
            recv_sem=pair_recv.at[z],
            device_id=(req, partner),
            device_id_type=pl.DeviceIdType.MESH,
        )

    for z in range(chips):
        pair_copy(z).start()
    for z in range(chips):
        pair_copy(z).wait()

    def summed(z):
        mine = part_ref[pl.ds(pl.multiple_of((z * 2 + core) * rows, rows), rows), :]
        return mine.astype(jnp.float32) + pair_buf[z].astype(jnp.float32)

    def ring_copy(kind, target):
        return pltpu.make_async_remote_copy(
            src_ref=send_buf.at[kind],
            dst_ref=ring_buf.at[kind],
            send_sem=ring_send.at[kind],
            recv_sem=ring_recv.at[kind],
            device_id=(req, target * 2 + core),
            device_id_type=pl.DeviceIdType.MESH,
        )

    send_buf[1] = summed(across).astype(send_buf.dtype)
    ring_copy(1, ahead).start()
    send_buf[0] = summed(behind).astype(send_buf.dtype)
    ring_copy(0, behind).start()
    ring_copy(1, ahead).wait_recv()
    send_buf[2] = (summed(ahead) + ring_buf[1].astype(jnp.float32)).astype(send_buf.dtype)
    ring_copy(2, ahead).start()
    total = summed(chip)
    ring_copy(0, behind).wait()
    total = total + ring_buf[0].astype(jnp.float32)
    ring_copy(1, ahead).wait_send()
    ring_copy(2, ahead).wait()
    o_ref[...] = total + ring_buf[2].astype(jnp.float32)


def scatter_sum(partial):
    groups = lax.axis_size("mlp")
    chips = groups // 2
    rows = partial.shape[0] // groups
    width = partial.shape[1]
    return pl.pallas_call(
        scatter_kernel,
        in_specs=[pl.BlockSpec(memory_space=pltpu.VMEM)],
        out_specs=pl.BlockSpec(memory_space=pltpu.VMEM),
        out_shape=jax.ShapeDtypeStruct((rows, width), jnp.float32),
        scratch_shapes=[
            pltpu.VMEM((chips, rows, width), partial.dtype),
            pltpu.VMEM((3, rows, width), partial.dtype),
            pltpu.VMEM((3, rows, width), partial.dtype),
            pltpu.SemaphoreType.DMA((chips,)),
            pltpu.SemaphoreType.DMA((chips,)),
            pltpu.SemaphoreType.DMA((3,)),
            pltpu.SemaphoreType.DMA((3,)),
        ],
        compiler_params=pltpu.CompilerParams(
            collective_id=1, has_side_effects=True, vmem_limit_bytes=48 * 1024 * 1024
        ),
    )(partial)


def gather_kernel(x_ref, o_ref, ring_send, ring_recv, pair_send, pair_recv):
    req = lax.axis_index("req")
    me = lax.axis_index("mlp")
    chips = lax.axis_size("mlp") // 2
    chip, core = me // 2, lax.rem(me, 2)
    partner = chip * 2 + 1 - core
    step = 1 - 2 * core
    ahead = lax.rem(chip + step + chips, chips)
    behind = lax.rem(chip - step + chips, chips)
    across = lax.rem(chip + 2, chips)
    rows = x_ref.shape[0]
    barrier = pltpu.get_barrier_semaphore()
    pl.semaphore_signal(barrier, 1, device_id=(req, partner), device_id_type=pl.DeviceIdType.MESH)
    pl.semaphore_signal(barrier, 1, device_id=(req, ahead * 2 + core), device_id_type=pl.DeviceIdType.MESH)
    pl.semaphore_signal(barrier, 1, device_id=(req, behind * 2 + core), device_id_type=pl.DeviceIdType.MESH)
    pl.semaphore_wait(barrier, 3)

    def block_rows(z):
        return pl.ds(pl.multiple_of((z * 2 + core) * rows, rows), rows)

    origins = (me // 2, behind, ahead, across)

    def ring_copy(kind):
        source = x_ref if kind < 2 else o_ref.at[block_rows(behind)]
        origin = chip if kind < 2 else behind
        target = ahead if kind != 1 else behind
        return pltpu.make_async_remote_copy(
            src_ref=source,
            dst_ref=o_ref.at[block_rows(origin)],
            send_sem=ring_send.at[kind],
            recv_sem=ring_recv.at[kind],
            device_id=(req, target * 2 + core),
            device_id_type=pl.DeviceIdType.MESH,
        )

    def pair_copy(kind):
        source = x_ref if kind == 0 else o_ref.at[block_rows(origins[kind])]
        return pltpu.make_async_remote_copy(
            src_ref=source,
            dst_ref=o_ref.at[block_rows(origins[kind])],
            send_sem=pair_send.at[kind],
            recv_sem=pair_recv.at[kind],
            device_id=(req, partner),
            device_id_type=pl.DeviceIdType.MESH,
        )

    ring_copy(0).start()
    ring_copy(1).start()
    pair_copy(0).start()
    o_ref[block_rows(chip), :] = x_ref[...]
    ring_copy(0).wait_recv()
    ring_copy(2).start()
    pair_copy(1).start()
    ring_copy(1).wait_recv()
    pair_copy(2).start()
    ring_copy(2).wait_recv()
    pair_copy(3).start()
    for kind in range(3):
        ring_copy(kind).wait_send()
    for kind in range(4):
        pair_copy(kind).wait()


def gather_rows(block):
    groups = lax.axis_size("mlp")
    chips = groups // 2
    return pl.pallas_call(
        gather_kernel,
        in_specs=[pl.BlockSpec(memory_space=pltpu.VMEM)],
        out_specs=pl.BlockSpec(memory_space=pltpu.VMEM),
        out_shape=jax.ShapeDtypeStruct((groups * block.shape[0], block.shape[1]), block.dtype),
        scratch_shapes=[
            pltpu.SemaphoreType.DMA((chips,)),
            pltpu.SemaphoreType.DMA((chips,)),
            pltpu.SemaphoreType.DMA((chips,)),
            pltpu.SemaphoreType.DMA((chips,)),
        ],
        compiler_params=pltpu.CompilerParams(
            collective_id=2, has_side_effects=True, vmem_limit_bytes=48 * 1024 * 1024
        ),
    )(block)


def per_device(
    tokens,
    token_owner,
    token_request,
    cache_len,
    cache_k,
    cache_v,
    w_qkv,
    w_out,
    w_fc1,
    w_fc2,
    ln1_gain,
    ln1_bias,
    ln2_gain,
    ln2_bias,
):
    n_req = lax.axis_size("req")
    n_mlp = lax.axis_size("mlp")
    devices = n_req * n_mlp
    owner_index = lax.axis_index("req") * n_mlp + lax.axis_index("mlp")
    tok_dev, width = tokens.shape
    capacity = max(2, 2 * tok_dev // devices)
    slot_count = devices * capacity
    owners_flat = token_owner.reshape(-1)
    my_owners = lax.dynamic_slice_in_dim(owners_flat, owner_index * tok_dev, tok_dev)
    owner_onehot = (my_owners[:, None] == jnp.arange(devices, dtype=jnp.int32)[None, :]).astype(
        jnp.int32
    )
    ranking = jnp.cumsum(owner_onehot, axis=0) - 1
    my_rank = jnp.sum(owner_onehot * ranking, axis=1)
    column = my_owners * capacity + my_rank
    dispatch = (column[:, None] == jnp.arange(slot_count, dtype=jnp.int32)[None, :]).astype(
        jnp.bfloat16
    )
    outgoing = jnp.einsum("tr,td->rd", dispatch, tokens, preferred_element_type=jnp.float32).astype(
        jnp.bfloat16
    )
    arrived = lax.all_to_all(
        outgoing.reshape(devices, capacity, width),
        ("req", "mlp"),
        split_axis=0,
        concat_axis=0,
        tiled=True,
    )
    projections = jnp.dot(
        arrived.reshape(slot_count, width), w_qkv, preferred_element_type=jnp.float32
    ).astype(jnp.bfloat16)
    global_row, slot_request, filled = slot_table(
        owners_flat, token_request, owner_index, devices, tok_dev, capacity
    )
    halves = 2
    per_half = width // 128 // halves
    projected_out = None
    for half in range(halves):
        attended = attend(
            projections, cache_k, cache_v, cache_len, global_row, slot_request, filled,
            half * per_half, per_half,
        )
        returned = lax.all_to_all(
            attended.reshape(devices, capacity, per_half * 128),
            ("req", "mlp"),
            split_axis=0,
            concat_axis=0,
            tiled=True,
        )
        attn_rows = jnp.dot(
            dispatch, returned.reshape(slot_count, per_half * 128), preferred_element_type=jnp.float32
        ).astype(jnp.bfloat16)
        columns = slice(half * per_half * 128, (half + 1) * per_half * 128)
        product = jnp.dot(attn_rows, w_out[columns, :], preferred_element_type=jnp.float32)
        projected_out = product if projected_out is None else projected_out + product
    normed = layer_norm(projected_out + tokens.astype(jnp.float32), ln1_gain, ln1_bias).astype(
        jnp.bfloat16
    )
    gathered = gather_rows(normed)
    hidden = jax.nn.gelu(
        jnp.dot(gathered, w_fc1, preferred_element_type=jnp.float32), approximate=False
    ).astype(jnp.bfloat16)
    summed = scatter_sum(
        jnp.dot(hidden, w_fc2, preferred_element_type=jnp.float32).astype(jnp.bfloat16)
    )
    return layer_norm(normed.astype(jnp.float32) + summed, ln2_gain, ln2_bias).astype(jnp.bfloat16)


def solution(mesh):
    placed = (
        P(("req", "mlp"), None),
        P(),
        P(),
        P(("req", "mlp")),
        P(("req", "mlp"), None, None),
        P(("req", "mlp"), None, None),
        P(),
        P(),
        P(None, "mlp"),
        P("mlp", None),
        P(),
        P(),
        P(),
        P(),
    )
    return jax.shard_map(
        per_device, mesh=mesh, in_specs=placed, out_specs=P(("req", "mlp"), None), check_vma=False
    )
```

```python
import jax
import jax.numpy as jnp
from jax import lax
from jax.sharding import PartitionSpec as P
from jax.experimental import pallas as pl
from jax.experimental.pallas import tpu as pltpu

HEADS = 16


epsilon = 1e-05


def layer_norm(values, gain, shift):
    center = values - jnp.mean(values, axis=-1, keepdims=True)
    spread = jnp.mean(center * center, axis=-1, keepdims=True)
    return center * lax.rsqrt(spread + epsilon) * gain + shift


def slot_table(owners_flat, requests_flat, owner_index, devices, tok_dev, capacity):
    owners = owners_flat.reshape(devices, tok_dev)
    requests = requests_flat.reshape(devices, tok_dev)
    mine_mask = (owners == owner_index).astype(jnp.int32)
    ranking = jnp.cumsum(mine_mask, axis=1) - 1
    places = jnp.arange(capacity, dtype=jnp.int32)
    hit_table = mine_mask[:, :, None] * (ranking[:, :, None] == places[None, None, :]).astype(
        jnp.int32
    )
    filled = jnp.sum(hit_table, axis=1)
    positions = jnp.arange(tok_dev, dtype=jnp.int32)
    local_row = jnp.sum(hit_table * positions[None, :, None], axis=1)
    sources = jnp.arange(devices, dtype=jnp.int32)[:, None]
    global_row = jnp.where(filled > 0, sources * tok_dev + local_row, -1).reshape(-1)
    slot_request = jnp.sum(hit_table * requests[:, :, None], axis=1).reshape(-1)
    return (global_row, slot_request, filled.reshape(-1))


def attention_kernel(
    q_ref, kn_ref, vn_ref, k_ref, v_ref, rreq_ref, rrow_ref, rfill_ref, ctag_ref, ntag_ref, nrow_ref, o_ref
):
    head_dim = q_ref.shape[1] // 2
    score_scale = head_dim ** (-0.5)
    q = q_ref[...]
    keys = k_ref[...]
    values = v_ref[...]
    key_new = kn_ref[...]
    value_new = vn_ref[...]
    row_request = rreq_ref[...]
    old_mask = ctag_ref[...] == row_request
    new_mask = (ntag_ref[...] == row_request) & (nrow_ref[...] <= rrow_ref[...])
    lane = lax.broadcasted_iota(jnp.int32, (1, q.shape[1]), 1)
    contract = (((1,), (1,)), ((), ()))
    result = None
    for half in range(2):
        in_head = (lane // head_dim) == half
        q_head = jnp.where(in_head, q, jnp.zeros_like(q))
        old_score = (
            lax.dot_general(q_head, keys, contract, preferred_element_type=jnp.float32) * score_scale
        )
        new_score = (
            lax.dot_general(q_head, key_new, contract, preferred_element_type=jnp.float32)
            * score_scale
        )
        old_exp = jnp.where(old_mask, jnp.exp(old_score), jnp.float32(0.0))
        new_exp = jnp.where(new_mask, jnp.exp(new_score), jnp.float32(0.0))
        total = jnp.sum(old_exp, axis=1, keepdims=True) + jnp.sum(new_exp, axis=1, keepdims=True)
        total = jnp.where(total > 0, total, jnp.float32(1.0))
        inverse = 1.0 / total
        old_weight = (old_exp * inverse).astype(jnp.bfloat16)
        new_weight = (new_exp * inverse).astype(jnp.bfloat16)
        part = jnp.dot(old_weight, values, preferred_element_type=jnp.float32) + jnp.dot(
            new_weight, value_new, preferred_element_type=jnp.float32
        )
        result = part if result is None else jnp.where(in_head, part, result)
    result = jnp.where(rfill_ref[...] > 0, result, jnp.float32(0.0))
    o_ref[...] = result.astype(o_ref.dtype)


def attend(projections, cache_keys, cache_values, lengths, global_row, slot_request, filled):
    slot_count = projections.shape[0]
    width = projections.shape[1] // 3
    requests, context = cache_keys.shape[0], cache_keys.shape[1]
    pair = 128
    pairs = width // pair
    keys = cache_keys.reshape(requests * context, width)
    values = cache_values.reshape(requests * context, width)
    key_owner = jnp.arange(requests * context, dtype=jnp.int32) // context
    key_place = jnp.arange(requests * context, dtype=jnp.int32) % context
    key_limit = jnp.repeat(lengths, context)
    column_tag = jnp.where(key_place < key_limit, key_owner, -1).reshape(1, -1)
    new_tag = jnp.where(filled > 0, slot_request, -1).reshape(1, -1)
    new_row = global_row.reshape(1, -1)
    row_request = slot_request.reshape(-1, 1)
    row_index = global_row.reshape(-1, 1)
    row_filled = filled.reshape(-1, 1)
    keyed = requests * context
    whole = lambda shape: pl.BlockSpec(shape, lambda p: (0, 0))
    return pl.pallas_call(
        attention_kernel,
        grid=(pairs,),
        in_specs=[
            pl.BlockSpec((slot_count, pair), lambda p: (0, p)),
            pl.BlockSpec((slot_count, pair), lambda p: (0, pairs + p)),
            pl.BlockSpec((slot_count, pair), lambda p: (0, 2 * pairs + p)),
            pl.BlockSpec((keyed, pair), lambda p: (0, p)),
            pl.BlockSpec((keyed, pair), lambda p: (0, p)),
            whole((slot_count, 1)),
            whole((slot_count, 1)),
            whole((slot_count, 1)),
            whole((1, keyed)),
            whole((1, slot_count)),
            whole((1, slot_count)),
        ],
        out_specs=pl.BlockSpec((slot_count, pair), lambda p: (0, p)),
        out_shape=jax.ShapeDtypeStruct((slot_count, width), jnp.bfloat16),
        compiler_params=pltpu.CompilerParams(vmem_limit_bytes=48 * 1024 * 1024),
    )(
        projections,
        projections,
        projections,
        keys,
        values,
        row_request,
        row_index,
        row_filled,
        column_tag,
        new_tag,
        new_row,
    )


def scatter_kernel(part_ref, o_ref, pair_buf, send_buf, ring_buf, pair_send, pair_recv, ring_send, ring_recv):
    req = lax.axis_index("req")
    me = lax.axis_index("mlp")
    chips = lax.axis_size("mlp") // 2
    chip, core = me // 2, lax.rem(me, 2)
    partner = chip * 2 + 1 - core
    step = 1 - 2 * core
    ahead = lax.rem(chip + step + chips, chips)
    behind = lax.rem(chip - step + chips, chips)
    across = lax.rem(chip + 2, chips)
    rows = o_ref.shape[0]
    barrier = pltpu.get_barrier_semaphore()
    pl.semaphore_signal(barrier, 1, device_id=(req, partner), device_id_type=pl.DeviceIdType.MESH)
    pl.semaphore_signal(barrier, 1, device_id=(req, ahead * 2 + core), device_id_type=pl.DeviceIdType.MESH)
    pl.semaphore_signal(barrier, 1, device_id=(req, behind * 2 + core), device_id_type=pl.DeviceIdType.MESH)
    pl.semaphore_wait(barrier, 3)

    def pair_copy(z):
        block = z * 2 + 1 - core
        return pltpu.make_async_remote_copy(
            src_ref=part_ref.at[pl.ds(pl.multiple_of(block * rows, rows), rows)],
            dst_ref=pair_buf.at[z],
            send_sem=pair_send.at[z],
            recv_sem=pair_recv.at[z],
            device_id=(req, partner),
            device_id_type=pl.DeviceIdType.MESH,
        )

    for z in range(chips):
        pair_copy(z).start()
    for z in range(chips):
        pair_copy(z).wait()

    def summed(z):
        mine = part_ref[pl.ds(pl.multiple_of((z * 2 + core) * rows, rows), rows), :]
        return mine.astype(jnp.float32) + pair_buf[z].astype(jnp.float32)

    def ring_copy(kind, target):
        return pltpu.make_async_remote_copy(
            src_ref=send_buf.at[kind],
            dst_ref=ring_buf.at[kind],
            send_sem=ring_send.at[kind],
            recv_sem=ring_recv.at[kind],
            device_id=(req, target * 2 + core),
            device_id_type=pl.DeviceIdType.MESH,
        )

    send_buf[1] = summed(across).astype(send_buf.dtype)
    ring_copy(1, ahead).start()
    send_buf[0] = summed(behind).astype(send_buf.dtype)
    ring_copy(0, behind).start()
    ring_copy(1, ahead).wait_recv()
    send_buf[2] = (summed(ahead) + ring_buf[1].astype(jnp.float32)).astype(send_buf.dtype)
    ring_copy(2, ahead).start()
    total = summed(chip)
    ring_copy(0, behind).wait()
    total = total + ring_buf[0].astype(jnp.float32)
    ring_copy(1, ahead).wait_send()
    ring_copy(2, ahead).wait()
    o_ref[...] = total + ring_buf[2].astype(jnp.float32)


def scatter_sum(partial):
    groups = lax.axis_size("mlp")
    chips = groups // 2
    rows = partial.shape[0] // groups
    width = partial.shape[1]
    return pl.pallas_call(
        scatter_kernel,
        in_specs=[pl.BlockSpec(memory_space=pltpu.VMEM)],
        out_specs=pl.BlockSpec(memory_space=pltpu.VMEM),
        out_shape=jax.ShapeDtypeStruct((rows, width), jnp.float32),
        scratch_shapes=[
            pltpu.VMEM((chips, rows, width), partial.dtype),
            pltpu.VMEM((3, rows, width), partial.dtype),
            pltpu.VMEM((3, rows, width), partial.dtype),
            pltpu.SemaphoreType.DMA((chips,)),
            pltpu.SemaphoreType.DMA((chips,)),
            pltpu.SemaphoreType.DMA((3,)),
            pltpu.SemaphoreType.DMA((3,)),
        ],
        compiler_params=pltpu.CompilerParams(
            collective_id=1, has_side_effects=True, vmem_limit_bytes=48 * 1024 * 1024
        ),
    )(partial)


def gather_kernel(
    x_ref, w1_ref, w2_ref, o_ref, held, ring_send, ring_recv, pair_send, pair_recv
):
    req = lax.axis_index("req")
    me = lax.axis_index("mlp")
    chips = lax.axis_size("mlp") // 2
    chip, core = me // 2, lax.rem(me, 2)
    partner = chip * 2 + 1 - core
    step = 1 - 2 * core
    ahead = lax.rem(chip + step + chips, chips)
    behind = lax.rem(chip - step + chips, chips)
    across = lax.rem(chip + 2, chips)
    rows = x_ref.shape[0]
    barrier = pltpu.get_barrier_semaphore()
    pl.semaphore_signal(barrier, 1, device_id=(req, partner), device_id_type=pl.DeviceIdType.MESH)
    pl.semaphore_signal(barrier, 1, device_id=(req, ahead * 2 + core), device_id_type=pl.DeviceIdType.MESH)
    pl.semaphore_signal(barrier, 1, device_id=(req, behind * 2 + core), device_id_type=pl.DeviceIdType.MESH)
    pl.semaphore_wait(barrier, 3)

    def block_rows(z, which):
        return pl.ds(pl.multiple_of((z * 2 + which) * rows, rows), rows)

    origins = (chip, behind, ahead, across)

    def ring_copy(kind):
        source = x_ref if kind < 2 else held.at[block_rows(behind, core)]
        origin = chip if kind < 2 else behind
        target = ahead if kind != 1 else behind
        return pltpu.make_async_remote_copy(
            src_ref=source,
            dst_ref=held.at[block_rows(origin, core)],
            send_sem=ring_send.at[kind],
            recv_sem=ring_recv.at[kind],
            device_id=(req, target * 2 + core),
            device_id_type=pl.DeviceIdType.MESH,
        )

    def pair_copy(kind):
        source = x_ref if kind == 0 else held.at[block_rows(origins[kind], core)]
        return pltpu.make_async_remote_copy(
            src_ref=source,
            dst_ref=held.at[block_rows(origins[kind], core)],
            send_sem=pair_send.at[kind],
            recv_sem=pair_recv.at[kind],
            device_id=(req, partner),
            device_id_type=pl.DeviceIdType.MESH,
        )

    def feed_forward(block, place):
        hidden = jnp.dot(block, w1_ref[...], preferred_element_type=jnp.float32)
        hidden = (hidden * 0.5 * (1.0 + lax.erf(hidden * (2.0 ** -0.5)))).astype(jnp.bfloat16)
        o_ref[place, :] = jnp.dot(hidden, w2_ref[...], preferred_element_type=jnp.float32).astype(
            o_ref.dtype
        )

    ring_copy(0).start()
    ring_copy(1).start()
    pair_copy(0).start()
    feed_forward(x_ref[...], block_rows(chip, core))
    ring_copy(0).wait_recv()
    ring_copy(2).start()
    pair_copy(1).start()
    feed_forward(held[block_rows(behind, core), :], block_rows(behind, core))
    ring_copy(1).wait_recv()
    pair_copy(2).start()
    feed_forward(held[block_rows(ahead, core), :], block_rows(ahead, core))
    ring_copy(2).wait_recv()
    pair_copy(3).start()
    feed_forward(held[block_rows(across, core), :], block_rows(across, core))
    partner_origins = (chip, ahead, behind, across)
    for kind in range(4):
        copy = pair_copy(kind)
        copy.wait_recv()
        place = block_rows(partner_origins[kind], 1 - core)
        feed_forward(held[place, :], place)
    for kind in range(3):
        ring_copy(kind).wait_send()
    for kind in range(4):
        pair_copy(kind).wait_send()


def gather_rows(block, w_fc1, w_fc2):
    groups = lax.axis_size("mlp")
    chips = groups // 2
    total = groups * block.shape[0]
    return pl.pallas_call(
        gather_kernel,
        in_specs=[pl.BlockSpec(memory_space=pltpu.VMEM)] * 3,
        out_specs=pl.BlockSpec(memory_space=pltpu.VMEM),
        out_shape=jax.ShapeDtypeStruct((total, w_fc2.shape[1]), jnp.bfloat16),
        scratch_shapes=[
            pltpu.VMEM((total, block.shape[1]), block.dtype),
            pltpu.SemaphoreType.DMA((chips,)),
            pltpu.SemaphoreType.DMA((chips,)),
            pltpu.SemaphoreType.DMA((chips,)),
            pltpu.SemaphoreType.DMA((chips,)),
        ],
        compiler_params=pltpu.CompilerParams(
            collective_id=2, has_side_effects=True, vmem_limit_bytes=48 * 1024 * 1024
        ),
    )(block, w_fc1, w_fc2)


def per_device(
    tokens,
    token_owner,
    token_request,
    cache_len,
    cache_k,
    cache_v,
    w_qkv,
    w_out,
    w_fc1,
    w_fc2,
    ln1_gain,
    ln1_bias,
    ln2_gain,
    ln2_bias,
):
    n_req = lax.axis_size("req")
    n_mlp = lax.axis_size("mlp")
    devices = n_req * n_mlp
    owner_index = lax.axis_index("req") * n_mlp + lax.axis_index("mlp")
    tok_dev, width = tokens.shape
    capacity = max(2, 2 * tok_dev // devices)
    slot_count = devices * capacity
    owners_flat = token_owner.reshape(-1)
    my_owners = lax.dynamic_slice_in_dim(owners_flat, owner_index * tok_dev, tok_dev)
    owner_onehot = (my_owners[:, None] == jnp.arange(devices, dtype=jnp.int32)[None, :]).astype(
        jnp.int32
    )
    ranking = jnp.cumsum(owner_onehot, axis=0) - 1
    my_rank = jnp.sum(owner_onehot * ranking, axis=1)
    column = my_owners * capacity + my_rank
    dispatch = (column[:, None] == jnp.arange(slot_count, dtype=jnp.int32)[None, :]).astype(
        jnp.bfloat16
    )
    outgoing = jnp.einsum("tr,td->rd", dispatch, tokens, preferred_element_type=jnp.float32).astype(
        jnp.bfloat16
    )
    arrived = lax.all_to_all(
        outgoing.reshape(devices, capacity, width),
        ("req", "mlp"),
        split_axis=0,
        concat_axis=0,
        tiled=True,
    )
    projections = jnp.dot(
        arrived.reshape(slot_count, width), w_qkv, preferred_element_type=jnp.float32
    ).astype(jnp.bfloat16)
    global_row, slot_request, filled = slot_table(
        owners_flat, token_request, owner_index, devices, tok_dev, capacity
    )
    attended = attend(projections, cache_k, cache_v, cache_len, global_row, slot_request, filled)
    returned = lax.all_to_all(
        attended.reshape(devices, capacity, width),
        ("req", "mlp"),
        split_axis=0,
        concat_axis=0,
        tiled=True,
    )
    attn_rows = jnp.dot(
        dispatch, returned.reshape(slot_count, width), preferred_element_type=jnp.float32
    ).astype(jnp.bfloat16)
    projected_out = jnp.dot(attn_rows, w_out, preferred_element_type=jnp.float32)
    normed = layer_norm(projected_out + tokens.astype(jnp.float32), ln1_gain, ln1_bias).astype(
        jnp.bfloat16
    )
    summed = scatter_sum(gather_rows(normed, w_fc1, w_fc2))
    return layer_norm(normed.astype(jnp.float32) + summed, ln2_gain, ln2_bias).astype(jnp.bfloat16)


def solution(mesh):
    placed = (
        P(("req", "mlp"), None),
        P(),
        P(),
        P(("req", "mlp")),
        P(("req", "mlp"), None, None),
        P(("req", "mlp"), None, None),
        P(),
        P(),
        P(None, "mlp"),
        P("mlp", None),
        P(),
        P(),
        P(),
        P(),
    )
    return jax.shard_map(
        per_device, mesh=mesh, in_specs=placed, out_specs=P(("req", "mlp"), None), check_vma=False
    )
```

```python
import jax
import jax.numpy as jnp
from jax import lax
from jax.sharding import PartitionSpec as P
from jax.experimental import pallas as pl
from jax.experimental.pallas import tpu as pltpu

HEADS = 16


epsilon = 1e-05


def layer_norm(values, gain, shift):
    center = values - jnp.mean(values, axis=-1, keepdims=True)
    spread = jnp.mean(center * center, axis=-1, keepdims=True)
    return center * lax.rsqrt(spread + epsilon) * gain + shift


def slot_table(owners_flat, requests_flat, owner_index, devices, tok_dev, capacity):
    owners = owners_flat.reshape(devices, tok_dev)
    requests = requests_flat.reshape(devices, tok_dev)
    mine_mask = (owners == owner_index).astype(jnp.int32)
    ranking = jnp.cumsum(mine_mask, axis=1) - 1
    places = jnp.arange(capacity, dtype=jnp.int32)
    hit_table = mine_mask[:, :, None] * (ranking[:, :, None] == places[None, None, :]).astype(
        jnp.int32
    )
    filled = jnp.sum(hit_table, axis=1)
    positions = jnp.arange(tok_dev, dtype=jnp.int32)
    local_row = jnp.sum(hit_table * positions[None, :, None], axis=1)
    sources = jnp.arange(devices, dtype=jnp.int32)[:, None]
    global_row = jnp.where(filled > 0, sources * tok_dev + local_row, -1).reshape(-1)
    slot_request = jnp.sum(hit_table * requests[:, :, None], axis=1).reshape(-1)
    return (global_row, slot_request, filled.reshape(-1))


def attention_kernel(
    q_ref, kn_ref, vn_ref, k_ref, v_ref, rreq_ref, rrow_ref, rfill_ref, ctag_ref, ntag_ref, nrow_ref, o_ref
):
    head_dim = q_ref.shape[1] // 2
    score_scale = head_dim ** (-0.5)
    q = q_ref[...]
    keys = k_ref[...]
    values = v_ref[...]
    key_new = kn_ref[...]
    value_new = vn_ref[...]
    row_request = rreq_ref[...]
    old_mask = ctag_ref[...] == row_request
    new_mask = (ntag_ref[...] == row_request) & (nrow_ref[...] <= rrow_ref[...])
    lane = lax.broadcasted_iota(jnp.int32, (1, q.shape[1]), 1)
    contract = (((1,), (1,)), ((), ()))
    result = None
    for half in range(2):
        in_head = (lane // head_dim) == half
        q_head = jnp.where(in_head, q, jnp.zeros_like(q))
        old_score = (
            lax.dot_general(q_head, keys, contract, preferred_element_type=jnp.float32) * score_scale
        )
        new_score = (
            lax.dot_general(q_head, key_new, contract, preferred_element_type=jnp.float32)
            * score_scale
        )
        old_exp = jnp.where(old_mask, jnp.exp(old_score), jnp.float32(0.0))
        new_exp = jnp.where(new_mask, jnp.exp(new_score), jnp.float32(0.0))
        total = jnp.sum(old_exp, axis=1, keepdims=True) + jnp.sum(new_exp, axis=1, keepdims=True)
        total = jnp.where(total > 0, total, jnp.float32(1.0))
        inverse = 1.0 / total
        old_weight = (old_exp * inverse).astype(jnp.bfloat16)
        new_weight = (new_exp * inverse).astype(jnp.bfloat16)
        part = jnp.dot(old_weight, values, preferred_element_type=jnp.float32) + jnp.dot(
            new_weight, value_new, preferred_element_type=jnp.float32
        )
        result = part if result is None else jnp.where(in_head, part, result)
    result = jnp.where(rfill_ref[...] > 0, result, jnp.float32(0.0))
    o_ref[...] = result.astype(o_ref.dtype)


def attend(projections, cache_keys, cache_values, lengths, global_row, slot_request, filled):
    slot_count = projections.shape[0]
    width = projections.shape[1] // 3
    requests, context = cache_keys.shape[0], cache_keys.shape[1]
    pair = 128
    pairs = width // pair
    keys = cache_keys.reshape(requests * context, width)
    values = cache_values.reshape(requests * context, width)
    key_owner = jnp.arange(requests * context, dtype=jnp.int32) // context
    key_place = jnp.arange(requests * context, dtype=jnp.int32) % context
    key_limit = jnp.repeat(lengths, context)
    column_tag = jnp.where(key_place < key_limit, key_owner, -1).reshape(1, -1)
    new_tag = jnp.where(filled > 0, slot_request, -1).reshape(1, -1)
    new_row = global_row.reshape(1, -1)
    row_request = slot_request.reshape(-1, 1)
    row_index = global_row.reshape(-1, 1)
    row_filled = filled.reshape(-1, 1)
    keyed = requests * context
    whole = lambda shape: pl.BlockSpec(shape, lambda p: (0, 0))
    return pl.pallas_call(
        attention_kernel,
        grid=(pairs,),
        in_specs=[
            pl.BlockSpec((slot_count, pair), lambda p: (0, p)),
            pl.BlockSpec((slot_count, pair), lambda p: (0, pairs + p)),
            pl.BlockSpec((slot_count, pair), lambda p: (0, 2 * pairs + p)),
            pl.BlockSpec((keyed, pair), lambda p: (0, p)),
            pl.BlockSpec((keyed, pair), lambda p: (0, p)),
            whole((slot_count, 1)),
            whole((slot_count, 1)),
            whole((slot_count, 1)),
            whole((1, keyed)),
            whole((1, slot_count)),
            whole((1, slot_count)),
        ],
        out_specs=pl.BlockSpec((slot_count, pair), lambda p: (0, p)),
        out_shape=jax.ShapeDtypeStruct((slot_count, width), jnp.bfloat16),
        compiler_params=pltpu.CompilerParams(vmem_limit_bytes=48 * 1024 * 1024),
    )(
        projections,
        projections,
        projections,
        keys,
        values,
        row_request,
        row_index,
        row_filled,
        column_tag,
        new_tag,
        new_row,
    )


def scatter_kernel(part_ref, o_ref, pair_buf, send_buf, ring_buf, pair_send, pair_recv, ring_send, ring_recv):
    req = lax.axis_index("req")
    me = lax.axis_index("mlp")
    chips = lax.axis_size("mlp") // 2
    chip, core = me // 2, lax.rem(me, 2)
    partner = chip * 2 + 1 - core
    step = 1 - 2 * core
    ahead = lax.rem(chip + step + chips, chips)
    behind = lax.rem(chip - step + chips, chips)
    across = lax.rem(chip + 2, chips)
    rows = o_ref.shape[0]
    barrier = pltpu.get_barrier_semaphore()
    pl.semaphore_signal(barrier, 1, device_id=(req, partner), device_id_type=pl.DeviceIdType.MESH)
    pl.semaphore_signal(barrier, 1, device_id=(req, ahead * 2 + core), device_id_type=pl.DeviceIdType.MESH)
    pl.semaphore_signal(barrier, 1, device_id=(req, behind * 2 + core), device_id_type=pl.DeviceIdType.MESH)
    pl.semaphore_wait(barrier, 3)

    def pair_copy(z):
        block = z * 2 + 1 - core
        return pltpu.make_async_remote_copy(
            src_ref=part_ref.at[pl.ds(pl.multiple_of(block * rows, rows), rows)],
            dst_ref=pair_buf.at[z],
            send_sem=pair_send.at[z],
            recv_sem=pair_recv.at[z],
            device_id=(req, partner),
            device_id_type=pl.DeviceIdType.MESH,
        )

    for z in range(chips):
        pair_copy(z).start()
    for z in range(chips):
        pair_copy(z).wait()

    def summed(z):
        mine = part_ref[pl.ds(pl.multiple_of((z * 2 + core) * rows, rows), rows), :]
        return mine.astype(jnp.float32) + pair_buf[z].astype(jnp.float32)

    def ring_copy(kind, target):
        return pltpu.make_async_remote_copy(
            src_ref=send_buf.at[kind],
            dst_ref=ring_buf.at[kind],
            send_sem=ring_send.at[kind],
            recv_sem=ring_recv.at[kind],
            device_id=(req, target * 2 + core),
            device_id_type=pl.DeviceIdType.MESH,
        )

    send_buf[1] = summed(across).astype(send_buf.dtype)
    ring_copy(1, ahead).start()
    send_buf[0] = summed(behind).astype(send_buf.dtype)
    ring_copy(0, behind).start()
    ring_copy(1, ahead).wait_recv()
    send_buf[2] = (summed(ahead) + ring_buf[1].astype(jnp.float32)).astype(send_buf.dtype)
    ring_copy(2, ahead).start()
    total = summed(chip)
    ring_copy(0, behind).wait()
    total = total + ring_buf[0].astype(jnp.float32)
    ring_copy(1, ahead).wait_send()
    ring_copy(2, ahead).wait()
    o_ref[...] = total + ring_buf[2].astype(jnp.float32)


def scatter_sum(partial):
    groups = lax.axis_size("mlp")
    chips = groups // 2
    rows = partial.shape[0] // groups
    width = partial.shape[1]
    return pl.pallas_call(
        scatter_kernel,
        in_specs=[pl.BlockSpec(memory_space=pltpu.VMEM)],
        out_specs=pl.BlockSpec(memory_space=pltpu.VMEM),
        out_shape=jax.ShapeDtypeStruct((rows, width), jnp.float32),
        scratch_shapes=[
            pltpu.VMEM((chips, rows, width), partial.dtype),
            pltpu.VMEM((3, rows, width), partial.dtype),
            pltpu.VMEM((3, rows, width), partial.dtype),
            pltpu.SemaphoreType.DMA((chips,)),
            pltpu.SemaphoreType.DMA((chips,)),
            pltpu.SemaphoreType.DMA((3,)),
            pltpu.SemaphoreType.DMA((3,)),
        ],
        compiler_params=pltpu.CompilerParams(
            collective_id=1, has_side_effects=True, vmem_limit_bytes=48 * 1024 * 1024
        ),
    )(partial)


def gather_kernel(
    x_ref, w1_ref, w2_ref, o_ref, held, ring_send, ring_recv, pair_send, pair_recv
):
    req = lax.axis_index("req")
    me = lax.axis_index("mlp")
    chips = lax.axis_size("mlp") // 2
    chip, core = me // 2, lax.rem(me, 2)
    partner = chip * 2 + 1 - core
    step = 1 - 2 * core
    ahead = lax.rem(chip + step + chips, chips)
    behind = lax.rem(chip - step + chips, chips)
    across = lax.rem(chip + 2, chips)
    rows = x_ref.shape[0]
    barrier = pltpu.get_barrier_semaphore()
    pl.semaphore_signal(barrier, 1, device_id=(req, partner), device_id_type=pl.DeviceIdType.MESH)
    pl.semaphore_signal(barrier, 1, device_id=(req, ahead * 2 + core), device_id_type=pl.DeviceIdType.MESH)
    pl.semaphore_signal(barrier, 1, device_id=(req, behind * 2 + core), device_id_type=pl.DeviceIdType.MESH)
    pl.semaphore_wait(barrier, 3)

    def block_rows(z, which):
        return pl.ds(pl.multiple_of((z * 2 + which) * rows, rows), rows)

    origins = (chip, behind, ahead, across)

    def ring_copy(kind):
        source = x_ref if kind < 2 else held.at[block_rows(behind, core)]
        origin = chip if kind < 2 else behind
        target = ahead if kind != 1 else behind
        return pltpu.make_async_remote_copy(
            src_ref=source,
            dst_ref=held.at[block_rows(origin, core)],
            send_sem=ring_send.at[kind],
            recv_sem=ring_recv.at[kind],
            device_id=(req, target * 2 + core),
            device_id_type=pl.DeviceIdType.MESH,
        )

    def pair_copy(kind):
        source = x_ref if kind == 0 else held.at[block_rows(origins[kind], core)]
        return pltpu.make_async_remote_copy(
            src_ref=source,
            dst_ref=held.at[block_rows(origins[kind], core)],
            send_sem=pair_send.at[kind],
            recv_sem=pair_recv.at[kind],
            device_id=(req, partner),
            device_id_type=pl.DeviceIdType.MESH,
        )

    def feed_forward(block, place):
        hidden = jnp.dot(block, w1_ref[...], preferred_element_type=jnp.float32)
        hidden = (hidden * 0.5 * (1.0 + lax.erf(hidden * (2.0 ** -0.5)))).astype(jnp.bfloat16)
        o_ref[place, :] = jnp.dot(hidden, w2_ref[...], preferred_element_type=jnp.float32).astype(
            o_ref.dtype
        )

    ring_copy(0).start()
    ring_copy(1).start()
    pair_copy(0).start()
    feed_forward(x_ref[...], block_rows(chip, core))
    ring_copy(0).wait_recv()
    ring_copy(2).start()
    pair_copy(1).start()
    feed_forward(held[block_rows(behind, core), :], block_rows(behind, core))
    ring_copy(1).wait_recv()
    pair_copy(2).start()
    feed_forward(held[block_rows(ahead, core), :], block_rows(ahead, core))
    ring_copy(2).wait_recv()
    pair_copy(3).start()
    feed_forward(held[block_rows(across, core), :], block_rows(across, core))
    partner_origins = (chip, ahead, behind, across)
    for kind in range(4):
        copy = pair_copy(kind)
        copy.wait_recv()
        place = block_rows(partner_origins[kind], 1 - core)
        feed_forward(held[place, :], place)
    for kind in range(3):
        ring_copy(kind).wait_send()
    for kind in range(4):
        pair_copy(kind).wait_send()


def gather_rows(block, w_fc1, w_fc2):
    groups = lax.axis_size("mlp")
    chips = groups // 2
    total = groups * block.shape[0]
    return pl.pallas_call(
        gather_kernel,
        in_specs=[pl.BlockSpec(memory_space=pltpu.VMEM)] * 3,
        out_specs=pl.BlockSpec(memory_space=pltpu.VMEM),
        out_shape=jax.ShapeDtypeStruct((total, w_fc2.shape[1]), jnp.bfloat16),
        scratch_shapes=[
            pltpu.VMEM((total, block.shape[1]), block.dtype),
            pltpu.SemaphoreType.DMA((chips,)),
            pltpu.SemaphoreType.DMA((chips,)),
            pltpu.SemaphoreType.DMA((chips,)),
            pltpu.SemaphoreType.DMA((chips,)),
        ],
        compiler_params=pltpu.CompilerParams(
            collective_id=2, has_side_effects=True, vmem_limit_bytes=48 * 1024 * 1024
        ),
    )(block, w_fc1, w_fc2)


def per_device(
    tokens,
    token_owner,
    token_request,
    cache_len,
    cache_k,
    cache_v,
    w_qkv,
    w_out,
    w_fc1,
    w_fc2,
    ln1_gain,
    ln1_bias,
    ln2_gain,
    ln2_bias,
):
    n_req = lax.axis_size("req")
    n_mlp = lax.axis_size("mlp")
    devices = n_req * n_mlp
    owner_index = lax.axis_index("req") * n_mlp + lax.axis_index("mlp")
    tok_dev, width = tokens.shape
    capacity = max(2, 2 * tok_dev // devices)
    slot_count = devices * capacity
    owners_flat = token_owner.reshape(-1)
    my_owners = lax.dynamic_slice_in_dim(owners_flat, owner_index * tok_dev, tok_dev)
    owner_onehot = (my_owners[:, None] == jnp.arange(devices, dtype=jnp.int32)[None, :]).astype(
        jnp.int32
    )
    ranking = jnp.cumsum(owner_onehot, axis=0) - 1
    my_rank = jnp.sum(owner_onehot * ranking, axis=1)
    column = my_owners * capacity + my_rank
    dispatch = (column[:, None] == jnp.arange(slot_count, dtype=jnp.int32)[None, :]).astype(
        jnp.bfloat16
    )
    outgoing = jnp.einsum("tr,td->rd", dispatch, tokens, preferred_element_type=jnp.float32).astype(
        jnp.bfloat16
    )
    arrived = lax.all_to_all(
        outgoing.reshape(devices, capacity * width // 128, 128),
        ("req", "mlp"),
        split_axis=0,
        concat_axis=0,
        tiled=True,
    )
    projections = jnp.dot(
        arrived.reshape(slot_count, width), w_qkv, preferred_element_type=jnp.float32
    ).astype(jnp.bfloat16)
    global_row, slot_request, filled = slot_table(
        owners_flat, token_request, owner_index, devices, tok_dev, capacity
    )
    attended = attend(projections, cache_k, cache_v, cache_len, global_row, slot_request, filled)
    returned = lax.all_to_all(
        attended.reshape(devices, capacity * width // 128, 128),
        ("req", "mlp"),
        split_axis=0,
        concat_axis=0,
        tiled=True,
    )
    attn_rows = jnp.dot(
        dispatch, returned.reshape(slot_count, width), preferred_element_type=jnp.float32
    ).astype(jnp.bfloat16)
    projected_out = jnp.dot(attn_rows, w_out, preferred_element_type=jnp.float32)
    normed = layer_norm(projected_out + tokens.astype(jnp.float32), ln1_gain, ln1_bias).astype(
        jnp.bfloat16
    )
    summed = scatter_sum(gather_rows(normed, w_fc1, w_fc2))
    return layer_norm(normed.astype(jnp.float32) + summed, ln2_gain, ln2_bias).astype(jnp.bfloat16)


def solution(mesh):
    placed = (
        P(("req", "mlp"), None),
        P(),
        P(),
        P(("req", "mlp")),
        P(("req", "mlp"), None, None),
        P(("req", "mlp"), None, None),
        P(),
        P(),
        P(None, "mlp"),
        P("mlp", None),
        P(),
        P(),
        P(),
        P(),
    )
    return jax.shard_map(
        per_device, mesh=mesh, in_specs=placed, out_specs=P(("req", "mlp"), None), check_vma=False
    )
```

```python
import jax
import jax.numpy as jnp
from jax import lax
from jax.sharding import PartitionSpec as P
from jax.experimental import pallas as pl
from jax.experimental.pallas import tpu as pltpu

HEADS = 16


epsilon = 1e-05


def layer_norm(values, gain, shift):
    center = values - jnp.mean(values, axis=-1, keepdims=True)
    spread = jnp.mean(center * center, axis=-1, keepdims=True)
    return center * lax.rsqrt(spread + epsilon) * gain + shift


def slot_table(owners_flat, requests_flat, owner_index, devices, tok_dev, capacity):
    owners = owners_flat.reshape(devices, tok_dev)
    requests = requests_flat.reshape(devices, tok_dev)
    mine_mask = (owners == owner_index).astype(jnp.int32)
    ranking = jnp.cumsum(mine_mask, axis=1) - 1
    places = jnp.arange(capacity, dtype=jnp.int32)
    hit_table = mine_mask[:, :, None] * (ranking[:, :, None] == places[None, None, :]).astype(
        jnp.int32
    )
    filled = jnp.sum(hit_table, axis=1)
    positions = jnp.arange(tok_dev, dtype=jnp.int32)
    local_row = jnp.sum(hit_table * positions[None, :, None], axis=1)
    sources = jnp.arange(devices, dtype=jnp.int32)[:, None]
    global_row = jnp.where(filled > 0, sources * tok_dev + local_row, -1).reshape(-1)
    slot_request = jnp.sum(hit_table * requests[:, :, None], axis=1).reshape(-1)
    return (global_row, slot_request, filled.reshape(-1))


def attention_kernel(
    q_ref, kn_ref, vn_ref, k_ref, v_ref, rreq_ref, rrow_ref, rfill_ref, ctag_ref, ntag_ref, nrow_ref, o_ref
):
    head_dim = q_ref.shape[1] // 2
    score_scale = head_dim ** (-0.5)
    q = q_ref[...]
    keys = k_ref[...]
    values = v_ref[...]
    key_new = kn_ref[...]
    value_new = vn_ref[...]
    row_request = rreq_ref[...]
    old_mask = ctag_ref[...] == row_request
    new_mask = (ntag_ref[...] == row_request) & (nrow_ref[...] <= rrow_ref[...])
    lane = lax.broadcasted_iota(jnp.int32, (1, q.shape[1]), 1)
    contract = (((1,), (1,)), ((), ()))
    result = None
    for half in range(2):
        in_head = (lane // head_dim) == half
        q_head = jnp.where(in_head, q, jnp.zeros_like(q))
        old_score = (
            lax.dot_general(q_head, keys, contract, preferred_element_type=jnp.float32) * score_scale
        )
        new_score = (
            lax.dot_general(q_head, key_new, contract, preferred_element_type=jnp.float32)
            * score_scale
        )
        old_exp = jnp.where(old_mask, jnp.exp(old_score), jnp.float32(0.0))
        new_exp = jnp.where(new_mask, jnp.exp(new_score), jnp.float32(0.0))
        total = jnp.sum(old_exp, axis=1, keepdims=True) + jnp.sum(new_exp, axis=1, keepdims=True)
        total = jnp.where(total > 0, total, jnp.float32(1.0))
        inverse = 1.0 / total
        old_weight = (old_exp * inverse).astype(jnp.bfloat16)
        new_weight = (new_exp * inverse).astype(jnp.bfloat16)
        part = jnp.dot(old_weight, values, preferred_element_type=jnp.float32) + jnp.dot(
            new_weight, value_new, preferred_element_type=jnp.float32
        )
        result = part if result is None else jnp.where(in_head, part, result)
    result = jnp.where(rfill_ref[...] > 0, result, jnp.float32(0.0))
    o_ref[...] = result.astype(o_ref.dtype)


def attend(projections, cache_keys, cache_values, lengths, global_row, slot_request, filled):
    slot_count = projections.shape[0]
    width = projections.shape[1] // 3
    requests, context = cache_keys.shape[0], cache_keys.shape[1]
    pair = 128
    pairs = width // pair
    keys = cache_keys.reshape(requests * context, width)
    values = cache_values.reshape(requests * context, width)
    key_owner = jnp.arange(requests * context, dtype=jnp.int32) // context
    key_place = jnp.arange(requests * context, dtype=jnp.int32) % context
    key_limit = jnp.repeat(lengths, context)
    column_tag = jnp.where(key_place < key_limit, key_owner, -1).reshape(1, -1)
    new_tag = jnp.where(filled > 0, slot_request, -1).reshape(1, -1)
    new_row = global_row.reshape(1, -1)
    row_request = slot_request.reshape(-1, 1)
    row_index = global_row.reshape(-1, 1)
    row_filled = filled.reshape(-1, 1)
    keyed = requests * context
    whole = lambda shape: pl.BlockSpec(shape, lambda p: (0, 0))
    return pl.pallas_call(
        attention_kernel,
        grid=(pairs,),
        in_specs=[
            pl.BlockSpec((slot_count, pair), lambda p: (0, p)),
            pl.BlockSpec((slot_count, pair), lambda p: (0, pairs + p)),
            pl.BlockSpec((slot_count, pair), lambda p: (0, 2 * pairs + p)),
            pl.BlockSpec((keyed, pair), lambda p: (0, p)),
            pl.BlockSpec((keyed, pair), lambda p: (0, p)),
            whole((slot_count, 1)),
            whole((slot_count, 1)),
            whole((slot_count, 1)),
            whole((1, keyed)),
            whole((1, slot_count)),
            whole((1, slot_count)),
        ],
        out_specs=pl.BlockSpec((slot_count, pair), lambda p: (0, p)),
        out_shape=jax.ShapeDtypeStruct((slot_count, width), jnp.bfloat16),
        compiler_params=pltpu.CompilerParams(vmem_limit_bytes=48 * 1024 * 1024),
    )(
        projections,
        projections,
        projections,
        keys,
        values,
        row_request,
        row_index,
        row_filled,
        column_tag,
        new_tag,
        new_row,
    )


def scatter_kernel(part_ref, o_ref, pair_buf, send_buf, ring_buf, pair_send, pair_recv, ring_send, ring_recv):
    req = lax.axis_index("req")
    me = lax.axis_index("mlp")
    chips = lax.axis_size("mlp") // 2
    chip, core = me // 2, lax.rem(me, 2)
    partner = chip * 2 + 1 - core
    step = 1 - 2 * core
    ahead = lax.rem(chip + step + chips, chips)
    behind = lax.rem(chip - step + chips, chips)
    across = lax.rem(chip + 2, chips)
    rows = o_ref.shape[0]
    barrier = pltpu.get_barrier_semaphore()
    pl.semaphore_signal(barrier, 1, device_id=(req, partner), device_id_type=pl.DeviceIdType.MESH)
    pl.semaphore_signal(barrier, 1, device_id=(req, ahead * 2 + core), device_id_type=pl.DeviceIdType.MESH)
    pl.semaphore_signal(barrier, 1, device_id=(req, behind * 2 + core), device_id_type=pl.DeviceIdType.MESH)
    pl.semaphore_wait(barrier, 3)

    def pair_copy(z):
        block = z * 2 + 1 - core
        return pltpu.make_async_remote_copy(
            src_ref=part_ref.at[pl.ds(pl.multiple_of(block * rows, rows), rows)],
            dst_ref=pair_buf.at[z],
            send_sem=pair_send.at[z],
            recv_sem=pair_recv.at[z],
            device_id=(req, partner),
            device_id_type=pl.DeviceIdType.MESH,
        )

    for z in range(chips):
        pair_copy(z).start()
    for z in range(chips):
        pair_copy(z).wait()

    def summed(z):
        mine = part_ref[pl.ds(pl.multiple_of((z * 2 + core) * rows, rows), rows), :]
        return mine.astype(jnp.float32) + pair_buf[z].astype(jnp.float32)

    def ring_copy(kind, target):
        return pltpu.make_async_remote_copy(
            src_ref=send_buf.at[kind],
            dst_ref=ring_buf.at[kind],
            send_sem=ring_send.at[kind],
            recv_sem=ring_recv.at[kind],
            device_id=(req, target * 2 + core),
            device_id_type=pl.DeviceIdType.MESH,
        )

    send_buf[1] = summed(across).astype(send_buf.dtype)
    ring_copy(1, ahead).start()
    send_buf[0] = summed(behind).astype(send_buf.dtype)
    ring_copy(0, behind).start()
    ring_copy(1, ahead).wait_recv()
    send_buf[2] = (summed(ahead) + ring_buf[1].astype(jnp.float32)).astype(send_buf.dtype)
    ring_copy(2, ahead).start()
    total = summed(chip)
    ring_copy(0, behind).wait()
    total = total + ring_buf[0].astype(jnp.float32)
    ring_copy(1, ahead).wait_send()
    ring_copy(2, ahead).wait()
    o_ref[...] = total + ring_buf[2].astype(jnp.float32)


def scatter_sum(partial):
    groups = lax.axis_size("mlp")
    chips = groups // 2
    rows = partial.shape[0] // groups
    width = partial.shape[1]
    return pl.pallas_call(
        scatter_kernel,
        in_specs=[pl.BlockSpec(memory_space=pltpu.VMEM)],
        out_specs=pl.BlockSpec(memory_space=pltpu.VMEM),
        out_shape=jax.ShapeDtypeStruct((rows, width), jnp.float32),
        scratch_shapes=[
            pltpu.VMEM((chips, rows, width), partial.dtype),
            pltpu.VMEM((3, rows, width), partial.dtype),
            pltpu.VMEM((3, rows, width), partial.dtype),
            pltpu.SemaphoreType.DMA((chips,)),
            pltpu.SemaphoreType.DMA((chips,)),
            pltpu.SemaphoreType.DMA((3,)),
            pltpu.SemaphoreType.DMA((3,)),
        ],
        compiler_params=pltpu.CompilerParams(
            collective_id=1, has_side_effects=True, vmem_limit_bytes=48 * 1024 * 1024
        ),
    )(partial)


def gather_kernel(
    x_ref, w1_hbm, w2_hbm, o_ref, held, w1_ref, w2_ref, load_sem, ring_send, ring_recv, pair_send, pair_recv
):
    load_one = pltpu.make_async_copy(w1_hbm, w1_ref, load_sem.at[0])
    load_two = pltpu.make_async_copy(w2_hbm, w2_ref, load_sem.at[1])
    load_one.start()
    load_two.start()
    req = lax.axis_index("req")
    me = lax.axis_index("mlp")
    chips = lax.axis_size("mlp") // 2
    chip, core = me // 2, lax.rem(me, 2)
    partner = chip * 2 + 1 - core
    step = 1 - 2 * core
    ahead = lax.rem(chip + step + chips, chips)
    behind = lax.rem(chip - step + chips, chips)
    across = lax.rem(chip + 2, chips)
    rows = x_ref.shape[0]
    barrier = pltpu.get_barrier_semaphore()
    pl.semaphore_signal(barrier, 1, device_id=(req, partner), device_id_type=pl.DeviceIdType.MESH)
    pl.semaphore_signal(barrier, 1, device_id=(req, ahead * 2 + core), device_id_type=pl.DeviceIdType.MESH)
    pl.semaphore_signal(barrier, 1, device_id=(req, behind * 2 + core), device_id_type=pl.DeviceIdType.MESH)
    pl.semaphore_wait(barrier, 3)

    def block_rows(z, which):
        return pl.ds(pl.multiple_of((z * 2 + which) * rows, rows), rows)

    origins = (chip, behind, ahead, across)

    def ring_copy(kind):
        source = x_ref if kind < 2 else held.at[block_rows(behind, core)]
        origin = chip if kind < 2 else behind
        target = ahead if kind != 1 else behind
        return pltpu.make_async_remote_copy(
            src_ref=source,
            dst_ref=held.at[block_rows(origin, core)],
            send_sem=ring_send.at[kind],
            recv_sem=ring_recv.at[kind],
            device_id=(req, target * 2 + core),
            device_id_type=pl.DeviceIdType.MESH,
        )

    def pair_copy(kind):
        source = x_ref if kind == 0 else held.at[block_rows(origins[kind], core)]
        return pltpu.make_async_remote_copy(
            src_ref=source,
            dst_ref=held.at[block_rows(origins[kind], core)],
            send_sem=pair_send.at[kind],
            recv_sem=pair_recv.at[kind],
            device_id=(req, partner),
            device_id_type=pl.DeviceIdType.MESH,
        )

    def feed_forward(block, place):
        hidden = jnp.dot(block, w1_ref[...], preferred_element_type=jnp.float32)
        hidden = (hidden * 0.5 * (1.0 + lax.erf(hidden * (2.0 ** -0.5)))).astype(jnp.bfloat16)
        o_ref[place, :] = jnp.dot(hidden, w2_ref[...], preferred_element_type=jnp.float32).astype(
            o_ref.dtype
        )

    ring_copy(0).start()
    ring_copy(1).start()
    pair_copy(0).start()
    load_one.wait()
    load_two.wait()
    feed_forward(x_ref[...], block_rows(chip, core))
    ring_copy(0).wait_recv()
    ring_copy(2).start()
    pair_copy(1).start()
    feed_forward(held[block_rows(behind, core), :], block_rows(behind, core))
    ring_copy(1).wait_recv()
    pair_copy(2).start()
    feed_forward(held[block_rows(ahead, core), :], block_rows(ahead, core))
    ring_copy(2).wait_recv()
    pair_copy(3).start()
    feed_forward(held[block_rows(across, core), :], block_rows(across, core))
    partner_origins = (chip, ahead, behind, across)
    for kind in range(4):
        copy = pair_copy(kind)
        copy.wait_recv()
        place = block_rows(partner_origins[kind], 1 - core)
        feed_forward(held[place, :], place)
    for kind in range(3):
        ring_copy(kind).wait_send()
    for kind in range(4):
        pair_copy(kind).wait_send()


def gather_rows(block, w_fc1, w_fc2):
    groups = lax.axis_size("mlp")
    chips = groups // 2
    total = groups * block.shape[0]
    return pl.pallas_call(
        gather_kernel,
        in_specs=[
            pl.BlockSpec(memory_space=pltpu.VMEM),
            pl.BlockSpec(memory_space=pl.ANY),
            pl.BlockSpec(memory_space=pl.ANY),
        ],
        out_specs=pl.BlockSpec(memory_space=pltpu.VMEM),
        out_shape=jax.ShapeDtypeStruct((total, w_fc2.shape[1]), jnp.bfloat16),
        scratch_shapes=[
            pltpu.VMEM((total, block.shape[1]), block.dtype),
            pltpu.VMEM(w_fc1.shape, w_fc1.dtype),
            pltpu.VMEM(w_fc2.shape, w_fc2.dtype),
            pltpu.SemaphoreType.DMA((2,)),
            pltpu.SemaphoreType.DMA((chips,)),
            pltpu.SemaphoreType.DMA((chips,)),
            pltpu.SemaphoreType.DMA((chips,)),
            pltpu.SemaphoreType.DMA((chips,)),
        ],
        compiler_params=pltpu.CompilerParams(
            collective_id=2, has_side_effects=True, vmem_limit_bytes=48 * 1024 * 1024
        ),
    )(block, w_fc1, w_fc2)


def per_device(
    tokens,
    token_owner,
    token_request,
    cache_len,
    cache_k,
    cache_v,
    w_qkv,
    w_out,
    w_fc1,
    w_fc2,
    ln1_gain,
    ln1_bias,
    ln2_gain,
    ln2_bias,
):
    n_req = lax.axis_size("req")
    n_mlp = lax.axis_size("mlp")
    devices = n_req * n_mlp
    owner_index = lax.axis_index("req") * n_mlp + lax.axis_index("mlp")
    tok_dev, width = tokens.shape
    capacity = max(2, 2 * tok_dev // devices)
    slot_count = devices * capacity
    owners_flat = token_owner.reshape(-1)
    my_owners = lax.dynamic_slice_in_dim(owners_flat, owner_index * tok_dev, tok_dev)
    owner_onehot = (my_owners[:, None] == jnp.arange(devices, dtype=jnp.int32)[None, :]).astype(
        jnp.int32
    )
    ranking = jnp.cumsum(owner_onehot, axis=0) - 1
    my_rank = jnp.sum(owner_onehot * ranking, axis=1)
    column = my_owners * capacity + my_rank
    dispatch = (column[:, None] == jnp.arange(slot_count, dtype=jnp.int32)[None, :]).astype(
        jnp.bfloat16
    )
    outgoing = jnp.einsum("tr,td->rd", dispatch, tokens, preferred_element_type=jnp.float32).astype(
        jnp.bfloat16
    )
    arrived = lax.all_to_all(
        outgoing.reshape(devices, capacity, width),
        ("req", "mlp"),
        split_axis=0,
        concat_axis=0,
        tiled=True,
    )
    projections = jnp.dot(
        arrived.reshape(slot_count, width), w_qkv, preferred_element_type=jnp.float32
    ).astype(jnp.bfloat16)
    global_row, slot_request, filled = slot_table(
        owners_flat, token_request, owner_index, devices, tok_dev, capacity
    )
    attended = attend(projections, cache_k, cache_v, cache_len, global_row, slot_request, filled)
    returned = lax.all_to_all(
        attended.reshape(devices, capacity, width),
        ("req", "mlp"),
        split_axis=0,
        concat_axis=0,
        tiled=True,
    )
    attn_rows = jnp.dot(
        dispatch, returned.reshape(slot_count, width), preferred_element_type=jnp.float32
    ).astype(jnp.bfloat16)
    projected_out = jnp.dot(attn_rows, w_out, preferred_element_type=jnp.float32)
    normed = layer_norm(projected_out + tokens.astype(jnp.float32), ln1_gain, ln1_bias).astype(
        jnp.bfloat16
    )
    summed = scatter_sum(gather_rows(normed, w_fc1, w_fc2))
    return layer_norm(normed.astype(jnp.float32) + summed, ln2_gain, ln2_bias).astype(jnp.bfloat16)


def solution(mesh):
    placed = (
        P(("req", "mlp"), None),
        P(),
        P(),
        P(("req", "mlp")),
        P(("req", "mlp"), None, None),
        P(("req", "mlp"), None, None),
        P(),
        P(),
        P(None, "mlp"),
        P("mlp", None),
        P(),
        P(),
        P(),
        P(),
    )
    return jax.shard_map(
        per_device, mesh=mesh, in_specs=placed, out_specs=P(("req", "mlp"), None), check_vma=False
    )
```

```python
import jax
import jax.numpy as jnp
from jax import lax
from jax.sharding import PartitionSpec as P
from jax.experimental import pallas as pl
from jax.experimental.pallas import tpu as pltpu

HEADS = 16


epsilon = 1e-05


def layer_norm(values, gain, shift):
    center = values - jnp.mean(values, axis=-1, keepdims=True)
    spread = jnp.mean(center * center, axis=-1, keepdims=True)
    return center * lax.rsqrt(spread + epsilon) * gain + shift


def slot_table(owners_flat, requests_flat, owner_index, devices, tok_dev, capacity):
    owners = owners_flat.reshape(devices, tok_dev)
    requests = requests_flat.reshape(devices, tok_dev)
    mine_mask = (owners == owner_index).astype(jnp.int32)
    ranking = jnp.cumsum(mine_mask, axis=1) - 1
    places = jnp.arange(capacity, dtype=jnp.int32)
    hit_table = mine_mask[:, :, None] * (ranking[:, :, None] == places[None, None, :]).astype(
        jnp.int32
    )
    filled = jnp.sum(hit_table, axis=1)
    positions = jnp.arange(tok_dev, dtype=jnp.int32)
    local_row = jnp.sum(hit_table * positions[None, :, None], axis=1)
    sources = jnp.arange(devices, dtype=jnp.int32)[:, None]
    global_row = jnp.where(filled > 0, sources * tok_dev + local_row, -1).reshape(-1)
    slot_request = jnp.sum(hit_table * requests[:, :, None], axis=1).reshape(-1)
    return (global_row, slot_request, filled.reshape(-1))


def attention_kernel(
    q_ref, kn_ref, vn_ref, k_ref, v_ref, rreq_ref, rrow_ref, rfill_ref, ctag_ref, ntag_ref, nrow_ref, o_ref
):
    head_dim = q_ref.shape[1] // 2
    score_scale = head_dim ** (-0.5)
    q = q_ref[...] * jnp.asarray(score_scale, q_ref.dtype)
    keys = k_ref[...]
    values = v_ref[...]
    key_new = kn_ref[...]
    value_new = vn_ref[...]
    row_request = rreq_ref[...]
    old_mask = ctag_ref[...] == row_request
    new_mask = (ntag_ref[...] == row_request) & (nrow_ref[...] <= rrow_ref[...])
    lane = lax.broadcasted_iota(jnp.int32, (1, q.shape[1]), 1)
    contract = (((1,), (1,)), ((), ()))
    result = None
    for half in range(2):
        in_head = (lane // head_dim) == half
        q_head = jnp.where(in_head, q, jnp.zeros_like(q))
        old_score = lax.dot_general(q_head, keys, contract, preferred_element_type=jnp.float32)
        new_score = lax.dot_general(q_head, key_new, contract, preferred_element_type=jnp.float32)
        old_exp = jnp.where(old_mask, jnp.exp(old_score), jnp.float32(0.0))
        new_exp = jnp.where(new_mask, jnp.exp(new_score), jnp.float32(0.0))
        total = jnp.sum(old_exp, axis=1, keepdims=True) + jnp.sum(new_exp, axis=1, keepdims=True)
        total = jnp.where(total > 0, total, jnp.float32(1.0))
        inverse = 1.0 / total
        old_weight = (old_exp * inverse).astype(jnp.bfloat16)
        new_weight = (new_exp * inverse).astype(jnp.bfloat16)
        part = jnp.dot(old_weight, values, preferred_element_type=jnp.float32) + jnp.dot(
            new_weight, value_new, preferred_element_type=jnp.float32
        )
        result = part if result is None else jnp.where(in_head, part, result)
    result = jnp.where(rfill_ref[...] > 0, result, jnp.float32(0.0))
    o_ref[...] = result.astype(o_ref.dtype)


def attend(projections, cache_keys, cache_values, lengths, global_row, slot_request, filled):
    slot_count = projections.shape[0]
    width = projections.shape[1] // 3
    requests, context = cache_keys.shape[0], cache_keys.shape[1]
    pair = 128
    pairs = width // pair
    keys = cache_keys.reshape(requests * context, width)
    values = cache_values.reshape(requests * context, width)
    key_owner = jnp.arange(requests * context, dtype=jnp.int32) // context
    key_place = jnp.arange(requests * context, dtype=jnp.int32) % context
    key_limit = jnp.repeat(lengths, context)
    column_tag = jnp.where(key_place < key_limit, key_owner, -1).reshape(1, -1)
    new_tag = jnp.where(filled > 0, slot_request, -1).reshape(1, -1)
    new_row = global_row.reshape(1, -1)
    row_request = slot_request.reshape(-1, 1)
    row_index = global_row.reshape(-1, 1)
    row_filled = filled.reshape(-1, 1)
    keyed = requests * context
    whole = lambda shape: pl.BlockSpec(shape, lambda p: (0, 0))
    return pl.pallas_call(
        attention_kernel,
        grid=(pairs,),
        in_specs=[
            pl.BlockSpec((slot_count, pair), lambda p: (0, p)),
            pl.BlockSpec((slot_count, pair), lambda p: (0, pairs + p)),
            pl.BlockSpec((slot_count, pair), lambda p: (0, 2 * pairs + p)),
            pl.BlockSpec((keyed, pair), lambda p: (0, p)),
            pl.BlockSpec((keyed, pair), lambda p: (0, p)),
            whole((slot_count, 1)),
            whole((slot_count, 1)),
            whole((slot_count, 1)),
            whole((1, keyed)),
            whole((1, slot_count)),
            whole((1, slot_count)),
        ],
        out_specs=pl.BlockSpec((slot_count, pair), lambda p: (0, p)),
        out_shape=jax.ShapeDtypeStruct((slot_count, width), jnp.bfloat16),
        compiler_params=pltpu.CompilerParams(vmem_limit_bytes=48 * 1024 * 1024),
    )(
        projections,
        projections,
        projections,
        keys,
        values,
        row_request,
        row_index,
        row_filled,
        column_tag,
        new_tag,
        new_row,
    )


def scatter_kernel(part_ref, o_ref, pair_buf, send_buf, ring_buf, pair_send, pair_recv, ring_send, ring_recv):
    req = lax.axis_index("req")
    me = lax.axis_index("mlp")
    chips = lax.axis_size("mlp") // 2
    chip, core = me // 2, lax.rem(me, 2)
    partner = chip * 2 + 1 - core
    step = 1 - 2 * core
    ahead = lax.rem(chip + step + chips, chips)
    behind = lax.rem(chip - step + chips, chips)
    across = lax.rem(chip + 2, chips)
    rows = o_ref.shape[0]
    barrier = pltpu.get_barrier_semaphore()
    pl.semaphore_signal(barrier, 1, device_id=(req, partner), device_id_type=pl.DeviceIdType.MESH)
    pl.semaphore_signal(barrier, 1, device_id=(req, ahead * 2 + core), device_id_type=pl.DeviceIdType.MESH)
    pl.semaphore_signal(barrier, 1, device_id=(req, behind * 2 + core), device_id_type=pl.DeviceIdType.MESH)
    pl.semaphore_wait(barrier, 3)

    def pair_copy(z):
        block = z * 2 + 1 - core
        return pltpu.make_async_remote_copy(
            src_ref=part_ref.at[pl.ds(pl.multiple_of(block * rows, rows), rows)],
            dst_ref=pair_buf.at[z],
            send_sem=pair_send.at[z],
            recv_sem=pair_recv.at[z],
            device_id=(req, partner),
            device_id_type=pl.DeviceIdType.MESH,
        )

    for z in range(chips):
        pair_copy(z).start()
    for z in range(chips):
        pair_copy(z).wait()

    def summed(z):
        mine = part_ref[pl.ds(pl.multiple_of((z * 2 + core) * rows, rows), rows), :]
        return mine.astype(jnp.float32) + pair_buf[z].astype(jnp.float32)

    def ring_copy(kind, target):
        return pltpu.make_async_remote_copy(
            src_ref=send_buf.at[kind],
            dst_ref=ring_buf.at[kind],
            send_sem=ring_send.at[kind],
            recv_sem=ring_recv.at[kind],
            device_id=(req, target * 2 + core),
            device_id_type=pl.DeviceIdType.MESH,
        )

    send_buf[1] = summed(across).astype(send_buf.dtype)
    ring_copy(1, ahead).start()
    send_buf[0] = summed(behind).astype(send_buf.dtype)
    ring_copy(0, behind).start()
    ring_copy(1, ahead).wait_recv()
    send_buf[2] = (summed(ahead) + ring_buf[1].astype(jnp.float32)).astype(send_buf.dtype)
    ring_copy(2, ahead).start()
    total = summed(chip)
    ring_copy(0, behind).wait()
    total = total + ring_buf[0].astype(jnp.float32)
    ring_copy(1, ahead).wait_send()
    ring_copy(2, ahead).wait()
    o_ref[...] = total + ring_buf[2].astype(jnp.float32)


def scatter_sum(partial):
    groups = lax.axis_size("mlp")
    chips = groups // 2
    rows = partial.shape[0] // groups
    width = partial.shape[1]
    return pl.pallas_call(
        scatter_kernel,
        in_specs=[pl.BlockSpec(memory_space=pltpu.VMEM)],
        out_specs=pl.BlockSpec(memory_space=pltpu.VMEM),
        out_shape=jax.ShapeDtypeStruct((rows, width), jnp.float32),
        scratch_shapes=[
            pltpu.VMEM((chips, rows, width), partial.dtype),
            pltpu.VMEM((3, rows, width), partial.dtype),
            pltpu.VMEM((3, rows, width), partial.dtype),
            pltpu.SemaphoreType.DMA((chips,)),
            pltpu.SemaphoreType.DMA((chips,)),
            pltpu.SemaphoreType.DMA((3,)),
            pltpu.SemaphoreType.DMA((3,)),
        ],
        compiler_params=pltpu.CompilerParams(
            collective_id=1, has_side_effects=True, vmem_limit_bytes=48 * 1024 * 1024
        ),
    )(partial)


def gather_kernel(
    x_ref, w1_ref, w2_ref, o_ref, held, ring_send, ring_recv, pair_send, pair_recv
):
    req = lax.axis_index("req")
    me = lax.axis_index("mlp")
    chips = lax.axis_size("mlp") // 2
    chip, core = me // 2, lax.rem(me, 2)
    partner = chip * 2 + 1 - core
    step = 1 - 2 * core
    ahead = lax.rem(chip + step + chips, chips)
    behind = lax.rem(chip - step + chips, chips)
    across = lax.rem(chip + 2, chips)
    rows = x_ref.shape[0]
    barrier = pltpu.get_barrier_semaphore()
    pl.semaphore_signal(barrier, 1, device_id=(req, partner), device_id_type=pl.DeviceIdType.MESH)
    pl.semaphore_signal(barrier, 1, device_id=(req, ahead * 2 + core), device_id_type=pl.DeviceIdType.MESH)
    pl.semaphore_signal(barrier, 1, device_id=(req, behind * 2 + core), device_id_type=pl.DeviceIdType.MESH)
    pl.semaphore_wait(barrier, 3)

    def block_rows(z, which):
        return pl.ds(pl.multiple_of((z * 2 + which) * rows, rows), rows)

    origins = (chip, behind, ahead, across)

    def ring_copy(kind):
        source = x_ref if kind < 2 else held.at[block_rows(behind, core)]
        origin = chip if kind < 2 else behind
        target = ahead if kind != 1 else behind
        return pltpu.make_async_remote_copy(
            src_ref=source,
            dst_ref=held.at[block_rows(origin, core)],
            send_sem=ring_send.at[kind],
            recv_sem=ring_recv.at[kind],
            device_id=(req, target * 2 + core),
            device_id_type=pl.DeviceIdType.MESH,
        )

    def pair_copy(kind):
        source = x_ref if kind == 0 else held.at[block_rows(origins[kind], core)]
        return pltpu.make_async_remote_copy(
            src_ref=source,
            dst_ref=held.at[block_rows(origins[kind], core)],
            send_sem=pair_send.at[kind],
            recv_sem=pair_recv.at[kind],
            device_id=(req, partner),
            device_id_type=pl.DeviceIdType.MESH,
        )

    def feed_forward(block, place):
        hidden = jnp.dot(block, w1_ref[...], preferred_element_type=jnp.float32)
        hidden = (hidden * 0.5 * (1.0 + lax.erf(hidden * (2.0 ** -0.5)))).astype(jnp.bfloat16)
        o_ref[place, :] = jnp.dot(hidden, w2_ref[...], preferred_element_type=jnp.float32).astype(
            o_ref.dtype
        )

    ring_copy(0).start()
    ring_copy(1).start()
    pair_copy(0).start()
    feed_forward(x_ref[...], block_rows(chip, core))
    ring_copy(0).wait_recv()
    ring_copy(2).start()
    pair_copy(1).start()
    feed_forward(held[block_rows(behind, core), :], block_rows(behind, core))
    ring_copy(1).wait_recv()
    pair_copy(2).start()
    feed_forward(held[block_rows(ahead, core), :], block_rows(ahead, core))
    ring_copy(2).wait_recv()
    pair_copy(3).start()
    feed_forward(held[block_rows(across, core), :], block_rows(across, core))
    partner_origins = (chip, ahead, behind, across)
    for kind in range(4):
        copy = pair_copy(kind)
        copy.wait_recv()
        place = block_rows(partner_origins[kind], 1 - core)
        feed_forward(held[place, :], place)
    for kind in range(3):
        ring_copy(kind).wait_send()
    for kind in range(4):
        pair_copy(kind).wait_send()


def gather_rows(block, w_fc1, w_fc2):
    groups = lax.axis_size("mlp")
    chips = groups // 2
    total = groups * block.shape[0]
    return pl.pallas_call(
        gather_kernel,
        in_specs=[pl.BlockSpec(memory_space=pltpu.VMEM)] * 3,
        out_specs=pl.BlockSpec(memory_space=pltpu.VMEM),
        out_shape=jax.ShapeDtypeStruct((total, w_fc2.shape[1]), jnp.bfloat16),
        scratch_shapes=[
            pltpu.VMEM((total, block.shape[1]), block.dtype),
            pltpu.SemaphoreType.DMA((chips,)),
            pltpu.SemaphoreType.DMA((chips,)),
            pltpu.SemaphoreType.DMA((chips,)),
            pltpu.SemaphoreType.DMA((chips,)),
        ],
        compiler_params=pltpu.CompilerParams(
            collective_id=2, has_side_effects=True, vmem_limit_bytes=48 * 1024 * 1024
        ),
    )(block, w_fc1, w_fc2)


def per_device(
    tokens,
    token_owner,
    token_request,
    cache_len,
    cache_k,
    cache_v,
    w_qkv,
    w_out,
    w_fc1,
    w_fc2,
    ln1_gain,
    ln1_bias,
    ln2_gain,
    ln2_bias,
):
    n_req = lax.axis_size("req")
    n_mlp = lax.axis_size("mlp")
    devices = n_req * n_mlp
    owner_index = lax.axis_index("req") * n_mlp + lax.axis_index("mlp")
    tok_dev, width = tokens.shape
    capacity = max(2, 2 * tok_dev // devices)
    slot_count = devices * capacity
    owners_flat = token_owner.reshape(-1)
    my_owners = lax.dynamic_slice_in_dim(owners_flat, owner_index * tok_dev, tok_dev)
    owner_onehot = (my_owners[:, None] == jnp.arange(devices, dtype=jnp.int32)[None, :]).astype(
        jnp.int32
    )
    ranking = jnp.cumsum(owner_onehot, axis=0) - 1
    my_rank = jnp.sum(owner_onehot * ranking, axis=1)
    column = my_owners * capacity + my_rank
    dispatch = (column[:, None] == jnp.arange(slot_count, dtype=jnp.int32)[None, :]).astype(
        jnp.bfloat16
    )
    outgoing = jnp.einsum("tr,td->rd", dispatch, tokens, preferred_element_type=jnp.float32).astype(
        jnp.bfloat16
    )
    arrived = lax.all_to_all(
        outgoing.reshape(devices, capacity, width),
        ("req", "mlp"),
        split_axis=0,
        concat_axis=0,
        tiled=True,
    )
    projections = jnp.dot(
        arrived.reshape(slot_count, width), w_qkv, preferred_element_type=jnp.float32
    ).astype(jnp.bfloat16)
    global_row, slot_request, filled = slot_table(
        owners_flat, token_request, owner_index, devices, tok_dev, capacity
    )
    attended = attend(projections, cache_k, cache_v, cache_len, global_row, slot_request, filled)
    returned = lax.all_to_all(
        attended.reshape(devices, capacity, width),
        ("req", "mlp"),
        split_axis=0,
        concat_axis=0,
        tiled=True,
    )
    attn_rows = jnp.dot(
        dispatch, returned.reshape(slot_count, width), preferred_element_type=jnp.float32
    ).astype(jnp.bfloat16)
    projected_out = jnp.dot(attn_rows, w_out, preferred_element_type=jnp.float32)
    normed = layer_norm(projected_out + tokens.astype(jnp.float32), ln1_gain, ln1_bias).astype(
        jnp.bfloat16
    )
    summed = scatter_sum(gather_rows(normed, w_fc1, w_fc2))
    return layer_norm(normed.astype(jnp.float32) + summed, ln2_gain, ln2_bias).astype(jnp.bfloat16)


def solution(mesh):
    placed = (
        P(("req", "mlp"), None),
        P(),
        P(),
        P(("req", "mlp")),
        P(("req", "mlp"), None, None),
        P(("req", "mlp"), None, None),
        P(),
        P(),
        P(None, "mlp"),
        P("mlp", None),
        P(),
        P(),
        P(),
        P(),
    )
    return jax.shard_map(
        per_device, mesh=mesh, in_specs=placed, out_specs=P(("req", "mlp"), None), check_vma=False
    )
```

```python
import jax
import jax.numpy as jnp
from jax import lax
from jax.sharding import PartitionSpec as P
from jax.experimental import pallas as pl
from jax.experimental.pallas import tpu as pltpu

HEADS = 16


epsilon = 1e-05


def layer_norm(values, gain, shift):
    center = values - jnp.mean(values, axis=-1, keepdims=True)
    spread = jnp.mean(center * center, axis=-1, keepdims=True)
    return center * lax.rsqrt(spread + epsilon) * gain + shift


def slot_table(owners_flat, requests_flat, owner_index, devices, tok_dev, capacity):
    owners = owners_flat.reshape(devices, tok_dev)
    requests = requests_flat.reshape(devices, tok_dev)
    mine_mask = (owners == owner_index).astype(jnp.int32)
    ranking = jnp.cumsum(mine_mask, axis=1) - 1
    places = jnp.arange(capacity, dtype=jnp.int32)
    hit_table = mine_mask[:, :, None] * (ranking[:, :, None] == places[None, None, :]).astype(
        jnp.int32
    )
    filled = jnp.sum(hit_table, axis=1)
    positions = jnp.arange(tok_dev, dtype=jnp.int32)
    local_row = jnp.sum(hit_table * positions[None, :, None], axis=1)
    sources = jnp.arange(devices, dtype=jnp.int32)[:, None]
    global_row = jnp.where(filled > 0, sources * tok_dev + local_row, -1).reshape(-1)
    slot_request = jnp.sum(hit_table * requests[:, :, None], axis=1).reshape(-1)
    return (global_row, slot_request, filled.reshape(-1))


def attention_kernel(
    q_ref, kn_ref, vn_ref, k_ref, v_ref, rreq_ref, rrow_ref, rfill_ref, ctag_ref, ntag_ref, nrow_ref, o_ref
):
    head_dim = q_ref.shape[1] // 2
    score_scale = head_dim ** (-0.5)
    q = q_ref[...] * jnp.asarray(score_scale, q_ref.dtype)
    keys = k_ref[...]
    values = v_ref[...]
    key_new = kn_ref[...]
    value_new = vn_ref[...]
    row_request = rreq_ref[...]
    old_mask = ctag_ref[...] == row_request
    new_mask = (ntag_ref[...] == row_request) & (nrow_ref[...] <= rrow_ref[...])
    lane = lax.broadcasted_iota(jnp.int32, (1, q.shape[1]), 1)
    contract = (((1,), (1,)), ((), ()))
    result = None
    for half in range(2):
        in_head = (lane // head_dim) == half
        q_head = jnp.where(in_head, q, jnp.zeros_like(q))
        old_score = lax.dot_general(q_head, keys, contract, preferred_element_type=jnp.float32)
        new_score = lax.dot_general(q_head, key_new, contract, preferred_element_type=jnp.float32)
        old_exp = jnp.where(old_mask, jnp.exp(old_score), jnp.float32(0.0))
        new_exp = jnp.where(new_mask, jnp.exp(new_score), jnp.float32(0.0))
        total = jnp.sum(old_exp, axis=1, keepdims=True) + jnp.sum(new_exp, axis=1, keepdims=True)
        total = jnp.where(total > 0, total, jnp.float32(1.0))
        inverse = 1.0 / total
        old_weight = (old_exp * inverse).astype(jnp.bfloat16)
        new_weight = (new_exp * inverse).astype(jnp.bfloat16)
        part = jnp.dot(old_weight, values, preferred_element_type=jnp.float32) + jnp.dot(
            new_weight, value_new, preferred_element_type=jnp.float32
        )
        result = part if result is None else jnp.where(in_head, part, result)
    result = jnp.where(rfill_ref[...] > 0, result, jnp.float32(0.0))
    o_ref[...] = result.astype(o_ref.dtype)


def attend(projections, cache_keys, cache_values, lengths, global_row, slot_request, filled):
    slot_count = projections.shape[0]
    width = projections.shape[1] // 3
    requests, context = cache_keys.shape[0], cache_keys.shape[1]
    pair = 128
    pairs = width // pair
    keys = cache_keys.reshape(requests * context, width)
    values = cache_values.reshape(requests * context, width)
    key_owner = jnp.arange(requests * context, dtype=jnp.int32) // context
    key_place = jnp.arange(requests * context, dtype=jnp.int32) % context
    key_limit = jnp.repeat(lengths, context)
    column_tag = jnp.where(key_place < key_limit, key_owner, -1).reshape(1, -1)
    new_tag = jnp.where(filled > 0, slot_request, -1).reshape(1, -1)
    new_row = global_row.reshape(1, -1)
    row_request = slot_request.reshape(-1, 1)
    row_index = global_row.reshape(-1, 1)
    row_filled = filled.reshape(-1, 1)
    keyed = requests * context
    whole = lambda shape: pl.BlockSpec(shape, lambda p: (0, 0))
    return pl.pallas_call(
        attention_kernel,
        grid=(pairs,),
        in_specs=[
            pl.BlockSpec((slot_count, pair), lambda p: (0, p)),
            pl.BlockSpec((slot_count, pair), lambda p: (0, pairs + p)),
            pl.BlockSpec((slot_count, pair), lambda p: (0, 2 * pairs + p)),
            pl.BlockSpec((keyed, pair), lambda p: (0, p)),
            pl.BlockSpec((keyed, pair), lambda p: (0, p)),
            whole((slot_count, 1)),
            whole((slot_count, 1)),
            whole((slot_count, 1)),
            whole((1, keyed)),
            whole((1, slot_count)),
            whole((1, slot_count)),
        ],
        out_specs=pl.BlockSpec((slot_count, pair), lambda p: (0, p)),
        out_shape=jax.ShapeDtypeStruct((slot_count, width), jnp.bfloat16),
        compiler_params=pltpu.CompilerParams(vmem_limit_bytes=48 * 1024 * 1024),
    )(
        projections,
        projections,
        projections,
        keys,
        values,
        row_request,
        row_index,
        row_filled,
        column_tag,
        new_tag,
        new_row,
    )


def block_kernel(
    x_ref, w1_ref, w2_ref, o_ref, held, parts, pair_buf, send_buf, ring_buf,
    ring_send, ring_recv, pair_send, pair_recv, back_send, back_recv, sum_send, sum_recv,
):
    req = lax.axis_index("req")
    me = lax.axis_index("mlp")
    chips = lax.axis_size("mlp") // 2
    chip, core = me // 2, lax.rem(me, 2)
    partner = chip * 2 + 1 - core
    step = 1 - 2 * core
    ahead = lax.rem(chip + step + chips, chips)
    behind = lax.rem(chip - step + chips, chips)
    across = lax.rem(chip + 2, chips)
    rows = x_ref.shape[0]
    barrier = pltpu.get_barrier_semaphore()
    pl.semaphore_signal(barrier, 1, device_id=(req, partner), device_id_type=pl.DeviceIdType.MESH)
    pl.semaphore_signal(barrier, 1, device_id=(req, ahead * 2 + core), device_id_type=pl.DeviceIdType.MESH)
    pl.semaphore_signal(barrier, 1, device_id=(req, behind * 2 + core), device_id_type=pl.DeviceIdType.MESH)
    pl.semaphore_wait(barrier, 3)

    def block_rows(z, which):
        return pl.ds(pl.multiple_of((z * 2 + which) * rows, rows), rows)

    origins = (chip, behind, ahead, across)

    def ring_copy(kind):
        source = x_ref if kind < 2 else held.at[block_rows(behind, core)]
        origin = chip if kind < 2 else behind
        target = ahead if kind != 1 else behind
        return pltpu.make_async_remote_copy(
            src_ref=source,
            dst_ref=held.at[block_rows(origin, core)],
            send_sem=ring_send.at[kind],
            recv_sem=ring_recv.at[kind],
            device_id=(req, target * 2 + core),
            device_id_type=pl.DeviceIdType.MESH,
        )

    def pair_copy(kind):
        source = x_ref if kind == 0 else held.at[block_rows(origins[kind], core)]
        return pltpu.make_async_remote_copy(
            src_ref=source,
            dst_ref=held.at[block_rows(origins[kind], core)],
            send_sem=pair_send.at[kind],
            recv_sem=pair_recv.at[kind],
            device_id=(req, partner),
            device_id_type=pl.DeviceIdType.MESH,
        )

    def back_copy(z):
        return pltpu.make_async_remote_copy(
            src_ref=parts.at[block_rows(z, 1 - core)],
            dst_ref=pair_buf.at[z],
            send_sem=back_send.at[z],
            recv_sem=back_recv.at[z],
            device_id=(req, partner),
            device_id_type=pl.DeviceIdType.MESH,
        )

    def feed_forward(block, place):
        hidden = jnp.dot(block, w1_ref[...], preferred_element_type=jnp.float32)
        hidden = (hidden * 0.5 * (1.0 + lax.erf(hidden * (2.0 ** -0.5)))).astype(jnp.bfloat16)
        parts[place, :] = jnp.dot(hidden, w2_ref[...], preferred_element_type=jnp.float32).astype(
            parts.dtype
        )

    ring_copy(0).start()
    ring_copy(1).start()
    pair_copy(0).start()
    feed_forward(x_ref[...], block_rows(chip, core))
    ring_copy(0).wait_recv()
    ring_copy(2).start()
    pair_copy(1).start()
    feed_forward(held[block_rows(behind, core), :], block_rows(behind, core))
    ring_copy(1).wait_recv()
    pair_copy(2).start()
    feed_forward(held[block_rows(ahead, core), :], block_rows(ahead, core))
    ring_copy(2).wait_recv()
    pair_copy(3).start()
    feed_forward(held[block_rows(across, core), :], block_rows(across, core))
    partner_origins = (chip, ahead, behind, across)
    for kind in range(4):
        pair_copy(kind).wait_recv()
        place = block_rows(partner_origins[kind], 1 - core)
        feed_forward(held[place, :], place)
        back_copy(partner_origins[kind]).start()
    for kind in range(3):
        ring_copy(kind).wait_send()
    for kind in range(4):
        pair_copy(kind).wait_send()
    for z in range(chips):
        back_copy(z).wait()

    def summed(z):
        mine = parts[block_rows(z, core), :]
        return mine.astype(jnp.float32) + pair_buf[z].astype(jnp.float32)

    def sum_copy(kind, target):
        return pltpu.make_async_remote_copy(
            src_ref=send_buf.at[kind],
            dst_ref=ring_buf.at[kind],
            send_sem=sum_send.at[kind],
            recv_sem=sum_recv.at[kind],
            device_id=(req, target * 2 + core),
            device_id_type=pl.DeviceIdType.MESH,
        )

    send_buf[1] = summed(across).astype(send_buf.dtype)
    sum_copy(1, ahead).start()
    send_buf[0] = summed(behind).astype(send_buf.dtype)
    sum_copy(0, behind).start()
    sum_copy(1, ahead).wait_recv()
    send_buf[2] = (summed(ahead) + ring_buf[1].astype(jnp.float32)).astype(send_buf.dtype)
    sum_copy(2, ahead).start()
    total = summed(chip)
    sum_copy(0, behind).wait()
    total = total + ring_buf[0].astype(jnp.float32)
    sum_copy(1, ahead).wait_send()
    sum_copy(2, ahead).wait()
    o_ref[...] = total + ring_buf[2].astype(jnp.float32)


def feed_forward_block(block, w_fc1, w_fc2):
    groups = lax.axis_size("mlp")
    chips = groups // 2
    rows, width = block.shape
    total = groups * rows
    out_width = w_fc2.shape[1]
    return pl.pallas_call(
        block_kernel,
        in_specs=[pl.BlockSpec(memory_space=pltpu.VMEM)] * 3,
        out_specs=pl.BlockSpec(memory_space=pltpu.VMEM),
        out_shape=jax.ShapeDtypeStruct((rows, out_width), jnp.float32),
        scratch_shapes=[
            pltpu.VMEM((total, width), block.dtype),
            pltpu.VMEM((total, out_width), jnp.bfloat16),
            pltpu.VMEM((chips, rows, out_width), jnp.bfloat16),
            pltpu.VMEM((3, rows, out_width), jnp.bfloat16),
            pltpu.VMEM((3, rows, out_width), jnp.bfloat16),
            pltpu.SemaphoreType.DMA((3,)),
            pltpu.SemaphoreType.DMA((3,)),
            pltpu.SemaphoreType.DMA((chips,)),
            pltpu.SemaphoreType.DMA((chips,)),
            pltpu.SemaphoreType.DMA((chips,)),
            pltpu.SemaphoreType.DMA((chips,)),
            pltpu.SemaphoreType.DMA((3,)),
            pltpu.SemaphoreType.DMA((3,)),
        ],
        compiler_params=pltpu.CompilerParams(
            collective_id=2, has_side_effects=True, vmem_limit_bytes=48 * 1024 * 1024
        ),
    )(block, w_fc1, w_fc2)


def per_device(
    tokens,
    token_owner,
    token_request,
    cache_len,
    cache_k,
    cache_v,
    w_qkv,
    w_out,
    w_fc1,
    w_fc2,
    ln1_gain,
    ln1_bias,
    ln2_gain,
    ln2_bias,
):
    n_req = lax.axis_size("req")
    n_mlp = lax.axis_size("mlp")
    devices = n_req * n_mlp
    owner_index = lax.axis_index("req") * n_mlp + lax.axis_index("mlp")
    tok_dev, width = tokens.shape
    capacity = max(2, 2 * tok_dev // devices)
    slot_count = devices * capacity
    owners_flat = token_owner.reshape(-1)
    my_owners = lax.dynamic_slice_in_dim(owners_flat, owner_index * tok_dev, tok_dev)
    owner_onehot = (my_owners[:, None] == jnp.arange(devices, dtype=jnp.int32)[None, :]).astype(
        jnp.int32
    )
    ranking = jnp.cumsum(owner_onehot, axis=0) - 1
    my_rank = jnp.sum(owner_onehot * ranking, axis=1)
    column = my_owners * capacity + my_rank
    dispatch = (column[:, None] == jnp.arange(slot_count, dtype=jnp.int32)[None, :]).astype(
        jnp.bfloat16
    )
    outgoing = jnp.einsum("tr,td->rd", dispatch, tokens, preferred_element_type=jnp.float32).astype(
        jnp.bfloat16
    )
    arrived = lax.all_to_all(
        outgoing.reshape(devices, capacity, width),
        ("req", "mlp"),
        split_axis=0,
        concat_axis=0,
        tiled=True,
    )
    projections = jnp.dot(
        arrived.reshape(slot_count, width), w_qkv, preferred_element_type=jnp.float32
    ).astype(jnp.bfloat16)
    global_row, slot_request, filled = slot_table(
        owners_flat, token_request, owner_index, devices, tok_dev, capacity
    )
    attended = attend(projections, cache_k, cache_v, cache_len, global_row, slot_request, filled)
    returned = lax.all_to_all(
        attended.reshape(devices, capacity, width),
        ("req", "mlp"),
        split_axis=0,
        concat_axis=0,
        tiled=True,
    )
    attn_rows = jnp.dot(
        dispatch, returned.reshape(slot_count, width), preferred_element_type=jnp.float32
    ).astype(jnp.bfloat16)
    projected_out = jnp.dot(attn_rows, w_out, preferred_element_type=jnp.float32)
    normed = layer_norm(projected_out + tokens.astype(jnp.float32), ln1_gain, ln1_bias).astype(
        jnp.bfloat16
    )
    summed = feed_forward_block(normed, w_fc1, w_fc2)
    return layer_norm(normed.astype(jnp.float32) + summed, ln2_gain, ln2_bias).astype(jnp.bfloat16)


def solution(mesh):
    placed = (
        P(("req", "mlp"), None),
        P(),
        P(),
        P(("req", "mlp")),
        P(("req", "mlp"), None, None),
        P(("req", "mlp"), None, None),
        P(),
        P(),
        P(None, "mlp"),
        P("mlp", None),
        P(),
        P(),
        P(),
        P(),
    )
    return jax.shard_map(
        per_device, mesh=mesh, in_specs=placed, out_specs=P(("req", "mlp"), None), check_vma=False
    )
```

```python
import jax
import jax.numpy as jnp
from jax import lax
from jax.sharding import PartitionSpec as P
from jax.experimental import pallas as pl
from jax.experimental.pallas import tpu as pltpu

HEADS = 16


epsilon = 1e-05


def layer_norm(values, gain, shift):
    center = values - jnp.mean(values, axis=-1, keepdims=True)
    spread = jnp.mean(center * center, axis=-1, keepdims=True)
    return center * lax.rsqrt(spread + epsilon) * gain + shift


def slot_table(owners_flat, requests_flat, owner_index, devices, tok_dev, capacity):
    owners = owners_flat.reshape(devices, tok_dev)
    requests = requests_flat.reshape(devices, tok_dev)
    mine_mask = (owners == owner_index).astype(jnp.int32)
    ranking = jnp.cumsum(mine_mask, axis=1) - 1
    places = jnp.arange(capacity, dtype=jnp.int32)
    hit_table = mine_mask[:, :, None] * (ranking[:, :, None] == places[None, None, :]).astype(
        jnp.int32
    )
    filled = jnp.sum(hit_table, axis=1)
    positions = jnp.arange(tok_dev, dtype=jnp.int32)
    local_row = jnp.sum(hit_table * positions[None, :, None], axis=1)
    sources = jnp.arange(devices, dtype=jnp.int32)[:, None]
    global_row = jnp.where(filled > 0, sources * tok_dev + local_row, -1).reshape(-1)
    slot_request = jnp.sum(hit_table * requests[:, :, None], axis=1).reshape(-1)
    return (global_row, slot_request, filled.reshape(-1))


def attention_kernel(
    q_ref, kn_ref, vn_ref, k_ref, v_ref, rreq_ref, rrow_ref, rfill_ref, ctag_ref, ntag_ref, nrow_ref, o_ref
):
    head_dim = q_ref.shape[1] // 2
    score_scale = head_dim ** (-0.5)
    q = q_ref[...] * jnp.asarray(score_scale, q_ref.dtype)
    keys = k_ref[...]
    values = v_ref[...]
    key_new = kn_ref[...]
    value_new = vn_ref[...]
    row_request = rreq_ref[...]
    old_mask = ctag_ref[...] == row_request
    new_mask = (ntag_ref[...] == row_request) & (nrow_ref[...] <= rrow_ref[...])
    lane = lax.broadcasted_iota(jnp.int32, (1, q.shape[1]), 1)
    contract = (((1,), (1,)), ((), ()))
    result = None
    for half in range(2):
        in_head = (lane // head_dim) == half
        q_head = jnp.where(in_head, q, jnp.zeros_like(q))
        old_score = lax.dot_general(q_head, keys, contract, preferred_element_type=jnp.float32)
        new_score = lax.dot_general(q_head, key_new, contract, preferred_element_type=jnp.float32)
        old_exp = jnp.where(old_mask, jnp.exp(old_score), jnp.float32(0.0))
        new_exp = jnp.where(new_mask, jnp.exp(new_score), jnp.float32(0.0))
        total = jnp.sum(old_exp, axis=1, keepdims=True) + jnp.sum(new_exp, axis=1, keepdims=True)
        total = jnp.where(total > 0, total, jnp.float32(1.0))
        inverse = 1.0 / total
        old_weight = (old_exp * inverse).astype(jnp.bfloat16)
        new_weight = (new_exp * inverse).astype(jnp.bfloat16)
        part = jnp.dot(old_weight, values, preferred_element_type=jnp.float32) + jnp.dot(
            new_weight, value_new, preferred_element_type=jnp.float32
        )
        result = part if result is None else jnp.where(in_head, part, result)
    result = jnp.where(rfill_ref[...] > 0, result, jnp.float32(0.0))
    o_ref[...] = result.astype(o_ref.dtype)


def attend(projections, cache_keys, cache_values, lengths, global_row, slot_request, filled):
    slot_count = projections.shape[0]
    width = projections.shape[1] // 3
    requests, context = cache_keys.shape[0], cache_keys.shape[1]
    pair = 128
    pairs = width // pair
    keys = cache_keys.reshape(requests * context, width)
    values = cache_values.reshape(requests * context, width)
    key_owner = jnp.arange(requests * context, dtype=jnp.int32) // context
    key_place = jnp.arange(requests * context, dtype=jnp.int32) % context
    key_limit = jnp.repeat(lengths, context)
    column_tag = jnp.where(key_place < key_limit, key_owner, -1).reshape(1, -1)
    new_tag = jnp.where(filled > 0, slot_request, -1).reshape(1, -1)
    new_row = global_row.reshape(1, -1)
    row_request = slot_request.reshape(-1, 1)
    row_index = global_row.reshape(-1, 1)
    row_filled = filled.reshape(-1, 1)
    keyed = requests * context
    whole = lambda shape: pl.BlockSpec(shape, lambda p: (0, 0))
    return pl.pallas_call(
        attention_kernel,
        grid=(pairs,),
        in_specs=[
            pl.BlockSpec((slot_count, pair), lambda p: (0, p)),
            pl.BlockSpec((slot_count, pair), lambda p: (0, pairs + p)),
            pl.BlockSpec((slot_count, pair), lambda p: (0, 2 * pairs + p)),
            pl.BlockSpec((keyed, pair), lambda p: (0, p)),
            pl.BlockSpec((keyed, pair), lambda p: (0, p)),
            whole((slot_count, 1)),
            whole((slot_count, 1)),
            whole((slot_count, 1)),
            whole((1, keyed)),
            whole((1, slot_count)),
            whole((1, slot_count)),
        ],
        out_specs=pl.BlockSpec((slot_count, pair), lambda p: (0, p)),
        out_shape=jax.ShapeDtypeStruct((slot_count, width), jnp.bfloat16),
        compiler_params=pltpu.CompilerParams(vmem_limit_bytes=48 * 1024 * 1024),
    )(
        projections,
        projections,
        projections,
        keys,
        values,
        row_request,
        row_index,
        row_filled,
        column_tag,
        new_tag,
        new_row,
    )


def block_kernel(
    x_ref, w1_ref, w2_ref, o_ref, held, parts, pair_buf, send_buf, ring_buf,
    ring_send, ring_recv, pair_send, pair_recv, back_send, back_recv, sum_send, sum_recv,
):
    req = lax.axis_index("req")
    me = lax.axis_index("mlp")
    chips = lax.axis_size("mlp") // 2
    chip, core = me // 2, lax.rem(me, 2)
    partner = chip * 2 + 1 - core
    step = 1 - 2 * core
    ahead = lax.rem(chip + step + chips, chips)
    behind = lax.rem(chip - step + chips, chips)
    across = lax.rem(chip + 2, chips)
    rows = x_ref.shape[0]
    barrier = pltpu.get_barrier_semaphore()
    pl.semaphore_signal(barrier, 1, device_id=(req, partner), device_id_type=pl.DeviceIdType.MESH)
    pl.semaphore_signal(barrier, 1, device_id=(req, ahead * 2 + core), device_id_type=pl.DeviceIdType.MESH)
    pl.semaphore_signal(barrier, 1, device_id=(req, behind * 2 + core), device_id_type=pl.DeviceIdType.MESH)
    pl.semaphore_wait(barrier, 3)

    def block_rows(z, which):
        return pl.ds(pl.multiple_of((z * 2 + which) * rows, rows), rows)

    origins = (chip, behind, ahead, across)

    def ring_copy(kind):
        source = x_ref if kind < 2 else held.at[block_rows(behind, core)]
        origin = chip if kind < 2 else behind
        target = ahead if kind != 1 else behind
        return pltpu.make_async_remote_copy(
            src_ref=source,
            dst_ref=held.at[block_rows(origin, core)],
            send_sem=ring_send.at[kind],
            recv_sem=ring_recv.at[kind],
            device_id=(req, target * 2 + core),
            device_id_type=pl.DeviceIdType.MESH,
        )

    def pair_copy(kind):
        source = x_ref if kind == 0 else held.at[block_rows(origins[kind], core)]
        return pltpu.make_async_remote_copy(
            src_ref=source,
            dst_ref=held.at[block_rows(origins[kind], core)],
            send_sem=pair_send.at[kind],
            recv_sem=pair_recv.at[kind],
            device_id=(req, partner),
            device_id_type=pl.DeviceIdType.MESH,
        )

    def back_copy(z):
        return pltpu.make_async_remote_copy(
            src_ref=parts.at[block_rows(z, 1 - core)],
            dst_ref=pair_buf.at[z],
            send_sem=back_send.at[z],
            recv_sem=back_recv.at[z],
            device_id=(req, partner),
            device_id_type=pl.DeviceIdType.MESH,
        )

    def feed_forward(block, place):
        hidden = jnp.dot(block, w1_ref[...], preferred_element_type=jnp.float32)
        hidden = (hidden * 0.5 * (1.0 + lax.erf(hidden * (2.0 ** -0.5)))).astype(jnp.bfloat16)
        parts[place, :] = jnp.dot(hidden, w2_ref[...], preferred_element_type=jnp.float32).astype(
            parts.dtype
        )

    ring_copy(0).start()
    ring_copy(1).start()
    pair_copy(0).start()
    feed_forward(x_ref[...], block_rows(chip, core))
    ring_copy(0).wait_recv()
    ring_copy(2).start()
    pair_copy(1).start()
    feed_forward(held[block_rows(behind, core), :], block_rows(behind, core))
    ring_copy(1).wait_recv()
    pair_copy(2).start()
    feed_forward(held[block_rows(ahead, core), :], block_rows(ahead, core))
    ring_copy(2).wait_recv()
    pair_copy(3).start()
    feed_forward(held[block_rows(across, core), :], block_rows(across, core))
    partner_origins = (chip, ahead, behind, across)
    for kind in range(4):
        pair_copy(kind).wait_recv()
        place = block_rows(partner_origins[kind], 1 - core)
        feed_forward(held[place, :], place)
        back_copy(partner_origins[kind]).start()
    for kind in range(3):
        ring_copy(kind).wait_send()
    for kind in range(4):
        pair_copy(kind).wait_send()

    def summed(z):
        mine = parts[block_rows(z, core), :]
        return mine.astype(jnp.float32) + pair_buf[z].astype(jnp.float32)

    def sum_copy(kind, target):
        return pltpu.make_async_remote_copy(
            src_ref=send_buf.at[kind],
            dst_ref=ring_buf.at[kind],
            send_sem=sum_send.at[kind],
            recv_sem=sum_recv.at[kind],
            device_id=(req, target * 2 + core),
            device_id_type=pl.DeviceIdType.MESH,
        )

    back_copy(behind).wait_recv()
    send_buf[0] = summed(behind).astype(send_buf.dtype)
    sum_copy(0, behind).start()
    back_copy(across).wait_recv()
    send_buf[1] = summed(across).astype(send_buf.dtype)
    sum_copy(1, ahead).start()
    back_copy(ahead).wait_recv()
    sum_copy(1, ahead).wait_recv()
    send_buf[2] = (summed(ahead) + ring_buf[1].astype(jnp.float32)).astype(send_buf.dtype)
    sum_copy(2, ahead).start()
    back_copy(chip).wait_recv()
    total = summed(chip)
    for z in range(chips):
        back_copy(z).wait_send()
    sum_copy(0, behind).wait()
    total = total + ring_buf[0].astype(jnp.float32)
    sum_copy(1, ahead).wait_send()
    sum_copy(2, ahead).wait()
    o_ref[...] = total + ring_buf[2].astype(jnp.float32)


def feed_forward_block(block, w_fc1, w_fc2):
    groups = lax.axis_size("mlp")
    chips = groups // 2
    rows, width = block.shape
    total = groups * rows
    out_width = w_fc2.shape[1]
    return pl.pallas_call(
        block_kernel,
        in_specs=[pl.BlockSpec(memory_space=pltpu.VMEM)] * 3,
        out_specs=pl.BlockSpec(memory_space=pltpu.VMEM),
        out_shape=jax.ShapeDtypeStruct((rows, out_width), jnp.float32),
        scratch_shapes=[
            pltpu.VMEM((total, width), block.dtype),
            pltpu.VMEM((total, out_width), jnp.bfloat16),
            pltpu.VMEM((chips, rows, out_width), jnp.bfloat16),
            pltpu.VMEM((3, rows, out_width), jnp.bfloat16),
            pltpu.VMEM((3, rows, out_width), jnp.bfloat16),
            pltpu.SemaphoreType.DMA((3,)),
            pltpu.SemaphoreType.DMA((3,)),
            pltpu.SemaphoreType.DMA((chips,)),
            pltpu.SemaphoreType.DMA((chips,)),
            pltpu.SemaphoreType.DMA((chips,)),
            pltpu.SemaphoreType.DMA((chips,)),
            pltpu.SemaphoreType.DMA((3,)),
            pltpu.SemaphoreType.DMA((3,)),
        ],
        compiler_params=pltpu.CompilerParams(
            collective_id=2, has_side_effects=True, vmem_limit_bytes=48 * 1024 * 1024
        ),
    )(block, w_fc1, w_fc2)


def per_device(
    tokens,
    token_owner,
    token_request,
    cache_len,
    cache_k,
    cache_v,
    w_qkv,
    w_out,
    w_fc1,
    w_fc2,
    ln1_gain,
    ln1_bias,
    ln2_gain,
    ln2_bias,
):
    n_req = lax.axis_size("req")
    n_mlp = lax.axis_size("mlp")
    devices = n_req * n_mlp
    owner_index = lax.axis_index("req") * n_mlp + lax.axis_index("mlp")
    tok_dev, width = tokens.shape
    capacity = max(2, 2 * tok_dev // devices)
    slot_count = devices * capacity
    owners_flat = token_owner.reshape(-1)
    my_owners = lax.dynamic_slice_in_dim(owners_flat, owner_index * tok_dev, tok_dev)
    owner_onehot = (my_owners[:, None] == jnp.arange(devices, dtype=jnp.int32)[None, :]).astype(
        jnp.int32
    )
    ranking = jnp.cumsum(owner_onehot, axis=0) - 1
    my_rank = jnp.sum(owner_onehot * ranking, axis=1)
    column = my_owners * capacity + my_rank
    dispatch = (column[:, None] == jnp.arange(slot_count, dtype=jnp.int32)[None, :]).astype(
        jnp.bfloat16
    )
    outgoing = jnp.einsum("tr,td->rd", dispatch, tokens, preferred_element_type=jnp.float32).astype(
        jnp.bfloat16
    )
    arrived = lax.all_to_all(
        outgoing.reshape(devices, capacity, width),
        ("req", "mlp"),
        split_axis=0,
        concat_axis=0,
        tiled=True,
    )
    projections = jnp.dot(
        arrived.reshape(slot_count, width), w_qkv, preferred_element_type=jnp.float32
    ).astype(jnp.bfloat16)
    global_row, slot_request, filled = slot_table(
        owners_flat, token_request, owner_index, devices, tok_dev, capacity
    )
    attended = attend(projections, cache_k, cache_v, cache_len, global_row, slot_request, filled)
    returned = lax.all_to_all(
        attended.reshape(devices, capacity, width),
        ("req", "mlp"),
        split_axis=0,
        concat_axis=0,
        tiled=True,
    )
    attn_rows = jnp.einsum(
        "tsc,scd->td",
        dispatch.reshape(tok_dev, devices, capacity),
        returned,
        preferred_element_type=jnp.float32,
    ).astype(jnp.bfloat16)
    projected_out = jnp.dot(attn_rows, w_out, preferred_element_type=jnp.float32)
    normed = layer_norm(projected_out + tokens.astype(jnp.float32), ln1_gain, ln1_bias).astype(
        jnp.bfloat16
    )
    summed = feed_forward_block(normed, w_fc1, w_fc2)
    return layer_norm(normed.astype(jnp.float32) + summed, ln2_gain, ln2_bias).astype(jnp.bfloat16)


def solution(mesh):
    placed = (
        P(("req", "mlp"), None),
        P(),
        P(),
        P(("req", "mlp")),
        P(("req", "mlp"), None, None),
        P(("req", "mlp"), None, None),
        P(),
        P(),
        P(None, "mlp"),
        P("mlp", None),
        P(),
        P(),
        P(),
        P(),
    )
    return jax.shard_map(
        per_device, mesh=mesh, in_specs=placed, out_specs=P(("req", "mlp"), None), check_vma=False
    )
```

```python
import jax
import jax.numpy as jnp
from jax import lax
from jax.sharding import PartitionSpec as P
from jax.experimental import pallas as pl
from jax.experimental.pallas import tpu as pltpu

HEADS = 16


epsilon = 1e-05


def layer_norm(values, gain, shift):
    center = values - jnp.mean(values, axis=-1, keepdims=True)
    spread = jnp.mean(center * center, axis=-1, keepdims=True)
    return center * lax.rsqrt(spread + epsilon) * gain + shift


def slot_table(owners_flat, requests_flat, owner_index, devices, tok_dev, capacity):
    owners = owners_flat.reshape(devices, tok_dev)
    requests = requests_flat.reshape(devices, tok_dev)
    mine_mask = (owners == owner_index).astype(jnp.int32)
    ranking = jnp.cumsum(mine_mask, axis=1) - 1
    places = jnp.arange(capacity, dtype=jnp.int32)
    hit_table = mine_mask[:, :, None] * (ranking[:, :, None] == places[None, None, :]).astype(
        jnp.int32
    )
    filled = jnp.sum(hit_table, axis=1)
    positions = jnp.arange(tok_dev, dtype=jnp.int32)
    local_row = jnp.sum(hit_table * positions[None, :, None], axis=1)
    sources = jnp.arange(devices, dtype=jnp.int32)[:, None]
    global_row = jnp.where(filled > 0, sources * tok_dev + local_row, -1).reshape(-1)
    slot_request = jnp.sum(hit_table * requests[:, :, None], axis=1).reshape(-1)
    return (global_row, slot_request, filled.reshape(-1))


def attention_kernel(
    q_ref, kn_ref, vn_ref, k_ref, v_ref, rreq_ref, rrow_ref, rfill_ref, ctag_ref, ntag_ref, nrow_ref, o_ref
):
    head_dim = q_ref.shape[1] // 2
    score_scale = head_dim ** (-0.5)
    q = q_ref[...] * jnp.asarray(score_scale, q_ref.dtype)
    keys = k_ref[...]
    values = v_ref[...]
    key_new = kn_ref[...]
    value_new = vn_ref[...]
    row_request = rreq_ref[...]
    old_mask = ctag_ref[...] == row_request
    new_mask = (ntag_ref[...] == row_request) & (nrow_ref[...] <= rrow_ref[...])
    lane = lax.broadcasted_iota(jnp.int32, (1, q.shape[1]), 1)
    contract = (((1,), (1,)), ((), ()))
    result = None
    for half in range(2):
        in_head = (lane // head_dim) == half
        q_head = jnp.where(in_head, q, jnp.zeros_like(q))
        old_score = lax.dot_general(q_head, keys, contract, preferred_element_type=jnp.float32)
        new_score = lax.dot_general(q_head, key_new, contract, preferred_element_type=jnp.float32)
        old_exp = jnp.where(old_mask, jnp.exp(old_score), jnp.float32(0.0))
        new_exp = jnp.where(new_mask, jnp.exp(new_score), jnp.float32(0.0))
        total = jnp.sum(old_exp, axis=1, keepdims=True) + jnp.sum(new_exp, axis=1, keepdims=True)
        total = jnp.where(total > 0, total, jnp.float32(1.0))
        inverse = 1.0 / total
        old_weight = (old_exp * inverse).astype(jnp.bfloat16)
        new_weight = (new_exp * inverse).astype(jnp.bfloat16)
        part = jnp.dot(old_weight, values, preferred_element_type=jnp.float32) + jnp.dot(
            new_weight, value_new, preferred_element_type=jnp.float32
        )
        result = part if result is None else jnp.where(in_head, part, result)
    result = jnp.where(rfill_ref[...] > 0, result, jnp.float32(0.0))
    o_ref[...] = result.astype(o_ref.dtype)


def attend(projections, cache_keys, cache_values, lengths, global_row, slot_request, filled):
    slot_count = projections.shape[0]
    width = projections.shape[1] // 3
    requests, context = cache_keys.shape[0], cache_keys.shape[1]
    pair = 128
    pairs = width // pair
    keys = cache_keys.reshape(requests * context, width)
    values = cache_values.reshape(requests * context, width)
    key_owner = jnp.arange(requests * context, dtype=jnp.int32) // context
    key_place = jnp.arange(requests * context, dtype=jnp.int32) % context
    key_limit = jnp.repeat(lengths, context)
    column_tag = jnp.where(key_place < key_limit, key_owner, -1).reshape(1, -1)
    new_tag = jnp.where(filled > 0, slot_request, -1).reshape(1, -1)
    new_row = global_row.reshape(1, -1)
    row_request = slot_request.reshape(-1, 1)
    row_index = global_row.reshape(-1, 1)
    row_filled = filled.reshape(-1, 1)
    keyed = requests * context
    whole = lambda shape: pl.BlockSpec(shape, lambda p: (0, 0))
    return pl.pallas_call(
        attention_kernel,
        grid=(pairs,),
        in_specs=[
            pl.BlockSpec((slot_count, pair), lambda p: (0, p)),
            pl.BlockSpec((slot_count, pair), lambda p: (0, pairs + p)),
            pl.BlockSpec((slot_count, pair), lambda p: (0, 2 * pairs + p)),
            pl.BlockSpec((keyed, pair), lambda p: (0, p)),
            pl.BlockSpec((keyed, pair), lambda p: (0, p)),
            whole((slot_count, 1)),
            whole((slot_count, 1)),
            whole((slot_count, 1)),
            whole((1, keyed)),
            whole((1, slot_count)),
            whole((1, slot_count)),
        ],
        out_specs=pl.BlockSpec((slot_count, pair), lambda p: (0, p)),
        out_shape=jax.ShapeDtypeStruct((slot_count, width), jnp.bfloat16),
        compiler_params=pltpu.CompilerParams(vmem_limit_bytes=48 * 1024 * 1024),
    )(
        projections,
        projections,
        projections,
        keys,
        values,
        row_request,
        row_index,
        row_filled,
        column_tag,
        new_tag,
        new_row,
    )


def block_kernel(
    y_ref, gain_ref, shift_ref, w1_ref, w2_ref, o_ref, x_ref, held, parts, pair_buf, send_buf, ring_buf,
    ring_send, ring_recv, pair_send, pair_recv, back_send, back_recv, sum_send, sum_recv,
):
    x_ref[...] = layer_norm(y_ref[...], gain_ref[...], shift_ref[...]).astype(x_ref.dtype)
    req = lax.axis_index("req")
    me = lax.axis_index("mlp")
    chips = lax.axis_size("mlp") // 2
    chip, core = me // 2, lax.rem(me, 2)
    partner = chip * 2 + 1 - core
    step = 1 - 2 * core
    ahead = lax.rem(chip + step + chips, chips)
    behind = lax.rem(chip - step + chips, chips)
    across = lax.rem(chip + 2, chips)
    rows = x_ref.shape[0]
    barrier = pltpu.get_barrier_semaphore()
    pl.semaphore_signal(barrier, 1, device_id=(req, partner), device_id_type=pl.DeviceIdType.MESH)
    pl.semaphore_signal(barrier, 1, device_id=(req, ahead * 2 + core), device_id_type=pl.DeviceIdType.MESH)
    pl.semaphore_signal(barrier, 1, device_id=(req, behind * 2 + core), device_id_type=pl.DeviceIdType.MESH)
    pl.semaphore_wait(barrier, 3)

    def block_rows(z, which):
        return pl.ds(pl.multiple_of((z * 2 + which) * rows, rows), rows)

    origins = (chip, behind, ahead, across)

    def ring_copy(kind):
        source = x_ref if kind < 2 else held.at[block_rows(behind, core)]
        origin = chip if kind < 2 else behind
        target = ahead if kind != 1 else behind
        return pltpu.make_async_remote_copy(
            src_ref=source,
            dst_ref=held.at[block_rows(origin, core)],
            send_sem=ring_send.at[kind],
            recv_sem=ring_recv.at[kind],
            device_id=(req, target * 2 + core),
            device_id_type=pl.DeviceIdType.MESH,
        )

    def pair_copy(kind):
        source = x_ref if kind == 0 else held.at[block_rows(origins[kind], core)]
        return pltpu.make_async_remote_copy(
            src_ref=source,
            dst_ref=held.at[block_rows(origins[kind], core)],
            send_sem=pair_send.at[kind],
            recv_sem=pair_recv.at[kind],
            device_id=(req, partner),
            device_id_type=pl.DeviceIdType.MESH,
        )

    def back_copy(z):
        return pltpu.make_async_remote_copy(
            src_ref=parts.at[block_rows(z, 1 - core)],
            dst_ref=pair_buf.at[z],
            send_sem=back_send.at[z],
            recv_sem=back_recv.at[z],
            device_id=(req, partner),
            device_id_type=pl.DeviceIdType.MESH,
        )

    def feed_forward(block, place):
        hidden = jnp.dot(block, w1_ref[...], preferred_element_type=jnp.float32)
        hidden = (hidden * 0.5 * (1.0 + lax.erf(hidden * (2.0 ** -0.5)))).astype(jnp.bfloat16)
        parts[place, :] = jnp.dot(hidden, w2_ref[...], preferred_element_type=jnp.float32).astype(
            parts.dtype
        )

    ring_copy(0).start()
    ring_copy(1).start()
    pair_copy(0).start()
    feed_forward(x_ref[...], block_rows(chip, core))
    ring_copy(0).wait_recv()
    ring_copy(2).start()
    pair_copy(1).start()
    feed_forward(held[block_rows(behind, core), :], block_rows(behind, core))
    ring_copy(1).wait_recv()
    pair_copy(2).start()
    feed_forward(held[block_rows(ahead, core), :], block_rows(ahead, core))
    ring_copy(2).wait_recv()
    pair_copy(3).start()
    feed_forward(held[block_rows(across, core), :], block_rows(across, core))
    partner_origins = (chip, ahead, behind, across)
    for kind in range(4):
        pair_copy(kind).wait_recv()
        place = block_rows(partner_origins[kind], 1 - core)
        feed_forward(held[place, :], place)
        back_copy(partner_origins[kind]).start()
    for kind in range(3):
        ring_copy(kind).wait_send()
    for kind in range(4):
        pair_copy(kind).wait_send()

    def summed(z):
        mine = parts[block_rows(z, core), :]
        return mine.astype(jnp.float32) + pair_buf[z].astype(jnp.float32)

    def sum_copy(kind, target):
        return pltpu.make_async_remote_copy(
            src_ref=send_buf.at[kind],
            dst_ref=ring_buf.at[kind],
            send_sem=sum_send.at[kind],
            recv_sem=sum_recv.at[kind],
            device_id=(req, target * 2 + core),
            device_id_type=pl.DeviceIdType.MESH,
        )

    back_copy(behind).wait_recv()
    send_buf[0] = summed(behind).astype(send_buf.dtype)
    sum_copy(0, behind).start()
    back_copy(across).wait_recv()
    send_buf[1] = summed(across).astype(send_buf.dtype)
    sum_copy(1, ahead).start()
    back_copy(ahead).wait_recv()
    sum_copy(1, ahead).wait_recv()
    send_buf[2] = (summed(ahead) + ring_buf[1].astype(jnp.float32)).astype(send_buf.dtype)
    sum_copy(2, ahead).start()
    back_copy(chip).wait_recv()
    total = summed(chip)
    for z in range(chips):
        back_copy(z).wait_send()
    sum_copy(0, behind).wait()
    total = total + ring_buf[0].astype(jnp.float32)
    sum_copy(1, ahead).wait_send()
    sum_copy(2, ahead).wait()
    o_ref[...] = x_ref[...].astype(jnp.float32) + (total + ring_buf[2].astype(jnp.float32))


def feed_forward_block(block, gain, shift, w_fc1, w_fc2):
    groups = lax.axis_size("mlp")
    chips = groups // 2
    rows, width = block.shape
    total = groups * rows
    out_width = w_fc2.shape[1]
    return pl.pallas_call(
        block_kernel,
        in_specs=[pl.BlockSpec(memory_space=pltpu.VMEM)] * 5,
        out_specs=pl.BlockSpec(memory_space=pltpu.VMEM),
        out_shape=jax.ShapeDtypeStruct((rows, out_width), jnp.float32),
        scratch_shapes=[
            pltpu.VMEM((rows, width), jnp.bfloat16),
            pltpu.VMEM((total, width), jnp.bfloat16),
            pltpu.VMEM((total, out_width), jnp.bfloat16),
            pltpu.VMEM((chips, rows, out_width), jnp.bfloat16),
            pltpu.VMEM((3, rows, out_width), jnp.bfloat16),
            pltpu.VMEM((3, rows, out_width), jnp.bfloat16),
            pltpu.SemaphoreType.DMA((3,)),
            pltpu.SemaphoreType.DMA((3,)),
            pltpu.SemaphoreType.DMA((chips,)),
            pltpu.SemaphoreType.DMA((chips,)),
            pltpu.SemaphoreType.DMA((chips,)),
            pltpu.SemaphoreType.DMA((chips,)),
            pltpu.SemaphoreType.DMA((3,)),
            pltpu.SemaphoreType.DMA((3,)),
        ],
        compiler_params=pltpu.CompilerParams(
            collective_id=2, has_side_effects=True, vmem_limit_bytes=48 * 1024 * 1024
        ),
    )(block, gain.reshape(1, -1), shift.reshape(1, -1), w_fc1, w_fc2)


def per_device(
    tokens,
    token_owner,
    token_request,
    cache_len,
    cache_k,
    cache_v,
    w_qkv,
    w_out,
    w_fc1,
    w_fc2,
    ln1_gain,
    ln1_bias,
    ln2_gain,
    ln2_bias,
):
    n_req = lax.axis_size("req")
    n_mlp = lax.axis_size("mlp")
    devices = n_req * n_mlp
    owner_index = lax.axis_index("req") * n_mlp + lax.axis_index("mlp")
    tok_dev, width = tokens.shape
    capacity = max(2, 2 * tok_dev // devices)
    slot_count = devices * capacity
    owners_flat = token_owner.reshape(-1)
    my_owners = lax.dynamic_slice_in_dim(owners_flat, owner_index * tok_dev, tok_dev)
    owner_onehot = (my_owners[:, None] == jnp.arange(devices, dtype=jnp.int32)[None, :]).astype(
        jnp.int32
    )
    ranking = jnp.cumsum(owner_onehot, axis=0) - 1
    my_rank = jnp.sum(owner_onehot * ranking, axis=1)
    column = my_owners * capacity + my_rank
    dispatch = (column[:, None] == jnp.arange(slot_count, dtype=jnp.int32)[None, :]).astype(
        jnp.bfloat16
    )
    outgoing = jnp.einsum("tr,td->rd", dispatch, tokens, preferred_element_type=jnp.float32).astype(
        jnp.bfloat16
    )
    arrived = lax.all_to_all(
        outgoing.reshape(devices, capacity, width),
        ("req", "mlp"),
        split_axis=0,
        concat_axis=0,
        tiled=True,
    )
    projections = jnp.dot(
        arrived.reshape(slot_count, width), w_qkv, preferred_element_type=jnp.float32
    ).astype(jnp.bfloat16)
    global_row, slot_request, filled = slot_table(
        owners_flat, token_request, owner_index, devices, tok_dev, capacity
    )
    attended = attend(projections, cache_k, cache_v, cache_len, global_row, slot_request, filled)
    returned = lax.all_to_all(
        attended.reshape(devices, capacity, width),
        ("req", "mlp"),
        split_axis=0,
        concat_axis=0,
        tiled=True,
    )
    attn_rows = jnp.einsum(
        "tsc,scd->td",
        dispatch.reshape(tok_dev, devices, capacity),
        returned,
        preferred_element_type=jnp.float32,
    ).astype(jnp.bfloat16)
    projected_out = jnp.dot(attn_rows, w_out, preferred_element_type=jnp.float32)
    mixed = feed_forward_block(
        projected_out + tokens.astype(jnp.float32), ln1_gain, ln1_bias, w_fc1, w_fc2
    )
    return layer_norm(mixed, ln2_gain, ln2_bias).astype(jnp.bfloat16)


def solution(mesh):
    placed = (
        P(("req", "mlp"), None),
        P(),
        P(),
        P(("req", "mlp")),
        P(("req", "mlp"), None, None),
        P(("req", "mlp"), None, None),
        P(),
        P(),
        P(None, "mlp"),
        P("mlp", None),
        P(),
        P(),
        P(),
        P(),
    )
    return jax.shard_map(
        per_device, mesh=mesh, in_specs=placed, out_specs=P(("req", "mlp"), None), check_vma=False
    )
```

```python
import jax
import jax.numpy as jnp
from jax import lax
from jax.sharding import PartitionSpec as P
from jax.experimental import pallas as pl
from jax.experimental.pallas import tpu as pltpu

HEADS = 16


epsilon = 1e-05


def layer_norm(values, gain, shift):
    center = values - jnp.mean(values, axis=-1, keepdims=True)
    spread = jnp.mean(center * center, axis=-1, keepdims=True)
    return center * lax.rsqrt(spread + epsilon) * gain + shift


def slot_table(owners_flat, requests_flat, owner_index, devices, tok_dev, capacity):
    owners = owners_flat.reshape(devices, tok_dev)
    requests = requests_flat.reshape(devices, tok_dev)
    mine_mask = (owners == owner_index).astype(jnp.int32)
    ranking = jnp.cumsum(mine_mask, axis=1) - 1
    places = jnp.arange(capacity, dtype=jnp.int32)
    hit_table = mine_mask[:, :, None] * (ranking[:, :, None] == places[None, None, :]).astype(
        jnp.int32
    )
    filled = jnp.sum(hit_table, axis=1)
    positions = jnp.arange(tok_dev, dtype=jnp.int32)
    local_row = jnp.sum(hit_table * positions[None, :, None], axis=1)
    sources = jnp.arange(devices, dtype=jnp.int32)[:, None]
    global_row = jnp.where(filled > 0, sources * tok_dev + local_row, -1).reshape(-1)
    slot_request = jnp.sum(hit_table * requests[:, :, None], axis=1).reshape(-1)
    return (global_row, slot_request, filled.reshape(-1))


def attention_kernel(
    q_ref, kn_ref, vn_ref, k_ref, v_ref, rreq_ref, rrow_ref, rfill_ref, ctag_ref, ntag_ref, nrow_ref, o_ref
):
    head_dim = q_ref.shape[1] // 2
    score_scale = head_dim ** (-0.5)
    q = q_ref[...] * jnp.asarray(score_scale, q_ref.dtype)
    keys = k_ref[...]
    values = v_ref[...]
    key_new = kn_ref[...]
    value_new = vn_ref[...]
    row_request = rreq_ref[...]
    old_mask = ctag_ref[...] == row_request
    new_mask = (ntag_ref[...] == row_request) & (nrow_ref[...] <= rrow_ref[...])
    lane = lax.broadcasted_iota(jnp.int32, (1, q.shape[1]), 1)
    contract = (((1,), (1,)), ((), ()))
    result = None
    for half in range(2):
        in_head = (lane // head_dim) == half
        q_head = jnp.where(in_head, q, jnp.zeros_like(q))
        old_score = lax.dot_general(q_head, keys, contract, preferred_element_type=jnp.float32)
        new_score = lax.dot_general(q_head, key_new, contract, preferred_element_type=jnp.float32)
        old_exp = jnp.where(old_mask, jnp.exp(old_score), jnp.float32(0.0))
        new_exp = jnp.where(new_mask, jnp.exp(new_score), jnp.float32(0.0))
        total = jnp.sum(old_exp, axis=1, keepdims=True) + jnp.sum(new_exp, axis=1, keepdims=True)
        total = jnp.where(total > 0, total, jnp.float32(1.0))
        inverse = 1.0 / total
        old_weight = (old_exp * inverse).astype(jnp.bfloat16)
        new_weight = (new_exp * inverse).astype(jnp.bfloat16)
        part = jnp.dot(old_weight, values, preferred_element_type=jnp.float32) + jnp.dot(
            new_weight, value_new, preferred_element_type=jnp.float32
        )
        result = part if result is None else jnp.where(in_head, part, result)
    result = jnp.where(rfill_ref[...] > 0, result, jnp.float32(0.0))
    o_ref[...] = result.astype(o_ref.dtype)


def attend(projections, cache_keys, cache_values, lengths, global_row, slot_request, filled):
    slot_count = projections.shape[0]
    width = projections.shape[1] // 3
    requests, context = cache_keys.shape[0], cache_keys.shape[1]
    pair = 128
    pairs = width // pair
    keys = cache_keys.reshape(requests * context, width)
    values = cache_values.reshape(requests * context, width)
    key_owner = jnp.arange(requests * context, dtype=jnp.int32) // context
    key_place = jnp.arange(requests * context, dtype=jnp.int32) % context
    key_limit = jnp.repeat(lengths, context)
    column_tag = jnp.where(key_place < key_limit, key_owner, -1).reshape(1, -1)
    new_tag = jnp.where(filled > 0, slot_request, -1).reshape(1, -1)
    new_row = global_row.reshape(1, -1)
    row_request = slot_request.reshape(-1, 1)
    row_index = global_row.reshape(-1, 1)
    row_filled = filled.reshape(-1, 1)
    keyed = requests * context
    whole = lambda shape: pl.BlockSpec(shape, lambda p: (0, 0))
    return pl.pallas_call(
        attention_kernel,
        grid=(pairs,),
        in_specs=[
            pl.BlockSpec((slot_count, pair), lambda p: (0, p)),
            pl.BlockSpec((slot_count, pair), lambda p: (0, pairs + p)),
            pl.BlockSpec((slot_count, pair), lambda p: (0, 2 * pairs + p)),
            pl.BlockSpec((keyed, pair), lambda p: (0, p)),
            pl.BlockSpec((keyed, pair), lambda p: (0, p)),
            whole((slot_count, 1)),
            whole((slot_count, 1)),
            whole((slot_count, 1)),
            whole((1, keyed)),
            whole((1, slot_count)),
            whole((1, slot_count)),
        ],
        out_specs=pl.BlockSpec((slot_count, pair), lambda p: (0, p)),
        out_shape=jax.ShapeDtypeStruct((slot_count, width), jnp.bfloat16),
        compiler_params=pltpu.CompilerParams(vmem_limit_bytes=48 * 1024 * 1024),
    )(
        projections,
        projections,
        projections,
        keys,
        values,
        row_request,
        row_index,
        row_filled,
        column_tag,
        new_tag,
        new_row,
    )


def block_kernel(
    y_ref, gain_ref, shift_ref, w1_hbm, w2_hbm, o_ref, w1_ref, w2_ref, load_sem, x_ref, held, parts, pair_buf, send_buf, ring_buf,
    ring_send, ring_recv, pair_send, pair_recv, back_send, back_recv, sum_send, sum_recv,
):
    load_one = pltpu.make_async_copy(w1_hbm, w1_ref, load_sem.at[0])
    load_two = pltpu.make_async_copy(w2_hbm, w2_ref, load_sem.at[1])
    load_one.start()
    load_two.start()
    x_ref[...] = layer_norm(y_ref[...], gain_ref[...], shift_ref[...]).astype(x_ref.dtype)
    req = lax.axis_index("req")
    me = lax.axis_index("mlp")
    chips = lax.axis_size("mlp") // 2
    chip, core = me // 2, lax.rem(me, 2)
    partner = chip * 2 + 1 - core
    step = 1 - 2 * core
    ahead = lax.rem(chip + step + chips, chips)
    behind = lax.rem(chip - step + chips, chips)
    across = lax.rem(chip + 2, chips)
    rows = x_ref.shape[0]
    barrier = pltpu.get_barrier_semaphore()
    pl.semaphore_signal(barrier, 1, device_id=(req, partner), device_id_type=pl.DeviceIdType.MESH)
    pl.semaphore_signal(barrier, 1, device_id=(req, ahead * 2 + core), device_id_type=pl.DeviceIdType.MESH)
    pl.semaphore_signal(barrier, 1, device_id=(req, behind * 2 + core), device_id_type=pl.DeviceIdType.MESH)
    pl.semaphore_wait(barrier, 3)

    def block_rows(z, which):
        return pl.ds(pl.multiple_of((z * 2 + which) * rows, rows), rows)

    origins = (chip, behind, ahead, across)

    def ring_copy(kind):
        source = x_ref if kind < 2 else held.at[block_rows(behind, core)]
        origin = chip if kind < 2 else behind
        target = ahead if kind != 1 else behind
        return pltpu.make_async_remote_copy(
            src_ref=source,
            dst_ref=held.at[block_rows(origin, core)],
            send_sem=ring_send.at[kind],
            recv_sem=ring_recv.at[kind],
            device_id=(req, target * 2 + core),
            device_id_type=pl.DeviceIdType.MESH,
        )

    def pair_copy(kind):
        source = x_ref if kind == 0 else held.at[block_rows(origins[kind], core)]
        return pltpu.make_async_remote_copy(
            src_ref=source,
            dst_ref=held.at[block_rows(origins[kind], core)],
            send_sem=pair_send.at[kind],
            recv_sem=pair_recv.at[kind],
            device_id=(req, partner),
            device_id_type=pl.DeviceIdType.MESH,
        )

    def back_copy(z):
        return pltpu.make_async_remote_copy(
            src_ref=parts.at[block_rows(z, 1 - core)],
            dst_ref=pair_buf.at[z],
            send_sem=back_send.at[z],
            recv_sem=back_recv.at[z],
            device_id=(req, partner),
            device_id_type=pl.DeviceIdType.MESH,
        )

    def feed_forward(block, place):
        hidden = jnp.dot(block, w1_ref[...], preferred_element_type=jnp.float32)
        hidden = (hidden * 0.5 * (1.0 + lax.erf(hidden * (2.0 ** -0.5)))).astype(jnp.bfloat16)
        parts[place, :] = jnp.dot(hidden, w2_ref[...], preferred_element_type=jnp.float32).astype(
            parts.dtype
        )

    ring_copy(0).start()
    ring_copy(1).start()
    pair_copy(0).start()
    load_one.wait()
    load_two.wait()
    feed_forward(x_ref[...], block_rows(chip, core))
    ring_copy(0).wait_recv()
    ring_copy(2).start()
    pair_copy(1).start()
    feed_forward(held[block_rows(behind, core), :], block_rows(behind, core))
    ring_copy(1).wait_recv()
    pair_copy(2).start()
    feed_forward(held[block_rows(ahead, core), :], block_rows(ahead, core))
    ring_copy(2).wait_recv()
    pair_copy(3).start()
    feed_forward(held[block_rows(across, core), :], block_rows(across, core))
    partner_origins = (chip, ahead, behind, across)
    for kind in range(4):
        pair_copy(kind).wait_recv()
        place = block_rows(partner_origins[kind], 1 - core)
        feed_forward(held[place, :], place)
        back_copy(partner_origins[kind]).start()
    for kind in range(3):
        ring_copy(kind).wait_send()
    for kind in range(4):
        pair_copy(kind).wait_send()

    def summed(z):
        mine = parts[block_rows(z, core), :]
        return mine.astype(jnp.float32) + pair_buf[z].astype(jnp.float32)

    def sum_copy(kind, target):
        return pltpu.make_async_remote_copy(
            src_ref=send_buf.at[kind],
            dst_ref=ring_buf.at[kind],
            send_sem=sum_send.at[kind],
            recv_sem=sum_recv.at[kind],
            device_id=(req, target * 2 + core),
            device_id_type=pl.DeviceIdType.MESH,
        )

    back_copy(behind).wait_recv()
    send_buf[0] = summed(behind).astype(send_buf.dtype)
    sum_copy(0, behind).start()
    back_copy(across).wait_recv()
    send_buf[1] = summed(across).astype(send_buf.dtype)
    sum_copy(1, ahead).start()
    back_copy(ahead).wait_recv()
    sum_copy(1, ahead).wait_recv()
    send_buf[2] = (summed(ahead) + ring_buf[1].astype(jnp.float32)).astype(send_buf.dtype)
    sum_copy(2, ahead).start()
    back_copy(chip).wait_recv()
    total = summed(chip)
    for z in range(chips):
        back_copy(z).wait_send()
    sum_copy(0, behind).wait()
    total = total + ring_buf[0].astype(jnp.float32)
    sum_copy(1, ahead).wait_send()
    sum_copy(2, ahead).wait()
    o_ref[...] = x_ref[...].astype(jnp.float32) + (total + ring_buf[2].astype(jnp.float32))


def feed_forward_block(block, gain, shift, w_fc1, w_fc2):
    groups = lax.axis_size("mlp")
    chips = groups // 2
    rows, width = block.shape
    total = groups * rows
    out_width = w_fc2.shape[1]
    return pl.pallas_call(
        block_kernel,
        in_specs=[pl.BlockSpec(memory_space=pltpu.VMEM)] * 3 + [pl.BlockSpec(memory_space=pl.ANY)] * 2,
        out_specs=pl.BlockSpec(memory_space=pltpu.VMEM),
        out_shape=jax.ShapeDtypeStruct((rows, out_width), jnp.float32),
        scratch_shapes=[
            pltpu.VMEM(w_fc1.shape, w_fc1.dtype),
            pltpu.VMEM(w_fc2.shape, w_fc2.dtype),
            pltpu.SemaphoreType.DMA((2,)),
            pltpu.VMEM((rows, width), jnp.bfloat16),
            pltpu.VMEM((total, width), jnp.bfloat16),
            pltpu.VMEM((total, out_width), jnp.bfloat16),
            pltpu.VMEM((chips, rows, out_width), jnp.bfloat16),
            pltpu.VMEM((3, rows, out_width), jnp.bfloat16),
            pltpu.VMEM((3, rows, out_width), jnp.bfloat16),
            pltpu.SemaphoreType.DMA((3,)),
            pltpu.SemaphoreType.DMA((3,)),
            pltpu.SemaphoreType.DMA((chips,)),
            pltpu.SemaphoreType.DMA((chips,)),
            pltpu.SemaphoreType.DMA((chips,)),
            pltpu.SemaphoreType.DMA((chips,)),
            pltpu.SemaphoreType.DMA((3,)),
            pltpu.SemaphoreType.DMA((3,)),
        ],
        compiler_params=pltpu.CompilerParams(
            collective_id=2, has_side_effects=True, vmem_limit_bytes=62 * 1024 * 1024
        ),
    )(block, gain.reshape(1, -1), shift.reshape(1, -1), w_fc1, w_fc2)


def per_device(
    tokens,
    token_owner,
    token_request,
    cache_len,
    cache_k,
    cache_v,
    w_qkv,
    w_out,
    w_fc1,
    w_fc2,
    ln1_gain,
    ln1_bias,
    ln2_gain,
    ln2_bias,
):
    n_req = lax.axis_size("req")
    n_mlp = lax.axis_size("mlp")
    devices = n_req * n_mlp
    owner_index = lax.axis_index("req") * n_mlp + lax.axis_index("mlp")
    tok_dev, width = tokens.shape
    capacity = max(2, 2 * tok_dev // devices)
    slot_count = devices * capacity
    owners_flat = token_owner.reshape(-1)
    my_owners = lax.dynamic_slice_in_dim(owners_flat, owner_index * tok_dev, tok_dev)
    owner_onehot = (my_owners[:, None] == jnp.arange(devices, dtype=jnp.int32)[None, :]).astype(
        jnp.int32
    )
    ranking = jnp.cumsum(owner_onehot, axis=0) - 1
    my_rank = jnp.sum(owner_onehot * ranking, axis=1)
    column = my_owners * capacity + my_rank
    dispatch = (column[:, None] == jnp.arange(slot_count, dtype=jnp.int32)[None, :]).astype(
        jnp.bfloat16
    )
    outgoing = jnp.einsum("tr,td->rd", dispatch, tokens, preferred_element_type=jnp.float32).astype(
        jnp.bfloat16
    )
    arrived = lax.all_to_all(
        outgoing.reshape(devices, capacity, width),
        ("req", "mlp"),
        split_axis=0,
        concat_axis=0,
        tiled=True,
    )
    projections = jnp.dot(
        arrived.reshape(slot_count, width), w_qkv, preferred_element_type=jnp.float32
    ).astype(jnp.bfloat16)
    global_row, slot_request, filled = slot_table(
        owners_flat, token_request, owner_index, devices, tok_dev, capacity
    )
    attended = attend(projections, cache_k, cache_v, cache_len, global_row, slot_request, filled)
    returned = lax.all_to_all(
        attended.reshape(devices, capacity, width),
        ("req", "mlp"),
        split_axis=0,
        concat_axis=0,
        tiled=True,
    )
    attn_rows = jnp.einsum(
        "tsc,scd->td",
        dispatch.reshape(tok_dev, devices, capacity),
        returned,
        preferred_element_type=jnp.float32,
    ).astype(jnp.bfloat16)
    projected_out = jnp.dot(attn_rows, w_out, preferred_element_type=jnp.float32)
    mixed = feed_forward_block(
        projected_out + tokens.astype(jnp.float32), ln1_gain, ln1_bias, w_fc1, w_fc2
    )
    return layer_norm(mixed, ln2_gain, ln2_bias).astype(jnp.bfloat16)


def solution(mesh):
    placed = (
        P(("req", "mlp"), None),
        P(),
        P(),
        P(("req", "mlp")),
        P(("req", "mlp"), None, None),
        P(("req", "mlp"), None, None),
        P(),
        P(),
        P(None, "mlp"),
        P("mlp", None),
        P(),
        P(),
        P(),
        P(),
    )
    return jax.shard_map(
        per_device, mesh=mesh, in_specs=placed, out_specs=P(("req", "mlp"), None), check_vma=False
    )
```

```python
import jax
import jax.numpy as jnp
from jax import lax
from jax.sharding import PartitionSpec as P
from jax.experimental import pallas as pl
from jax.experimental.pallas import tpu as pltpu

HEADS = 16


epsilon = 1e-05


def layer_norm(values, gain, shift):
    center = values - jnp.mean(values, axis=-1, keepdims=True)
    spread = jnp.mean(center * center, axis=-1, keepdims=True)
    return center * lax.rsqrt(spread + epsilon) * gain + shift


def slot_table(owners_flat, requests_flat, owner_index, devices, tok_dev, capacity):
    owners = owners_flat.reshape(devices, tok_dev)
    requests = requests_flat.reshape(devices, tok_dev)
    mine_mask = (owners == owner_index).astype(jnp.int32)
    ranking = jnp.cumsum(mine_mask, axis=1) - 1
    places = jnp.arange(capacity, dtype=jnp.int32)
    hit_table = mine_mask[:, :, None] * (ranking[:, :, None] == places[None, None, :]).astype(
        jnp.int32
    )
    filled = jnp.sum(hit_table, axis=1)
    positions = jnp.arange(tok_dev, dtype=jnp.int32)
    local_row = jnp.sum(hit_table * positions[None, :, None], axis=1)
    sources = jnp.arange(devices, dtype=jnp.int32)[:, None]
    global_row = jnp.where(filled > 0, sources * tok_dev + local_row, -1).reshape(-1)
    slot_request = jnp.sum(hit_table * requests[:, :, None], axis=1).reshape(-1)
    return (global_row, slot_request, filled.reshape(-1))


def attention_kernel(
    q_ref, kn_ref, vn_ref, k_ref, v_ref, rreq_ref, rrow_ref, rfill_ref, ctag_ref, ntag_ref, nrow_ref, o_ref
):
    head_dim = q_ref.shape[1] // 2
    score_scale = head_dim ** (-0.5)
    q = q_ref[...] * jnp.asarray(score_scale, q_ref.dtype)
    keys = k_ref[...]
    values = v_ref[...]
    key_new = kn_ref[...]
    value_new = vn_ref[...]
    row_request = rreq_ref[...]
    key_tag = ctag_ref[...]
    new_mask = (ntag_ref[...] == row_request) & (nrow_ref[...] <= rrow_ref[...])
    lane = lax.broadcasted_iota(jnp.int32, (1, q.shape[1]), 1)
    contract = (((1,), (1,)), ((), ()))
    result = None
    for half in range(2):
        in_head = (lane // head_dim) == half
        slot = lane - (1 - half) * head_dim
        spare = (slot >= 0) & (slot < 8)
        q_head = jnp.where(in_head, q, jnp.zeros_like(q))
        q_bias = jnp.where(spare & (row_request == slot), jnp.ones_like(q), q_head)
        key_bias = jnp.where(key_tag == slot, jnp.float32(0.0), jnp.float32(-1e30)).astype(keys.dtype)
        keys_bias = jnp.where(spare, key_bias, keys)
        old_score = lax.dot_general(q_bias, keys_bias, contract, preferred_element_type=jnp.float32)
        new_score = lax.dot_general(q_head, key_new, contract, preferred_element_type=jnp.float32)
        old_exp = jnp.exp(old_score)
        new_exp = jnp.where(new_mask, jnp.exp(new_score), jnp.float32(0.0))
        total = jnp.sum(old_exp, axis=1, keepdims=True) + jnp.sum(new_exp, axis=1, keepdims=True)
        total = jnp.where(total > 0, total, jnp.float32(1.0))
        inverse = 1.0 / total
        old_weight = (old_exp * inverse).astype(jnp.bfloat16)
        new_weight = (new_exp * inverse).astype(jnp.bfloat16)
        part = jnp.dot(old_weight, values, preferred_element_type=jnp.float32) + jnp.dot(
            new_weight, value_new, preferred_element_type=jnp.float32
        )
        result = part if result is None else jnp.where(in_head, part, result)
    result = jnp.where(rfill_ref[...] > 0, result, jnp.float32(0.0))
    o_ref[...] = result.astype(o_ref.dtype)


def attend(projections, cache_keys, cache_values, lengths, global_row, slot_request, filled):
    slot_count = projections.shape[0]
    width = projections.shape[1] // 3
    requests, context = cache_keys.shape[0], cache_keys.shape[1]
    pair = 128
    pairs = width // pair
    keys = cache_keys.reshape(requests * context, width)
    values = cache_values.reshape(requests * context, width)
    key_owner = jnp.arange(requests * context, dtype=jnp.int32) // context
    key_place = jnp.arange(requests * context, dtype=jnp.int32) % context
    key_limit = jnp.repeat(lengths, context)
    column_tag = jnp.where(key_place < key_limit, key_owner, -1).reshape(-1, 1)
    new_tag = jnp.where(filled > 0, slot_request, -1).reshape(1, -1)
    new_row = global_row.reshape(1, -1)
    row_request = slot_request.reshape(-1, 1)
    row_index = global_row.reshape(-1, 1)
    row_filled = filled.reshape(-1, 1)
    keyed = requests * context
    whole = lambda shape: pl.BlockSpec(shape, lambda p: (0, 0))
    return pl.pallas_call(
        attention_kernel,
        grid=(pairs,),
        in_specs=[
            pl.BlockSpec((slot_count, pair), lambda p: (0, p)),
            pl.BlockSpec((slot_count, pair), lambda p: (0, pairs + p)),
            pl.BlockSpec((slot_count, pair), lambda p: (0, 2 * pairs + p)),
            pl.BlockSpec((keyed, pair), lambda p: (0, p)),
            pl.BlockSpec((keyed, pair), lambda p: (0, p)),
            whole((slot_count, 1)),
            whole((slot_count, 1)),
            whole((slot_count, 1)),
            whole((keyed, 1)),
            whole((1, slot_count)),
            whole((1, slot_count)),
        ],
        out_specs=pl.BlockSpec((slot_count, pair), lambda p: (0, p)),
        out_shape=jax.ShapeDtypeStruct((slot_count, width), jnp.bfloat16),
        compiler_params=pltpu.CompilerParams(vmem_limit_bytes=48 * 1024 * 1024),
    )(
        projections,
        projections,
        projections,
        keys,
        values,
        row_request,
        row_index,
        row_filled,
        column_tag,
        new_tag,
        new_row,
    )


def block_kernel(
    y_ref, gain_ref, shift_ref, w1_ref, w2_ref, o_ref, x_ref, held, parts, pair_buf, send_buf, ring_buf,
    ring_send, ring_recv, pair_send, pair_recv, back_send, back_recv, sum_send, sum_recv,
):
    x_ref[...] = layer_norm(y_ref[...], gain_ref[...], shift_ref[...]).astype(x_ref.dtype)
    req = lax.axis_index("req")
    me = lax.axis_index("mlp")
    chips = lax.axis_size("mlp") // 2
    chip, core = me // 2, lax.rem(me, 2)
    partner = chip * 2 + 1 - core
    step = 1 - 2 * core
    ahead = lax.rem(chip + step + chips, chips)
    behind = lax.rem(chip - step + chips, chips)
    across = lax.rem(chip + 2, chips)
    rows = x_ref.shape[0]
    barrier = pltpu.get_barrier_semaphore()
    pl.semaphore_signal(barrier, 1, device_id=(req, partner), device_id_type=pl.DeviceIdType.MESH)
    pl.semaphore_signal(barrier, 1, device_id=(req, ahead * 2 + core), device_id_type=pl.DeviceIdType.MESH)
    pl.semaphore_signal(barrier, 1, device_id=(req, behind * 2 + core), device_id_type=pl.DeviceIdType.MESH)
    pl.semaphore_wait(barrier, 3)

    def block_rows(z, which):
        return pl.ds(pl.multiple_of((z * 2 + which) * rows, rows), rows)

    origins = (chip, behind, ahead, across)

    def ring_copy(kind):
        source = x_ref if kind < 2 else held.at[block_rows(behind, core)]
        origin = chip if kind < 2 else behind
        target = ahead if kind != 1 else behind
        return pltpu.make_async_remote_copy(
            src_ref=source,
            dst_ref=held.at[block_rows(origin, core)],
            send_sem=ring_send.at[kind],
            recv_sem=ring_recv.at[kind],
            device_id=(req, target * 2 + core),
            device_id_type=pl.DeviceIdType.MESH,
        )

    def pair_copy(kind):
        source = x_ref if kind == 0 else held.at[block_rows(origins[kind], core)]
        return pltpu.make_async_remote_copy(
            src_ref=source,
            dst_ref=held.at[block_rows(origins[kind], core)],
            send_sem=pair_send.at[kind],
            recv_sem=pair_recv.at[kind],
            device_id=(req, partner),
            device_id_type=pl.DeviceIdType.MESH,
        )

    def back_copy(z):
        return pltpu.make_async_remote_copy(
            src_ref=parts.at[block_rows(z, 1 - core)],
            dst_ref=pair_buf.at[z],
            send_sem=back_send.at[z],
            recv_sem=back_recv.at[z],
            device_id=(req, partner),
            device_id_type=pl.DeviceIdType.MESH,
        )

    def feed_forward(block, place):
        hidden = jnp.dot(block, w1_ref[...], preferred_element_type=jnp.float32)
        hidden = (hidden * 0.5 * (1.0 + lax.erf(hidden * (2.0 ** -0.5)))).astype(jnp.bfloat16)
        parts[place, :] = jnp.dot(hidden, w2_ref[...], preferred_element_type=jnp.float32).astype(
            parts.dtype
        )

    ring_copy(0).start()
    ring_copy(1).start()
    pair_copy(0).start()
    feed_forward(x_ref[...], block_rows(chip, core))
    ring_copy(0).wait_recv()
    ring_copy(2).start()
    pair_copy(1).start()
    feed_forward(held[block_rows(behind, core), :], block_rows(behind, core))
    ring_copy(1).wait_recv()
    pair_copy(2).start()
    feed_forward(held[block_rows(ahead, core), :], block_rows(ahead, core))
    ring_copy(2).wait_recv()
    pair_copy(3).start()
    feed_forward(held[block_rows(across, core), :], block_rows(across, core))
    partner_origins = (chip, ahead, behind, across)
    for kind in range(4):
        pair_copy(kind).wait_recv()
        place = block_rows(partner_origins[kind], 1 - core)
        feed_forward(held[place, :], place)
        back_copy(partner_origins[kind]).start()
    for kind in range(3):
        ring_copy(kind).wait_send()
    for kind in range(4):
        pair_copy(kind).wait_send()

    def summed(z):
        mine = parts[block_rows(z, core), :]
        return mine.astype(jnp.float32) + pair_buf[z].astype(jnp.float32)

    def sum_copy(kind, target):
        return pltpu.make_async_remote_copy(
            src_ref=send_buf.at[kind],
            dst_ref=ring_buf.at[kind],
            send_sem=sum_send.at[kind],
            recv_sem=sum_recv.at[kind],
            device_id=(req, target * 2 + core),
            device_id_type=pl.DeviceIdType.MESH,
        )

    back_copy(behind).wait_recv()
    send_buf[0] = summed(behind).astype(send_buf.dtype)
    sum_copy(0, behind).start()
    back_copy(across).wait_recv()
    send_buf[1] = summed(across).astype(send_buf.dtype)
    sum_copy(1, ahead).start()
    back_copy(ahead).wait_recv()
    sum_copy(1, ahead).wait_recv()
    send_buf[2] = (summed(ahead) + ring_buf[1].astype(jnp.float32)).astype(send_buf.dtype)
    sum_copy(2, ahead).start()
    back_copy(chip).wait_recv()
    total = summed(chip)
    for z in range(chips):
        back_copy(z).wait_send()
    sum_copy(0, behind).wait()
    total = total + ring_buf[0].astype(jnp.float32)
    sum_copy(1, ahead).wait_send()
    sum_copy(2, ahead).wait()
    o_ref[...] = x_ref[...].astype(jnp.float32) + (total + ring_buf[2].astype(jnp.float32))


def feed_forward_block(block, gain, shift, w_fc1, w_fc2):
    groups = lax.axis_size("mlp")
    chips = groups // 2
    rows, width = block.shape
    total = groups * rows
    out_width = w_fc2.shape[1]
    return pl.pallas_call(
        block_kernel,
        in_specs=[pl.BlockSpec(memory_space=pltpu.VMEM)] * 5,
        out_specs=pl.BlockSpec(memory_space=pltpu.VMEM),
        out_shape=jax.ShapeDtypeStruct((rows, out_width), jnp.float32),
        scratch_shapes=[
            pltpu.VMEM((rows, width), jnp.bfloat16),
            pltpu.VMEM((total, width), jnp.bfloat16),
            pltpu.VMEM((total, out_width), jnp.bfloat16),
            pltpu.VMEM((chips, rows, out_width), jnp.bfloat16),
            pltpu.VMEM((3, rows, out_width), jnp.bfloat16),
            pltpu.VMEM((3, rows, out_width), jnp.bfloat16),
            pltpu.SemaphoreType.DMA((3,)),
            pltpu.SemaphoreType.DMA((3,)),
            pltpu.SemaphoreType.DMA((chips,)),
            pltpu.SemaphoreType.DMA((chips,)),
            pltpu.SemaphoreType.DMA((chips,)),
            pltpu.SemaphoreType.DMA((chips,)),
            pltpu.SemaphoreType.DMA((3,)),
            pltpu.SemaphoreType.DMA((3,)),
        ],
        compiler_params=pltpu.CompilerParams(
            collective_id=2, has_side_effects=True, vmem_limit_bytes=48 * 1024 * 1024
        ),
    )(block, gain.reshape(1, -1), shift.reshape(1, -1), w_fc1, w_fc2)


def per_device(
    tokens,
    token_owner,
    token_request,
    cache_len,
    cache_k,
    cache_v,
    w_qkv,
    w_out,
    w_fc1,
    w_fc2,
    ln1_gain,
    ln1_bias,
    ln2_gain,
    ln2_bias,
):
    n_req = lax.axis_size("req")
    n_mlp = lax.axis_size("mlp")
    devices = n_req * n_mlp
    owner_index = lax.axis_index("req") * n_mlp + lax.axis_index("mlp")
    tok_dev, width = tokens.shape
    capacity = max(2, 2 * tok_dev // devices)
    slot_count = devices * capacity
    owners_flat = token_owner.reshape(-1)
    my_owners = lax.dynamic_slice_in_dim(owners_flat, owner_index * tok_dev, tok_dev)
    owner_onehot = (my_owners[:, None] == jnp.arange(devices, dtype=jnp.int32)[None, :]).astype(
        jnp.int32
    )
    ranking = jnp.cumsum(owner_onehot, axis=0) - 1
    my_rank = jnp.sum(owner_onehot * ranking, axis=1)
    column = my_owners * capacity + my_rank
    dispatch = (column[:, None] == jnp.arange(slot_count, dtype=jnp.int32)[None, :]).astype(
        jnp.bfloat16
    )
    outgoing = jnp.einsum("tr,td->rd", dispatch, tokens, preferred_element_type=jnp.float32).astype(
        jnp.bfloat16
    )
    arrived = lax.all_to_all(
        outgoing.reshape(devices, capacity, width),
        ("req", "mlp"),
        split_axis=0,
        concat_axis=0,
        tiled=True,
    )
    projections = jnp.dot(
        arrived.reshape(slot_count, width), w_qkv, preferred_element_type=jnp.float32
    ).astype(jnp.bfloat16)
    global_row, slot_request, filled = slot_table(
        owners_flat, token_request, owner_index, devices, tok_dev, capacity
    )
    attended = attend(projections, cache_k, cache_v, cache_len, global_row, slot_request, filled)
    returned = lax.all_to_all(
        attended.reshape(devices, capacity, width),
        ("req", "mlp"),
        split_axis=0,
        concat_axis=0,
        tiled=True,
    )
    attn_rows = jnp.einsum(
        "tsc,scd->td",
        dispatch.reshape(tok_dev, devices, capacity),
        returned,
        preferred_element_type=jnp.float32,
    ).astype(jnp.bfloat16)
    projected_out = jnp.dot(attn_rows, w_out, preferred_element_type=jnp.float32)
    mixed = feed_forward_block(
        projected_out + tokens.astype(jnp.float32), ln1_gain, ln1_bias, w_fc1, w_fc2
    )
    return layer_norm(mixed, ln2_gain, ln2_bias).astype(jnp.bfloat16)


def solution(mesh):
    placed = (
        P(("req", "mlp"), None),
        P(),
        P(),
        P(("req", "mlp")),
        P(("req", "mlp"), None, None),
        P(("req", "mlp"), None, None),
        P(),
        P(),
        P(None, "mlp"),
        P("mlp", None),
        P(),
        P(),
        P(),
        P(),
    )
    return jax.shard_map(
        per_device, mesh=mesh, in_specs=placed, out_specs=P(("req", "mlp"), None), check_vma=False
    )
```

```python
import jax
import jax.numpy as jnp
from jax import lax
from jax.sharding import PartitionSpec as P
from jax.experimental import pallas as pl
from jax.experimental.pallas import tpu as pltpu

HEADS = 16


epsilon = 1e-05


def layer_norm(values, gain, shift):
    center = values - jnp.mean(values, axis=-1, keepdims=True)
    spread = jnp.mean(center * center, axis=-1, keepdims=True)
    return center * lax.rsqrt(spread + epsilon) * gain + shift


def slot_table(owners_flat, requests_flat, owner_index, devices, tok_dev, capacity):
    owners = owners_flat.reshape(devices, tok_dev)
    requests = requests_flat.reshape(devices, tok_dev)
    mine_mask = (owners == owner_index).astype(jnp.int32)
    ranking = jnp.cumsum(mine_mask, axis=1) - 1
    places = jnp.arange(capacity, dtype=jnp.int32)
    hit_table = mine_mask[:, :, None] * (ranking[:, :, None] == places[None, None, :]).astype(
        jnp.int32
    )
    filled = jnp.sum(hit_table, axis=1)
    positions = jnp.arange(tok_dev, dtype=jnp.int32)
    local_row = jnp.sum(hit_table * positions[None, :, None], axis=1)
    sources = jnp.arange(devices, dtype=jnp.int32)[:, None]
    global_row = jnp.where(filled > 0, sources * tok_dev + local_row, -1).reshape(-1)
    slot_request = jnp.sum(hit_table * requests[:, :, None], axis=1).reshape(-1)
    return (global_row, slot_request, filled.reshape(-1))


def attention_kernel(
    q_ref, kn_ref, vn_ref, k_ref, v_ref, rreq_ref, rrow_ref, rfill_ref, ctag_ref, ntag_ref, nrow_ref, o_ref
):
    head_dim = q_ref.shape[1] // 2
    score_scale = head_dim ** (-0.5)
    q = q_ref[...] * jnp.asarray(score_scale, q_ref.dtype)
    keys = k_ref[...]
    values = v_ref[...]
    key_new = kn_ref[...]
    value_new = vn_ref[...]
    row_request = rreq_ref[...]
    old_mask = ctag_ref[...] == row_request
    new_mask = (ntag_ref[...] == row_request) & (nrow_ref[...] <= rrow_ref[...])
    lane = lax.broadcasted_iota(jnp.int32, (1, q.shape[1]), 1)
    contract = (((1,), (1,)), ((), ()))
    result = None
    for half in range(2):
        in_head = (lane // head_dim) == half
        q_head = jnp.where(in_head, q, jnp.zeros_like(q))
        old_score = lax.dot_general(q_head, keys, contract, preferred_element_type=jnp.float32)
        new_score = lax.dot_general(q_head, key_new, contract, preferred_element_type=jnp.float32)
        old_exp = jnp.where(old_mask, jnp.exp(old_score), jnp.float32(0.0))
        new_exp = jnp.where(new_mask, jnp.exp(new_score), jnp.float32(0.0))
        total = jnp.sum(old_exp, axis=1, keepdims=True) + jnp.sum(new_exp, axis=1, keepdims=True)
        total = jnp.where(total > 0, total, jnp.float32(1.0))
        inverse = 1.0 / total
        old_weight = (old_exp * inverse).astype(jnp.bfloat16)
        new_weight = (new_exp * inverse).astype(jnp.bfloat16)
        part = jnp.dot(old_weight, values, preferred_element_type=jnp.float32) + jnp.dot(
            new_weight, value_new, preferred_element_type=jnp.float32
        )
        result = part if result is None else jnp.where(in_head, part, result)
    result = jnp.where(rfill_ref[...] > 0, result, jnp.float32(0.0))
    o_ref[...] = result.astype(o_ref.dtype)


def attend(projections, cache_keys, cache_values, lengths, global_row, slot_request, filled):
    slot_count = projections.shape[0]
    width = projections.shape[1] // 3
    requests, context = cache_keys.shape[0], cache_keys.shape[1]
    pair = 128
    pairs = width // pair
    keys = cache_keys.reshape(requests * context, width)
    values = cache_values.reshape(requests * context, width)
    key_owner = jnp.arange(requests * context, dtype=jnp.int32) // context
    key_place = jnp.arange(requests * context, dtype=jnp.int32) % context
    key_limit = jnp.repeat(lengths, context)
    column_tag = jnp.where(key_place < key_limit, key_owner, -1).reshape(1, -1)
    new_tag = jnp.where(filled > 0, slot_request, -1).reshape(1, -1)
    new_row = global_row.reshape(1, -1)
    row_request = slot_request.reshape(-1, 1)
    row_index = global_row.reshape(-1, 1)
    row_filled = filled.reshape(-1, 1)
    keyed = requests * context
    whole = lambda shape: pl.BlockSpec(shape, lambda p: (0, 0))
    return pl.pallas_call(
        attention_kernel,
        grid=(pairs,),
        in_specs=[
            pl.BlockSpec((slot_count, pair), lambda p: (0, p)),
            pl.BlockSpec((slot_count, pair), lambda p: (0, pairs + p)),
            pl.BlockSpec((slot_count, pair), lambda p: (0, 2 * pairs + p)),
            pl.BlockSpec((keyed, pair), lambda p: (0, p)),
            pl.BlockSpec((keyed, pair), lambda p: (0, p)),
            whole((slot_count, 1)),
            whole((slot_count, 1)),
            whole((slot_count, 1)),
            whole((1, keyed)),
            whole((1, slot_count)),
            whole((1, slot_count)),
        ],
        out_specs=pl.BlockSpec((slot_count, pair), lambda p: (0, p)),
        out_shape=jax.ShapeDtypeStruct((slot_count, width), jnp.bfloat16),
        compiler_params=pltpu.CompilerParams(vmem_limit_bytes=48 * 1024 * 1024),
    )(
        projections,
        projections,
        projections,
        keys,
        values,
        row_request,
        row_index,
        row_filled,
        column_tag,
        new_tag,
        new_row,
    )


def block_kernel(
    y_ref, gain_ref, shift_ref, w1_hbm, w2_hbm, o_ref, w1_ref, w2_ref, load_sem, x_ref, held, parts, pair_buf, send_buf, ring_buf,
    ring_send, ring_recv, pair_send, pair_recv, back_send, back_recv, sum_send, sum_recv,
):
    load_one = pltpu.make_async_copy(w1_hbm, w1_ref, load_sem.at[0])
    load_two = pltpu.make_async_copy(w2_hbm, w2_ref, load_sem.at[1])
    load_one.start()
    load_two.start()
    x_ref[...] = layer_norm(y_ref[...], gain_ref[...], shift_ref[...]).astype(x_ref.dtype)
    req = lax.axis_index("req")
    me = lax.axis_index("mlp")
    chips = lax.axis_size("mlp") // 2
    chip, core = me // 2, lax.rem(me, 2)
    partner = chip * 2 + 1 - core
    step = 1 - 2 * core
    ahead = lax.rem(chip + step + chips, chips)
    behind = lax.rem(chip - step + chips, chips)
    across = lax.rem(chip + 2, chips)
    rows = x_ref.shape[0]
    barrier = pltpu.get_barrier_semaphore()
    pl.semaphore_signal(barrier, 1, device_id=(req, partner), device_id_type=pl.DeviceIdType.MESH)
    pl.semaphore_signal(barrier, 1, device_id=(req, ahead * 2 + core), device_id_type=pl.DeviceIdType.MESH)
    pl.semaphore_signal(barrier, 1, device_id=(req, behind * 2 + core), device_id_type=pl.DeviceIdType.MESH)
    pl.semaphore_wait(barrier, 3)

    def block_rows(z, which):
        return pl.ds(pl.multiple_of((z * 2 + which) * rows, rows), rows)

    origins = (chip, behind, ahead, across)

    def ring_copy(kind):
        source = x_ref if kind < 2 else held.at[block_rows(behind, core)]
        origin = chip if kind < 2 else behind
        target = ahead if kind != 1 else behind
        return pltpu.make_async_remote_copy(
            src_ref=source,
            dst_ref=held.at[block_rows(origin, core)],
            send_sem=ring_send.at[kind],
            recv_sem=ring_recv.at[kind],
            device_id=(req, target * 2 + core),
            device_id_type=pl.DeviceIdType.MESH,
        )

    def pair_copy(kind):
        source = x_ref if kind == 0 else held.at[block_rows(origins[kind], core)]
        return pltpu.make_async_remote_copy(
            src_ref=source,
            dst_ref=held.at[block_rows(origins[kind], core)],
            send_sem=pair_send.at[kind],
            recv_sem=pair_recv.at[kind],
            device_id=(req, partner),
            device_id_type=pl.DeviceIdType.MESH,
        )

    def back_copy(z):
        return pltpu.make_async_remote_copy(
            src_ref=parts.at[block_rows(z, 1 - core)],
            dst_ref=pair_buf.at[z],
            send_sem=back_send.at[z],
            recv_sem=back_recv.at[z],
            device_id=(req, partner),
            device_id_type=pl.DeviceIdType.MESH,
        )

    def feed_forward(block, place):
        hidden = jnp.dot(block, w1_ref[...], preferred_element_type=jnp.float32)
        hidden = (hidden * 0.5 * (1.0 + lax.erf(hidden * (2.0 ** -0.5)))).astype(jnp.bfloat16)
        parts[place, :] = jnp.dot(hidden, w2_ref[...], preferred_element_type=jnp.float32).astype(
            parts.dtype
        )

    ring_copy(0).start()
    ring_copy(1).start()
    pair_copy(0).start()
    load_one.wait()
    load_two.wait()
    feed_forward(x_ref[...], block_rows(chip, core))
    ring_copy(0).wait_recv()
    ring_copy(2).start()
    pair_copy(1).start()
    feed_forward(held[block_rows(behind, core), :], block_rows(behind, core))
    ring_copy(1).wait_recv()
    pair_copy(2).start()
    feed_forward(held[block_rows(ahead, core), :], block_rows(ahead, core))
    ring_copy(2).wait_recv()
    pair_copy(3).start()
    feed_forward(held[block_rows(across, core), :], block_rows(across, core))
    partner_origins = (chip, ahead, behind, across)
    for kind in range(4):
        pair_copy(kind).wait_recv()
        place = block_rows(partner_origins[kind], 1 - core)
        feed_forward(held[place, :], place)
        back_copy(partner_origins[kind]).start()
    for kind in range(3):
        ring_copy(kind).wait_send()
    for kind in range(4):
        pair_copy(kind).wait_send()

    def summed(z):
        mine = parts[block_rows(z, core), :]
        return mine.astype(jnp.float32) + pair_buf[z].astype(jnp.float32)

    def sum_copy(kind, target):
        return pltpu.make_async_remote_copy(
            src_ref=send_buf.at[kind],
            dst_ref=ring_buf.at[kind],
            send_sem=sum_send.at[kind],
            recv_sem=sum_recv.at[kind],
            device_id=(req, target * 2 + core),
            device_id_type=pl.DeviceIdType.MESH,
        )

    back_copy(behind).wait_recv()
    send_buf[0] = summed(behind).astype(send_buf.dtype)
    sum_copy(0, behind).start()
    back_copy(across).wait_recv()
    send_buf[1] = summed(across).astype(send_buf.dtype)
    sum_copy(1, ahead).start()
    back_copy(ahead).wait_recv()
    sum_copy(1, ahead).wait_recv()
    send_buf[2] = (summed(ahead) + ring_buf[1].astype(jnp.float32)).astype(send_buf.dtype)
    sum_copy(2, ahead).start()
    back_copy(chip).wait_recv()
    total = summed(chip)
    for z in range(chips):
        back_copy(z).wait_send()
    sum_copy(0, behind).wait()
    total = total + ring_buf[0].astype(jnp.float32)
    sum_copy(1, ahead).wait_send()
    sum_copy(2, ahead).wait()
    o_ref[...] = x_ref[...].astype(jnp.float32) + (total + ring_buf[2].astype(jnp.float32))


def feed_forward_block(block, gain, shift, w_fc1, w_fc2):
    groups = lax.axis_size("mlp")
    chips = groups // 2
    rows, width = block.shape
    total = groups * rows
    out_width = w_fc2.shape[1]
    return pl.pallas_call(
        block_kernel,
        in_specs=[pl.BlockSpec(memory_space=pltpu.VMEM)] * 3 + [pl.BlockSpec(memory_space=pl.ANY)] * 2,
        out_specs=pl.BlockSpec(memory_space=pltpu.VMEM),
        out_shape=jax.ShapeDtypeStruct((rows, out_width), jnp.float32),
        scratch_shapes=[
            pltpu.VMEM(w_fc1.shape, w_fc1.dtype),
            pltpu.VMEM(w_fc2.shape, w_fc2.dtype),
            pltpu.SemaphoreType.DMA((2,)),
            pltpu.VMEM((rows, width), jnp.bfloat16),
            pltpu.VMEM((total, width), jnp.bfloat16),
            pltpu.VMEM((total, out_width), jnp.bfloat16),
            pltpu.VMEM((chips, rows, out_width), jnp.bfloat16),
            pltpu.VMEM((3, rows, out_width), jnp.bfloat16),
            pltpu.VMEM((3, rows, out_width), jnp.bfloat16),
            pltpu.SemaphoreType.DMA((3,)),
            pltpu.SemaphoreType.DMA((3,)),
            pltpu.SemaphoreType.DMA((chips,)),
            pltpu.SemaphoreType.DMA((chips,)),
            pltpu.SemaphoreType.DMA((chips,)),
            pltpu.SemaphoreType.DMA((chips,)),
            pltpu.SemaphoreType.DMA((3,)),
            pltpu.SemaphoreType.DMA((3,)),
        ],
        compiler_params=pltpu.CompilerParams(
            collective_id=2, has_side_effects=True, vmem_limit_bytes=53 * 1024 * 1024
        ),
    )(block, gain.reshape(1, -1), shift.reshape(1, -1), w_fc1, w_fc2)


def per_device(
    tokens,
    token_owner,
    token_request,
    cache_len,
    cache_k,
    cache_v,
    w_qkv,
    w_out,
    w_fc1,
    w_fc2,
    ln1_gain,
    ln1_bias,
    ln2_gain,
    ln2_bias,
):
    n_req = lax.axis_size("req")
    n_mlp = lax.axis_size("mlp")
    devices = n_req * n_mlp
    owner_index = lax.axis_index("req") * n_mlp + lax.axis_index("mlp")
    tok_dev, width = tokens.shape
    capacity = max(2, 2 * tok_dev // devices)
    slot_count = devices * capacity
    owners_flat = token_owner.reshape(-1)
    my_owners = lax.dynamic_slice_in_dim(owners_flat, owner_index * tok_dev, tok_dev)
    owner_onehot = (my_owners[:, None] == jnp.arange(devices, dtype=jnp.int32)[None, :]).astype(
        jnp.int32
    )
    ranking = jnp.cumsum(owner_onehot, axis=0) - 1
    my_rank = jnp.sum(owner_onehot * ranking, axis=1)
    column = my_owners * capacity + my_rank
    dispatch = (column[:, None] == jnp.arange(slot_count, dtype=jnp.int32)[None, :]).astype(
        jnp.bfloat16
    )
    outgoing = jnp.einsum("tr,td->rd", dispatch, tokens, preferred_element_type=jnp.float32).astype(
        jnp.bfloat16
    )
    arrived = lax.all_to_all(
        outgoing.reshape(devices, capacity, width),
        ("req", "mlp"),
        split_axis=0,
        concat_axis=0,
        tiled=True,
    )
    projections = jnp.dot(
        arrived.reshape(slot_count, width), w_qkv, preferred_element_type=jnp.float32
    ).astype(jnp.bfloat16)
    global_row, slot_request, filled = slot_table(
        owners_flat, token_request, owner_index, devices, tok_dev, capacity
    )
    attended = attend(projections, cache_k, cache_v, cache_len, global_row, slot_request, filled)
    returned = lax.all_to_all(
        attended.reshape(devices, capacity, width),
        ("req", "mlp"),
        split_axis=0,
        concat_axis=0,
        tiled=True,
    )
    attn_rows = jnp.einsum(
        "tsc,scd->td",
        dispatch.reshape(tok_dev, devices, capacity),
        returned,
        preferred_element_type=jnp.float32,
    ).astype(jnp.bfloat16)
    projected_out = jnp.dot(attn_rows, w_out, preferred_element_type=jnp.float32)
    mixed = feed_forward_block(
        projected_out + tokens.astype(jnp.float32), ln1_gain, ln1_bias, w_fc1, w_fc2
    )
    return layer_norm(mixed, ln2_gain, ln2_bias).astype(jnp.bfloat16)


def solution(mesh):
    placed = (
        P(("req", "mlp"), None),
        P(),
        P(),
        P(("req", "mlp")),
        P(("req", "mlp"), None, None),
        P(("req", "mlp"), None, None),
        P(),
        P(),
        P(None, "mlp"),
        P("mlp", None),
        P(),
        P(),
        P(),
        P(),
    )
    return jax.shard_map(
        per_device, mesh=mesh, in_specs=placed, out_specs=P(("req", "mlp"), None), check_vma=False
    )
```

```python
import jax
import jax.numpy as jnp
from jax import lax
from jax.sharding import PartitionSpec as P
from jax.experimental import pallas as pl
from jax.experimental.pallas import tpu as pltpu

HEADS = 16


epsilon = 1e-05


def layer_norm(values, gain, shift):
    center = values - jnp.mean(values, axis=-1, keepdims=True)
    spread = jnp.mean(center * center, axis=-1, keepdims=True)
    return center * lax.rsqrt(spread + epsilon) * gain + shift


def slot_table(owners_flat, requests_flat, owner_index, devices, tok_dev, capacity):
    owners = owners_flat.reshape(devices, tok_dev)
    requests = requests_flat.reshape(devices, tok_dev)
    mine_mask = (owners == owner_index).astype(jnp.int32)
    ranking = jnp.cumsum(mine_mask, axis=1) - 1
    places = jnp.arange(capacity, dtype=jnp.int32)
    hit_table = mine_mask[:, :, None] * (ranking[:, :, None] == places[None, None, :]).astype(
        jnp.int32
    )
    filled = jnp.sum(hit_table, axis=1)
    positions = jnp.arange(tok_dev, dtype=jnp.int32)
    local_row = jnp.sum(hit_table * positions[None, :, None], axis=1)
    sources = jnp.arange(devices, dtype=jnp.int32)[:, None]
    global_row = jnp.where(filled > 0, sources * tok_dev + local_row, -1).reshape(-1)
    slot_request = jnp.sum(hit_table * requests[:, :, None], axis=1).reshape(-1)
    return (global_row, slot_request, filled.reshape(-1))


def attention_kernel(
    q_ref, kn_ref, vn_ref, k_ref, v_ref, rreq_ref, rrow_ref, rfill_ref, ctag_ref, ntag_ref, nrow_ref, o_ref
):
    head_dim = q_ref.shape[1] // 2
    score_scale = head_dim ** (-0.5)
    q = q_ref[...] * jnp.asarray(score_scale, q_ref.dtype)
    keys = k_ref[...]
    values = v_ref[...]
    key_new = kn_ref[...]
    value_new = vn_ref[...]
    row_request = rreq_ref[...]
    old_mask = ctag_ref[...] == row_request
    new_mask = (ntag_ref[...] == row_request) & (nrow_ref[...] <= rrow_ref[...])
    lane = lax.broadcasted_iota(jnp.int32, (1, q.shape[1]), 1)
    contract = (((1,), (1,)), ((), ()))
    result = None
    for half in range(2):
        in_head = (lane // head_dim) == half
        q_head = jnp.where(in_head, q, jnp.zeros_like(q))
        old_score = lax.dot_general(q_head, keys, contract, preferred_element_type=jnp.float32)
        new_score = lax.dot_general(q_head, key_new, contract, preferred_element_type=jnp.float32)
        old_exp = jnp.where(old_mask, jnp.exp(old_score), jnp.float32(0.0))
        new_exp = jnp.where(new_mask, jnp.exp(new_score), jnp.float32(0.0))
        total = jnp.sum(old_exp, axis=1, keepdims=True) + jnp.sum(new_exp, axis=1, keepdims=True)
        total = jnp.where(total > 0, total, jnp.float32(1.0))
        inverse = 1.0 / total
        old_weight = (old_exp * inverse).astype(jnp.bfloat16)
        new_weight = (new_exp * inverse).astype(jnp.bfloat16)
        part = jnp.dot(old_weight, values, preferred_element_type=jnp.float32) + jnp.dot(
            new_weight, value_new, preferred_element_type=jnp.float32
        )
        result = part if result is None else jnp.where(in_head, part, result)
    result = jnp.where(rfill_ref[...] > 0, result, jnp.float32(0.0))
    o_ref[...] = result.astype(o_ref.dtype)


def attend(projections, cache_keys, cache_values, lengths, global_row, slot_request, filled):
    slot_count = projections.shape[0]
    width = projections.shape[1] // 3
    requests, context = cache_keys.shape[0], cache_keys.shape[1]
    pair = 128
    pairs = width // pair
    keys = cache_keys.reshape(requests * context, width)
    values = cache_values.reshape(requests * context, width)
    key_owner = jnp.arange(requests * context, dtype=jnp.int32) // context
    key_place = jnp.arange(requests * context, dtype=jnp.int32) % context
    key_limit = jnp.repeat(lengths, context)
    column_tag = jnp.where(key_place < key_limit, key_owner, -1).reshape(1, -1)
    new_tag = jnp.where(filled > 0, slot_request, -1).reshape(1, -1)
    new_row = global_row.reshape(1, -1)
    row_request = slot_request.reshape(-1, 1)
    row_index = global_row.reshape(-1, 1)
    row_filled = filled.reshape(-1, 1)
    keyed = requests * context
    whole = lambda shape: pl.BlockSpec(shape, lambda p: (0, 0))
    return pl.pallas_call(
        attention_kernel,
        grid=(pairs,),
        in_specs=[
            pl.BlockSpec((slot_count, pair), lambda p: (0, p)),
            pl.BlockSpec((slot_count, pair), lambda p: (0, pairs + p)),
            pl.BlockSpec((slot_count, pair), lambda p: (0, 2 * pairs + p)),
            pl.BlockSpec((keyed, pair), lambda p: (0, p)),
            pl.BlockSpec((keyed, pair), lambda p: (0, p)),
            whole((slot_count, 1)),
            whole((slot_count, 1)),
            whole((slot_count, 1)),
            whole((1, keyed)),
            whole((1, slot_count)),
            whole((1, slot_count)),
        ],
        out_specs=pl.BlockSpec((slot_count, pair), lambda p: (0, p)),
        out_shape=jax.ShapeDtypeStruct((slot_count, width), jnp.bfloat16),
        compiler_params=pltpu.CompilerParams(vmem_limit_bytes=48 * 1024 * 1024),
    )(
        projections,
        projections,
        projections,
        keys,
        values,
        row_request,
        row_index,
        row_filled,
        column_tag,
        new_tag,
        new_row,
    )


def block_kernel(
    y_ref, gain_ref, shift_ref, w1_hbm, w2_hbm, o_ref, w1_ref, w2_ref, load_sem, x_ref, held, parts, pair_buf, send_buf, ring_buf,
    ring_send, ring_recv, pair_send, pair_recv, back_send, back_recv, sum_send, sum_recv,
):
    load_one = pltpu.make_async_copy(w1_hbm, w1_ref, load_sem.at[0])
    load_two = pltpu.make_async_copy(w2_hbm, w2_ref, load_sem.at[1])
    load_one.start()
    load_two.start()
    x_ref[...] = layer_norm(y_ref[...], gain_ref[...], shift_ref[...]).astype(x_ref.dtype)
    req = lax.axis_index("req")
    me = lax.axis_index("mlp")
    chips = lax.axis_size("mlp") // 2
    chip, core = me // 2, lax.rem(me, 2)
    partner = chip * 2 + 1 - core
    step = 1 - 2 * core
    ahead = lax.rem(chip + step + chips, chips)
    behind = lax.rem(chip - step + chips, chips)
    across = lax.rem(chip + 2, chips)
    rows = x_ref.shape[0]
    barrier = pltpu.get_barrier_semaphore()
    pl.semaphore_signal(barrier, 1, device_id=(req, partner), device_id_type=pl.DeviceIdType.MESH)
    pl.semaphore_signal(barrier, 1, device_id=(req, ahead * 2 + core), device_id_type=pl.DeviceIdType.MESH)
    pl.semaphore_signal(barrier, 1, device_id=(req, behind * 2 + core), device_id_type=pl.DeviceIdType.MESH)
    pl.semaphore_wait(barrier, 3)

    def block_rows(z, which):
        return pl.ds(pl.multiple_of((z * 2 + which) * rows, rows), rows)

    origins = (chip, behind, ahead, across)

    def ring_copy(kind):
        source = x_ref if kind < 2 else held.at[block_rows(behind, core)]
        origin = chip if kind < 2 else behind
        target = ahead if kind != 1 else behind
        return pltpu.make_async_remote_copy(
            src_ref=source,
            dst_ref=held.at[block_rows(origin, core)],
            send_sem=ring_send.at[kind],
            recv_sem=ring_recv.at[kind],
            device_id=(req, target * 2 + core),
            device_id_type=pl.DeviceIdType.MESH,
        )

    def pair_copy(kind):
        source = x_ref if kind == 0 else held.at[block_rows(origins[kind], core)]
        return pltpu.make_async_remote_copy(
            src_ref=source,
            dst_ref=held.at[block_rows(origins[kind], core)],
            send_sem=pair_send.at[kind],
            recv_sem=pair_recv.at[kind],
            device_id=(req, partner),
            device_id_type=pl.DeviceIdType.MESH,
        )

    def back_copy(z):
        return pltpu.make_async_remote_copy(
            src_ref=parts.at[block_rows(z, 1 - core)],
            dst_ref=pair_buf.at[z],
            send_sem=back_send.at[z],
            recv_sem=back_recv.at[z],
            device_id=(req, partner),
            device_id_type=pl.DeviceIdType.MESH,
        )

    def feed_forward(block, place):
        hidden = jnp.dot(block, w1_ref[...], preferred_element_type=jnp.float32)
        hidden = (hidden * 0.5 * (1.0 + lax.erf(hidden * (2.0 ** -0.5)))).astype(jnp.bfloat16)
        parts[place, :] = jnp.dot(hidden, w2_ref[...], preferred_element_type=jnp.float32).astype(
            parts.dtype
        )

    ring_copy(0).start()
    ring_copy(1).start()
    pair_copy(0).start()
    load_one.wait()
    load_two.wait()
    feed_forward(x_ref[...], block_rows(chip, core))
    ring_copy(0).wait_recv()
    ring_copy(2).start()
    pair_copy(1).start()
    feed_forward(held[block_rows(behind, core), :], block_rows(behind, core))
    ring_copy(1).wait_recv()
    pair_copy(2).start()
    feed_forward(held[block_rows(ahead, core), :], block_rows(ahead, core))
    ring_copy(2).wait_recv()
    pair_copy(3).start()
    feed_forward(held[block_rows(across, core), :], block_rows(across, core))
    partner_origins = (chip, ahead, behind, across)
    for kind in range(4):
        pair_copy(kind).wait_recv()
        place = block_rows(partner_origins[kind], 1 - core)
        feed_forward(held[place, :], place)
        back_copy(partner_origins[kind]).start()
    for kind in range(3):
        ring_copy(kind).wait_send()
    for kind in range(4):
        pair_copy(kind).wait_send()

    def summed(z):
        mine = parts[block_rows(z, core), :]
        return mine.astype(jnp.float32) + pair_buf[z].astype(jnp.float32)

    def sum_copy(kind, target):
        return pltpu.make_async_remote_copy(
            src_ref=send_buf.at[kind],
            dst_ref=ring_buf.at[kind],
            send_sem=sum_send.at[kind],
            recv_sem=sum_recv.at[kind],
            device_id=(req, target * 2 + core),
            device_id_type=pl.DeviceIdType.MESH,
        )

    back_copy(behind).wait_recv()
    send_buf[0] = summed(behind).astype(send_buf.dtype)
    sum_copy(0, behind).start()
    back_copy(across).wait_recv()
    send_buf[1] = summed(across).astype(send_buf.dtype)
    sum_copy(1, ahead).start()
    back_copy(ahead).wait_recv()
    sum_copy(1, ahead).wait_recv()
    send_buf[2] = (summed(ahead) + ring_buf[1].astype(jnp.float32)).astype(send_buf.dtype)
    sum_copy(2, ahead).start()
    back_copy(chip).wait_recv()
    total = summed(chip)
    for z in range(chips):
        back_copy(z).wait_send()
    sum_copy(0, behind).wait()
    total = total + ring_buf[0].astype(jnp.float32)
    sum_copy(1, ahead).wait_send()
    sum_copy(2, ahead).wait()
    o_ref[...] = x_ref[...].astype(jnp.float32) + (total + ring_buf[2].astype(jnp.float32))


def feed_forward_block(block, gain, shift, w_fc1, w_fc2):
    groups = lax.axis_size("mlp")
    chips = groups // 2
    rows, width = block.shape
    total = groups * rows
    out_width = w_fc2.shape[1]
    return pl.pallas_call(
        block_kernel,
        in_specs=[pl.BlockSpec(memory_space=pltpu.VMEM)] * 3 + [pl.BlockSpec(memory_space=pl.ANY)] * 2,
        out_specs=pl.BlockSpec(memory_space=pltpu.VMEM),
        out_shape=jax.ShapeDtypeStruct((rows, out_width), jnp.float32),
        scratch_shapes=[
            pltpu.VMEM(w_fc1.shape, w_fc1.dtype),
            pltpu.VMEM(w_fc2.shape, w_fc2.dtype),
            pltpu.SemaphoreType.DMA((2,)),
            pltpu.VMEM((rows, width), jnp.bfloat16),
            pltpu.VMEM((total, width), jnp.bfloat16),
            pltpu.VMEM((total, out_width), jnp.bfloat16),
            pltpu.VMEM((chips, rows, out_width), jnp.bfloat16),
            pltpu.VMEM((3, rows, out_width), jnp.bfloat16),
            pltpu.VMEM((3, rows, out_width), jnp.bfloat16),
            pltpu.SemaphoreType.DMA((3,)),
            pltpu.SemaphoreType.DMA((3,)),
            pltpu.SemaphoreType.DMA((chips,)),
            pltpu.SemaphoreType.DMA((chips,)),
            pltpu.SemaphoreType.DMA((chips,)),
            pltpu.SemaphoreType.DMA((chips,)),
            pltpu.SemaphoreType.DMA((3,)),
            pltpu.SemaphoreType.DMA((3,)),
        ],
        compiler_params=pltpu.CompilerParams(
            collective_id=2, has_side_effects=True, vmem_limit_bytes=52 * 1024 * 1024
        ),
    )(block, gain.reshape(1, -1), shift.reshape(1, -1), w_fc1, w_fc2)


def per_device(
    tokens,
    token_owner,
    token_request,
    cache_len,
    cache_k,
    cache_v,
    w_qkv,
    w_out,
    w_fc1,
    w_fc2,
    ln1_gain,
    ln1_bias,
    ln2_gain,
    ln2_bias,
):
    n_req = lax.axis_size("req")
    n_mlp = lax.axis_size("mlp")
    devices = n_req * n_mlp
    owner_index = lax.axis_index("req") * n_mlp + lax.axis_index("mlp")
    tok_dev, width = tokens.shape
    capacity = max(2, 2 * tok_dev // devices)
    slot_count = devices * capacity
    owners_flat = token_owner.reshape(-1)
    my_owners = lax.dynamic_slice_in_dim(owners_flat, owner_index * tok_dev, tok_dev)
    owner_onehot = (my_owners[:, None] == jnp.arange(devices, dtype=jnp.int32)[None, :]).astype(
        jnp.int32
    )
    ranking = jnp.cumsum(owner_onehot, axis=0) - 1
    my_rank = jnp.sum(owner_onehot * ranking, axis=1)
    column = my_owners * capacity + my_rank
    dispatch = (column[:, None] == jnp.arange(slot_count, dtype=jnp.int32)[None, :]).astype(
        jnp.bfloat16
    )
    outgoing = jnp.einsum("tr,td->rd", dispatch, tokens, preferred_element_type=jnp.float32).astype(
        jnp.bfloat16
    )
    arrived = lax.all_to_all(
        outgoing.reshape(devices, capacity, width),
        ("req", "mlp"),
        split_axis=0,
        concat_axis=0,
        tiled=True,
    )
    projections = jnp.dot(
        arrived.reshape(slot_count, width), w_qkv, preferred_element_type=jnp.float32
    ).astype(jnp.bfloat16)
    global_row, slot_request, filled = slot_table(
        owners_flat, token_request, owner_index, devices, tok_dev, capacity
    )
    attended = attend(projections, cache_k, cache_v, cache_len, global_row, slot_request, filled)
    returned = lax.all_to_all(
        attended.reshape(devices, capacity, width),
        ("req", "mlp"),
        split_axis=0,
        concat_axis=0,
        tiled=True,
    )
    attn_rows = jnp.einsum(
        "tsc,scd->td",
        dispatch.reshape(tok_dev, devices, capacity),
        returned,
        preferred_element_type=jnp.float32,
    ).astype(jnp.bfloat16)
    projected_out = jnp.dot(attn_rows, w_out, preferred_element_type=jnp.float32)
    mixed = feed_forward_block(
        projected_out + tokens.astype(jnp.float32), ln1_gain, ln1_bias, w_fc1, w_fc2
    )
    return layer_norm(mixed, ln2_gain, ln2_bias).astype(jnp.bfloat16)


def solution(mesh):
    placed = (
        P(("req", "mlp"), None),
        P(),
        P(),
        P(("req", "mlp")),
        P(("req", "mlp"), None, None),
        P(("req", "mlp"), None, None),
        P(),
        P(),
        P(None, "mlp"),
        P("mlp", None),
        P(),
        P(),
        P(),
        P(),
    )
    return jax.shard_map(
        per_device, mesh=mesh, in_specs=placed, out_specs=P(("req", "mlp"), None), check_vma=False
    )
```
